32 devices in a mesh: row: 4 (over z), col: 8 (over y, x, core).
Axes of the slice: x: 2, y: 2, z: 4, core: 2. Of those that a mesh axis runs over, the one named last changes fastest.
Arguments:
- inputs: float32 [8192, 768], P(('row', 'col')), may hold values from -4 to 4
- rho: float32 [8192], P(('row', 'col')), may hold values from 38.243683 to 40.18358
- sigma: float32 [8192], P(('row', 'col')), may hold values from 0.4 to 2
- embed: float32 [64, 8192], P(None, ('row', 'col')), may hold values from -0.72 to 0.72
- knn_blocks: int32 [4, 8, 8, 4, 2], P('row', 'col'), may hold values from 0 to 1, as said below
- knn_seeds: int32 [4, 8, 8, 4], P('row', 'col'), may hold values from 0 to 8388607
- neg_rows: int32 [4, 8, 48], P('row', 'col'), may hold values from 0 to 15
- neg_cols: int32 [4, 8, 48], P('row', 'col'), may hold values from 0 to 7
- neg_count: int32 [4, 8], P('row', 'col'), may hold values from 1 to 48, as said below
Outputs:
- embedding: float32 [64, 8192], P(None, ('row', 'col'))
- last_force: float32 [64, 8192], P(None, ('row', 'col'))
The draws below stay inside these ranges and needn't reach their ends.
Inputs may be any that keep to these rules, and one draw needn't show every extreme that they name: `knn_blocks`: if tile (r, c, a, s) lists blocks (u, v), tile (s, a, c, r) lists blocks (v, u); where both name the same span, u = v. `neg_count`: one device's list is full, 48 live slots.
All inputs are finite; a program needn't handle non-finite values.
Results may differ from the reference program's by a relative error of at most 0.0003.
Values sent between devices are 32-bit elements; how exact they have to be, the bound alone decides.
No kernel may reach another device: no remote copies, remote signals or barrier semaphores. Data moves between devices by JAX's collectives and lax.ppermute only.
A program may use at most 128 MiB of HBM per device.

```python
import math
import jax
import jax.numpy as jnp
from jax import lax

D_IN = 768
D_EMB = 64
BLK = 128
CB = 2
NEG_DEV = 48
STEPS = 2
NR = 4
NC = 8
NPTS = 8192


def draw_inputs(key, part):
    values = jax.random.truncated_normal(key, -4.0, 4.0, (NPTS, D_IN), jnp.float32)
    return values


def draw_knn_blocks(key, part):
    spans = NR * NC
    raw = jax.random.randint(jax.random.fold_in(key, 11), (spans, spans), 0, CB * CB)
    lower = jnp.arange(spans)[:, None]
    upper = jnp.arange(spans)[None, :]
    shared = jnp.where(lower <= upper, raw, raw.T)
    first = shared // CB
    second = shared % CB
    row_block = jnp.where(lower < upper, first, second)
    col_block = jnp.where(lower > upper, first, second)
    stacked = jnp.stack([row_block, col_block], axis=-1)
    stacked = stacked.reshape(NR, NC, NR, NC, 2)
    return jnp.transpose(stacked, (0, 3, 1, 2, 4)).astype(jnp.int32)


def draw_neg_count(key, part):
    devices = NR * NC
    first = jax.random.randint(jax.random.fold_in(key, 21), (devices,), 1, NEG_DEV + 1)
    second = jax.random.randint(jax.random.fold_in(key, 22), (devices,), 1, NEG_DEV + 1)
    picked = jax.random.randint(jax.random.fold_in(key, 23), (), 0, devices)
    counts = jnp.where(jnp.arange(devices) == picked, NEG_DEV, jnp.minimum(first, second))
    return counts.reshape(NR, NC).astype(jnp.int32)


def set_ends(result, own_key, least, top_value):
    shape = result.shape
    index_at = [jax.random.randint(jax.random.fold_in(own_key, axis), (), 0, shape[axis]) for axis in range(len(shape))]
    result = result.at[tuple(index_at)].set(least)
    longest = shape.index(max(shape))
    index_at[longest] = (index_at[longest] + 1) % shape[longest]
    return result.at[tuple(index_at)].set(top_value)


def level_of(rng, dims, split, least, largest):
    level = 1.0
    for axis_at, blocks in split:
        draws = jax.random.uniform(jax.random.fold_in(jax.random.fold_in(rng, 6), axis_at), (blocks,), jnp.float32, least / len(split), largest / len(split))
        level = level * jnp.repeat(jnp.exp(draws), dims[axis_at] // blocks).reshape((-1,) + (1,) * (len(dims) - 1 - axis_at))
    return level


def noise(key, dims, scale, most, shards=(), kind=jnp.bfloat16):
    drawn = scale * jax.random.normal(key, dims, jnp.float32)
    if shards:
        drawn = drawn * level_of(key, dims, shards, -0.22, 0.18)
    return jnp.clip(drawn, -most, most).astype(kind)


def setup_inputs(seed: int = 0) -> dict:
    arg_keys = jax.random.split(jax.random.key(seed), 10)
    inputs = draw_inputs(jax.random.fold_in(arg_keys[9], 71), 0)
    rho = jnp.clip(38.243683 + 1.9398956 * jax.random.uniform(arg_keys[1], (NPTS,), jnp.float32) ** level_of(arg_keys[1], (NPTS,), ((0, 32),), -0.2, 0.2), 38.243683, 40.18358)
    sigma = jnp.clip(jnp.exp(math.log(2.0) - 1.609438 * jax.random.uniform(arg_keys[2], (NPTS,), jnp.float32) ** level_of(arg_keys[2], (NPTS,), ((0, 32),), -0.2, 0.2)), 0.4, 2.0)
    embed = noise(arg_keys[3], (D_EMB, NPTS), 0.12, 0.72, ((1, 32),), jnp.float32)
    knn_blocks = draw_knn_blocks(jax.random.fold_in(arg_keys[9], 71), 0)
    knn_seeds = set_ends(jax.random.randint(arg_keys[5], (NR, NC, NC, NR), 0, 8388608), jax.random.fold_in(arg_keys[5], 1), 0, 8388607).astype(jnp.int32)
    neg_rows = set_ends(jax.random.randint(arg_keys[6], (NR, NC, NEG_DEV), 0, NC * CB), jax.random.fold_in(arg_keys[6], 1), 0, (NC * CB) - 1).astype(jnp.int32)
    neg_cols = set_ends(jax.random.randint(arg_keys[7], (NR, NC, NEG_DEV), 0, NR * CB), jax.random.fold_in(arg_keys[7], 1), 0, (NR * CB) - 1).astype(jnp.int32)
    neg_count = draw_neg_count(jax.random.fold_in(arg_keys[9], 71), 0)
    return {"inputs": inputs, "rho": rho, "sigma": sigma, "embed": embed, "knn_blocks": knn_blocks, "knn_seeds": knn_seeds, "neg_rows": neg_rows, "neg_cols": neg_cols, "neg_count": neg_count}


STEP_SIZE = 0.0005
REPULSION = 2.0
FORCE_SCALE = 0.015625
FULL_PRECISION = lax.Precision.HIGHEST

def hash_bits(salt_value, first, second):
    mixed = first * 1103515245 + salt_value
    mixed = (mixed ^ second * 747796405) * 277803737
    return (mixed >> 17 & 1).astype(jnp.float32)

def conditional(distance, offset, spread, mask):
    return mask * jnp.exp(-jnp.maximum(distance - offset, 0.0) / spread)

def pair_kernel(left, right):
    gram = jnp.einsum('dsi,dsj->sij', left, right, precision=FULL_PRECISION)
    total = lax.optimization_barrier(jnp.sum(left * left, axis=0))[:, :, None] + lax.optimization_barrier(jnp.sum(right * right, axis=0))[:, None, :] - 2.0 * gram
    return 1.0 / (1.0 + total)

def affinity_tiles(inputs, rho, sigma, knn_blocks, knn_seeds):
    blocks_x = inputs.reshape(NR, NC, CB, BLK, D_IN)
    squares = lax.optimization_barrier(jnp.sum(inputs * inputs, axis=1)).reshape(NR, NC, CB, BLK)
    offsets = rho.reshape(NR, NC, CB, BLK)
    spreads = sigma.reshape(NR, NC, CB, BLK)
    seeds_back = jnp.transpose(knn_seeds, (3, 2, 1, 0))
    positions = jnp.arange(BLK, dtype=jnp.int32)
    chosen = jnp.arange(NR, dtype=jnp.int32)

    def one_device(index):
        row_dev = index // NC
        col_dev = index % NC
        listing = knn_blocks[row_dev, col_dev]
        seeds = knn_seeds[row_dev, col_dev]
        partner = seeds_back[row_dev, col_dev]
        col_x = blocks_x[:, col_dev]
        col_squares = squares[:, col_dev]
        col_offsets = offsets[:, col_dev]
        col_spreads = spreads[:, col_dev]

        def one_group(group):
            row_pick = listing[group, :, 0]
            col_pick = listing[group, :, 1]
            left = blocks_x[row_dev, group][row_pick]
            right = col_x[chosen, col_pick]
            gram = jnp.einsum('sid,sjd->sij', left, right, precision=FULL_PRECISION)
            total = squares[row_dev, group][row_pick][:, :, None] + col_squares[chosen, col_pick][:, None, :] - 2.0 * gram
            distance = jnp.sqrt(jnp.maximum(total, 1.0))
            mask = hash_bits(seeds[group][:, None, None], positions[None, :, None], positions[None, None, :])
            forward = conditional(distance, offsets[row_dev, group][row_pick][:, :, None], spreads[row_dev, group][row_pick][:, :, None], mask)
            mask_back = hash_bits(partner[group][:, None, None], positions[None, None, :], positions[None, :, None])
            backward = conditional(distance, col_offsets[chosen, col_pick][:, None, :], col_spreads[chosen, col_pick][:, None, :], mask_back)
            return (forward + backward - forward * backward).astype(jnp.bfloat16)
        return lax.map(one_group, jnp.arange(NC, dtype=jnp.int32))
    return lax.map(one_device, jnp.arange(NR * NC, dtype=jnp.int32))

def step_forces(embed, weights, knn_blocks, neg_rows, neg_cols, neg_count):
    blocks_y = embed.reshape(D_EMB, NR, NC, CB, BLK)
    chosen = jnp.arange(NR, dtype=jnp.int32)
    block_ids = jnp.arange(CB, dtype=jnp.int32)
    row_slots = jnp.arange(NC * CB, dtype=jnp.int32)
    col_slots = jnp.arange(NR * CB, dtype=jnp.int32)

    def one_device(index):
        row_dev = index // NC
        col_dev = index % NC
        row_y = blocks_y[:, row_dev]
        col_y = blocks_y[:, :, col_dev]
        listing = knn_blocks[row_dev, col_dev]
        tiles = weights[index]

        def one_group(group):
            row_pick = listing[group, :, 0]
            col_pick = listing[group, :, 1]
            left = row_y[:, group][:, row_pick]
            right = col_y[:, chosen, col_pick]
            pull_weight = tiles[group].astype(jnp.float32) * pair_kernel(left, right)
            pull = jnp.einsum('dsj,sij->dsi', right, pull_weight, precision=FULL_PRECISION) - left * lax.optimization_barrier(jnp.sum(pull_weight, axis=2))[None]
            onehot = (row_pick[:, None] == block_ids[None, :]).astype(jnp.float32)
            return jnp.einsum('sb,dsi->dbi', onehot, pull, precision=FULL_PRECISION)
        attract = lax.map(one_group, jnp.arange(NC, dtype=jnp.int32))
        row_force = jnp.transpose(attract, (1, 0, 2, 3)).reshape(D_EMB, NC * CB, BLK)
        live = (jnp.arange(NEG_DEV, dtype=jnp.int32) < neg_count[row_dev, col_dev]).astype(jnp.float32)
        row_list = neg_rows[row_dev, col_dev]
        col_list = neg_cols[row_dev, col_dev]
        left = row_y.reshape(D_EMB, NC * CB, BLK)[:, row_list]
        right = col_y.reshape(D_EMB, NR * CB, BLK)[:, col_list]
        kernel = pair_kernel(left, right)
        push = REPULSION * kernel * kernel * live[:, None, None]
        row_push = left * lax.optimization_barrier(jnp.sum(push, axis=2))[None] - jnp.einsum('dkj,kij->dki', right, push, precision=FULL_PRECISION)
        col_push = right * lax.optimization_barrier(jnp.sum(push, axis=1))[None] - jnp.einsum('dki,kij->dkj', left, push, precision=FULL_PRECISION)
        row_hot = (row_list[:, None] == row_slots[None, :]).astype(jnp.float32)
        col_hot = (col_list[:, None] == col_slots[None, :]).astype(jnp.float32)
        row_force = row_force + jnp.einsum('ku,dki->dui', row_hot, row_push, precision=FULL_PRECISION)
        col_force = jnp.einsum('kv,dkj->dvj', col_hot, col_push, precision=FULL_PRECISION)
        return (row_force, col_force)
    row_all, col_all = lax.map(one_device, jnp.arange(NR * NC, dtype=jnp.int32))
    row_sum = lax.optimization_barrier(jnp.sum(row_all.reshape(NR, NC, D_EMB, NC, CB * BLK), axis=1))
    row_sum = jnp.transpose(row_sum, (1, 0, 2, 3))
    col_sum = lax.optimization_barrier(jnp.sum(col_all.reshape(NR, NC, D_EMB, NR, CB * BLK), axis=0))
    col_sum = jnp.transpose(col_sum, (1, 2, 0, 3))
    return (row_sum + col_sum).reshape(D_EMB, NR * NC * CB * BLK)

def reference(inputs, rho, sigma, embed, knn_blocks, knn_seeds, neg_rows, neg_cols, neg_count):
    weights = affinity_tiles(inputs, rho, sigma, knn_blocks, knn_seeds)
    force = jnp.zeros_like(embed)
    for step in range(STEPS):
        force = step_forces(embed, weights, knn_blocks, neg_rows, neg_cols, neg_count)
        embed = embed + STEP_SIZE * force
    return (embed, force * FORCE_SCALE)
```

```python
import functools

import jax
import jax.numpy as jnp
from jax import lax
from jax.experimental import pallas as pl
from jax.experimental.pallas import tpu as pltpu
from jax.sharding import PartitionSpec as P

D_EMB = 64
BLK = 128
CB = 2
SPAN = CB * BLK
STEPS = 2

STEP_SIZE = 0.0005
REPULSION = 2.0
FORCE_SCALE = 0.015625

RHO, SIGMA, SQUARES, SEEDS = D_EMB, D_EMB + 1, D_EMB + 2, D_EMB + 3
PACK = 72
STACK = 4 * D_EMB
PULL = 2 * D_EMB + 16
UNROLL = 4
F32, BF16, I32 = jnp.float32, jnp.bfloat16, jnp.int32
VMEM_LIMIT = 56 * 2**20


def split(value):
    high = value.astype(BF16)
    return high, (value - high.astype(F32)).astype(BF16)


def nt_dot(left, right):
    return lax.dot_general(left, right, (((1,), (1,)), ((), ())), preferred_element_type=F32)


def nn_dot(left, right):
    return lax.dot_general(left, right, (((1,), (0,)), ((), ())), preferred_element_type=F32)


def hash_bits(salt_value, first, second):
    mixed = first * 1103515245 + salt_value
    mixed = (mixed ^ second * 747796405) * 277803737
    return (mixed >> 17 & 1).astype(F32)


def takes_shift(shift, row, row_count):
    if 2 * shift != row_count:
        return True
    half = row_count // 2
    return jnp.where(row < half, row % 2 == 0, (row - half) % 2 == 1)


def weights_kernel(row_count, col_count, meta, listing, seeds, seeds_back, row_x, row_pack, *rest):
    shifts = row_count // 2 + 1
    col_x, col_pack = rest[:shifts], rest[shifts : 2 * shifts]
    out, high_c, low_c, col_params = rest[2 * shifts :]
    group = pl.program_id(0)
    row, col = meta[0], meta[1]

    @pl.when(group == 0)
    def _():
        for shift in range(shifts):
            high, low = split(col_x[shift][...])
            high_c[shift], low_c[shift] = high, low
            for block in range(CB):
                params = col_pack[shift][RHO : RHO + 8, block * BLK : (block + 1) * BLK]
                col_params[shift, block] = params.T

    high_r, low_r = split(row_x[0])
    high_r = high_r.reshape(CB, BLK, high_r.shape[1])
    low_r = low_r.reshape(CB, BLK, low_r.shape[1])
    positions_j = lax.broadcasted_iota(I32, (BLK, BLK), 0)
    positions_i = lax.broadcasted_iota(I32, (BLK, BLK), 1)

    for shift in range(shifts):
        if shift == 0:
            offset = lax.rem(group - col + col_count, col_count)
            active = (2 * offset < col_count) | ((2 * offset == col_count) & (2 * col < col_count))
        else:
            active = takes_shift(shift, row, row_count)
        other = lax.rem(row + shift, row_count)
        entry = (group * row_count + other) * 2
        row_pick, col_pick = listing[entry], listing[entry + 1]

        @pl.when(jnp.logical_not(active))
        def _():
            out[0, shift] = jnp.zeros((BLK, BLK), BF16)

        for pick in range(CB):

            @pl.when(active & (row_pick == pick))
            def _():
                start = pl.multiple_of(col_pick * BLK, BLK)
                left_high = high_c[shift, pl.ds(start, BLK), :]
                left_low = low_c[shift, pl.ds(start, BLK), :]
                gram = (
                    nt_dot(left_high, low_r[pick])
                    + nt_dot(left_low, high_r[pick])
                    + nt_dot(left_high, high_r[pick])
                )
                lanes = slice(pick * BLK, (pick + 1) * BLK)
                rho_i = row_pack[0, RHO - D_EMB : RHO - D_EMB + 1, lanes]
                sigma_i = row_pack[0, SIGMA - D_EMB : SIGMA - D_EMB + 1, lanes]
                square_i = row_pack[0, SQUARES - D_EMB : SQUARES - D_EMB + 1, lanes]
                params_j = col_params[shift, col_pick]
                rho_j, sigma_j, square_j = params_j[:, 0:1], params_j[:, 1:2], params_j[:, 2:3]
                total = square_j + square_i - 2.0 * gram
                distance = jnp.sqrt(jnp.maximum(total, 1.0))
                seed = seeds[group * row_count + other]
                seed_back = seeds_back[shift * col_count + group]
                ahead = hash_bits(seed, positions_i, positions_j) * jnp.exp(
                    jnp.maximum(distance - rho_i, 0.0) * (-1.0 / sigma_i)
                )
                behind = hash_bits(seed_back, positions_j, positions_i) * jnp.exp(
                    jnp.maximum(distance - rho_j, 0.0) * (-1.0 / sigma_j)
                )
                weights = (ahead + behind - ahead * behind).astype(BF16)
                if shift == 0:
                    weights = (weights.astype(F32) * jnp.where(group == col, 0.5, 1.0)).astype(BF16)
                out[0, shift] = weights


def pair_weights(row_count, col_count, meta, listing, seeds, seeds_back, row_x, row_pack, col_x, col_pack):
    shifts = row_count // 2 + 1
    depth = row_x.shape[-1]
    smem = pl.BlockSpec(memory_space=pltpu.SMEM)
    vmem = pl.BlockSpec(memory_space=pltpu.VMEM)
    tiles = col_count * shifts
    return pl.pallas_call(
        functools.partial(weights_kernel, row_count, col_count),
        grid=(col_count,),
        in_specs=[smem] * 4
        + [
            pl.BlockSpec((1, SPAN, depth), lambda a: (a, 0, 0)),
            pl.BlockSpec((1, 8, SPAN), lambda a: (a, D_EMB // 8, 0)),
        ]
        + [vmem] * (2 * shifts),
        out_specs=pl.BlockSpec((1, shifts, BLK, BLK), lambda a: (a, 0, 0, 0)),
        out_shape=jax.ShapeDtypeStruct((col_count, shifts, BLK, BLK), BF16),
        scratch_shapes=[
            pltpu.VMEM((shifts, SPAN, depth), BF16),
            pltpu.VMEM((shifts, SPAN, depth), BF16),
            pltpu.VMEM((shifts, CB, BLK, 8), F32),
        ],
        compiler_params=pltpu.CompilerParams(vmem_limit_bytes=VMEM_LIMIT),
        cost_estimate=pl.CostEstimate(
            flops=tiles * 6 * BLK * BLK * depth,
            bytes_accessed=(col_count + shifts) * SPAN * depth * 4,
            transcendentals=tiles * 3 * BLK * BLK,
        ),
        name="weights",
    )(meta, listing, seeds, seeds_back, row_x, row_pack, *col_x, *col_pack)


def force_kernel(row_count, col_count, meta, listing, neg_rows, neg_cols, weights, row_y, *rest):
    shifts = row_count // 2 + 1
    col_y = rest[:row_count]
    row_force, col_force = rest[row_count], rest[row_count + 1 : 2 * row_count + 1]
    left_gram, right_gram, left_pull, right_pull, left_acc, right_acc = rest[2 * row_count + 1 :]
    row, col, live = meta[0], meta[1], meta[2]
    iota = lax.broadcasted_iota(I32, (D_EMB, BLK), 0)
    ones = jnp.ones((16, BLK), BF16)
    blank = jnp.zeros((D_EMB, BLK), BF16)

    def norm_rows(value, first):
        norm = jnp.sum(value * value, axis=0, keepdims=True)
        high, rest_ = split(norm)
        left_over = norm - high.astype(F32) - rest_.astype(F32)
        high, middle = high.astype(F32), rest_.astype(F32)
        return jnp.where(
            iota == first,
            high,
            jnp.where(iota == first + 1, middle, jnp.where(iota == first + 2, left_over, 0.0)),
        )

    def pulls(high, low):
        top = jnp.concatenate([high, ones, low], axis=0)
        bottom = jnp.concatenate([high, ones, blank], axis=0)
        return jnp.concatenate([top, bottom], axis=1)

    def left_block(index, value):
        high, low = split(value)
        extra = norm_rows(value, 0) + jnp.where((iota >= 3) & (iota < 7), 1.0, 0.0)
        left_gram[index] = jnp.concatenate([high, low, high, extra.astype(BF16)], axis=0)
        left_pull[index] = pulls(high, low)
        left_acc[index] = jnp.zeros((PULL, BLK), F32)

    def right_block(index, value):
        high, low = split(value)
        extra = norm_rows(value, 3) + jnp.where((iota < 3) | (iota == 6), 1.0, 0.0)
        twice_high, twice_low = -2.0 * high.astype(F32), -2.0 * low.astype(F32)
        stack = jnp.concatenate([twice_high, twice_high, twice_low, extra], axis=0)
        right_gram[index] = stack.T.astype(BF16)
        right_pull[index] = pulls(high, low)
        right_acc[index] = jnp.zeros((PULL, BLK), F32)

    @pl.loop(0, col_count)
    def _(group):
        for block in range(CB):
            left_block(group * CB + block, row_y[group, :D_EMB, block * BLK : (block + 1) * BLK])

    for shift in range(row_count):
        for block in range(CB):
            right_block(shift * CB + block, col_y[shift][:D_EMB, block * BLK : (block + 1) * BLK])

    def kernel_of(left, right):
        return 1.0 / nn_dot(right_gram[right], left_gram[left])

    def apply(left, right, coefficient):
        high, low = split(coefficient)
        left_part = nn_dot(right_pull[right], jnp.concatenate([high, low], axis=0))
        right_part = nt_dot(left_pull[left], jnp.concatenate([high, low], axis=1))
        left_acc[left] += left_part
        right_acc[right] += right_part

    near = col_count // 2 + 1
    tiles = near + col_count * (shifts - 1)
    spare = lax.rem(col + col_count - 1, col_count) * shifts
    last = jnp.where(takes_shift(shifts - 1, row, row_count), tiles, tiles - col_count)

    @pl.loop(0, lax.div(last + UNROLL - 1, UNROLL))
    def _(step):
        for lane in range(UNROLL):
            index = step * UNROLL + lane
            far = jnp.maximum(index - near, 0)
            shift = jnp.where(index < near, 0, 1 + lax.div(far, col_count))
            group = jnp.where(index < near, lax.rem(col + index, col_count), lax.rem(far, col_count))
            inside = index < last
            shift = jnp.where(inside, shift, 0)
            slot = jnp.where(inside, group * shifts + shift, spare)
            entry = (group * row_count + lax.rem(row + shift, row_count)) * 2
            left = group * CB + listing[entry]
            right = shift * CB + listing[entry + 1]
            apply(left, right, weights[slot].astype(F32) * kernel_of(left, right))

    @pl.loop(0, lax.div(live + UNROLL - 1, UNROLL))
    def _(step):
        for lane in range(UNROLL):
            index = step * UNROLL + lane
            strength = jnp.where(index < live, -REPULSION, 0.0)
            place = jnp.minimum(index, live - 1)
            left = neg_rows[place]
            other = neg_cols[place]
            shift = lax.rem(lax.div(other, CB) - row + row_count, row_count)
            right = shift * CB + lax.rem(other, CB)
            kernel = kernel_of(left, right)
            apply(left, right, strength * kernel * kernel)

    def force_of(acc, value):
        return acc[:D_EMB] + acc[D_EMB + 16 :] - value * acc[D_EMB : D_EMB + 1]

    @pl.loop(0, col_count)
    def _(group):
        for block in range(CB):
            lanes = slice(block * BLK, (block + 1) * BLK)
            row_force[group, :, lanes] = force_of(left_acc[group * CB + block], row_y[group, :D_EMB, lanes])

    for shift in range(row_count):
        for block in range(CB):
            lanes = slice(block * BLK, (block + 1) * BLK)
            col_force[shift][:, lanes] = force_of(right_acc[shift * CB + block], col_y[shift][:D_EMB, lanes])


def pair_forces(row_count, col_count, meta, listing, neg_rows, neg_cols, weights, row_y, col_y):
    smem = pl.BlockSpec(memory_space=pltpu.SMEM)
    vmem = pl.BlockSpec(memory_space=pltpu.VMEM)
    lefts, rights = col_count * CB, row_count * CB
    tiles = col_count * 2 + 48
    weights = weights.reshape(-1, BLK, BLK)
    outs = pl.pallas_call(
        functools.partial(force_kernel, row_count, col_count),
        in_specs=[smem] * 4 + [vmem] * (2 + row_count),
        out_specs=[vmem] * (1 + row_count),
        out_shape=[jax.ShapeDtypeStruct((col_count, D_EMB, SPAN), F32)]
        + [jax.ShapeDtypeStruct((D_EMB, SPAN), F32)] * row_count,
        scratch_shapes=[
            pltpu.VMEM((lefts, STACK, BLK), BF16),
            pltpu.VMEM((rights, BLK, STACK), BF16),
            pltpu.VMEM((lefts, PULL, 2 * BLK), BF16),
            pltpu.VMEM((rights, PULL, 2 * BLK), BF16),
            pltpu.VMEM((lefts, PULL, BLK), F32),
            pltpu.VMEM((rights, PULL, BLK), F32),
        ],
        compiler_params=pltpu.CompilerParams(vmem_limit_bytes=VMEM_LIMIT),
        cost_estimate=pl.CostEstimate(
            flops=tiles * 2 * BLK * BLK * (STACK + 4 * PULL),
            bytes_accessed=4 * D_EMB * SPAN * 2 * (col_count + row_count),
            transcendentals=tiles * BLK * BLK,
        ),
        name="forces",
    )(meta, listing, neg_rows, neg_cols, weights, row_y, *col_y)
    return outs[0], outs[1:]


def shards(inputs, rho, sigma, embed, knn_blocks, knn_seeds, neg_rows, neg_cols, neg_count):
    row_count = lax.axis_size("row")
    col_count = lax.axis_size("col")
    shifts = row_count // 2 + 1
    row, col = lax.axis_index("row"), lax.axis_index("col")
    listing = knn_blocks.reshape(-1)
    seeds = knn_seeds.reshape(-1)
    row_list, col_list = neg_rows.reshape(-1), neg_cols.reshape(-1)
    meta = jnp.stack([row, col, neg_count[0, 0]]).astype(I32)

    def from_shift(value, shift):
        pairs = [((r + shift) % row_count, r) for r in range(row_count)]
        return lax.ppermute(value, "row", pairs)

    def from_half(value):
        half = row_count // 2
        pairs = [(r + half, r) if r % 2 == 0 else (r, r + half) for r in range(half)]
        return lax.ppermute(value, "row", pairs)

    def to_shift(value, shift):
        pairs = [(r, (r + shift) % row_count) for r in range(row_count)]
        return lax.ppermute(value, "row", pairs)

    row_x = lax.all_gather(inputs, "col", axis=0, tiled=False)
    col_x = [inputs]
    for shift in range(1, shifts):
        col_x.append(from_half(inputs) if 2 * shift == row_count else from_shift(inputs, shift))

    squares = jnp.sum(inputs * inputs, axis=1)
    seed_row = jnp.zeros((SPAN,), F32).at[: seeds.shape[0]].set(seeds.astype(F32))
    params = jnp.stack([rho, sigma, squares, seed_row])
    pack = jnp.concatenate([embed, params, jnp.zeros((PACK - D_EMB - 4, SPAN), F32)], axis=0)
    row_pack = lax.all_gather(pack, "col", axis=0, tiled=False)
    col_pack = [pack] + [from_shift(pack, shift) for shift in range(1, row_count)]

    plane_seeds = row_pack[:, SEEDS, : seeds.shape[0]].reshape(col_count, col_count, row_count)
    own_column = lax.dynamic_index_in_dim(plane_seeds, col, 1, keepdims=False)
    seeds_back = []
    for shift in range(shifts):
        wanted = lax.dynamic_index_in_dim(own_column, (row - shift) % row_count, 1, keepdims=False)
        seeds_back.append(from_shift(wanted, shift) if shift else wanted)
    seeds_back = jnp.concatenate(seeds_back).astype(I32)

    weights = pair_weights(
        row_count, col_count, meta, listing, seeds, seeds_back, row_x, row_pack, col_x, col_pack[:shifts]
    )

    row_y, col_y = row_pack, col_pack
    for step in range(STEPS):
        if step:
            row_y = lax.all_gather(embed, "col", axis=0, tiled=False)
            col_y = [embed] + [from_shift(embed, shift) for shift in range(1, row_count)]
        row_force, col_force = pair_forces(
            row_count, col_count, meta, listing, row_list, col_list, weights, row_y, col_y
        )
        row_parts = lax.all_to_all(row_force, "col", split_axis=0, concat_axis=0, tiled=True)
        force = jnp.sum(row_parts, axis=0) + col_force[0]
        for shift in range(1, row_count):
            force = force + to_shift(col_force[shift], shift)
        embed = embed + STEP_SIZE * force
    return (embed, force * FORCE_SCALE)


def solution(mesh):
    in_specs = (
        P(("row", "col"), None),
        P(("row", "col")),
        P(("row", "col")),
        P(None, ("row", "col")),
        P("row", "col", None, None, None),
        P("row", "col", None, None),
        P("row", "col", None),
        P("row", "col", None),
        P("row", "col"),
    )
    out_specs = (P(None, ("row", "col")), P(None, ("row", "col")))
    return jax.shard_map(shards, mesh=mesh, in_specs=in_specs, out_specs=out_specs, check_vma=False)
```

```python
import functools

import jax
import jax.numpy as jnp
from jax import lax
from jax.experimental import pallas as pl
from jax.experimental.pallas import tpu as pltpu
from jax.sharding import PartitionSpec as P

D_EMB = 64
BLK = 128
CB = 2
SPAN = CB * BLK
STEPS = 2

STEP_SIZE = 0.0005
REPULSION = 2.0
FORCE_SCALE = 0.015625

RHO, SIGMA, SQUARES, SEEDS = D_EMB, D_EMB + 1, D_EMB + 2, D_EMB + 3
PACK = 72
STACK = 4 * D_EMB
PULL = 2 * D_EMB + 16
UNROLL = 12
F32, BF16, I32 = jnp.float32, jnp.bfloat16, jnp.int32
VMEM_LIMIT = 56 * 2**20


def split(value):
    high = value.astype(BF16)
    return high, (value - high.astype(F32)).astype(BF16)


def nt_dot(left, right):
    return lax.dot_general(left, right, (((1,), (1,)), ((), ())), preferred_element_type=F32)


def nn_dot(left, right):
    return lax.dot_general(left, right, (((1,), (0,)), ((), ())), preferred_element_type=F32)


def hash_bits(salt_value, first, second):
    mixed = first * 1103515245 + salt_value
    mixed = (mixed ^ second * 747796405) * 277803737
    return (mixed >> 17 & 1).astype(F32)


def takes_shift(shift, row, row_count):
    if 2 * shift != row_count:
        return True
    half = row_count // 2
    return jnp.where(row < half, row % 2 == 0, (row - half) % 2 == 1)


def weights_kernel(sizes, plan, spans, meta, listing, seeds, seeds_back, *rest):
    row_count, col_count = sizes
    row_spans, col_spans = spans
    count = len(row_spans) + len(col_spans)
    arrays = rest[: len(rest) - 7 - count]
    packs = rest[len(arrays) : len(arrays) + count]
    out, raw, high, low, col_params, grams, sems = rest[len(arrays) + count :]
    row, col = meta[0], meta[1]
    places = col_spans + row_spans
    copies = []
    for place, (array, index) in enumerate(places):
        source = arrays[array] if index is None else arrays[array].at[index]
        copies.append(pltpu.make_async_copy(source, raw.at[place], sems.at[place]))
        copies[-1].start()
    for place in range(len(col_spans)):
        for block in range(CB):
            params = packs[place][RHO : RHO + 8, block * BLK : (block + 1) * BLK]
            col_params[place, block] = params.T
    positions_j = lax.broadcasted_iota(I32, (BLK, BLK), 0)
    positions_i = lax.broadcasted_iota(I32, (BLK, BLK), 1)

    def take(place):
        copies[place].wait()
        high[place], low[place] = split(raw[place])

    for place in range(len(col_spans)):
        take(place)
    for line in range(len(row_spans)):
        place = len(col_spans) + line
        take(place)
        tiles = [(tile, entry) for tile, entry in enumerate(plan) if entry[0] == line]
        picks = {}
        for tile, (_, column, shift) in tiles:
            group = meta[3 + line]
            other = lax.rem(row + shift, row_count)
            entry = (group * row_count + other) * 2
            start_i = pl.multiple_of(listing[entry] * BLK, BLK)
            start_j = pl.multiple_of(listing[entry + 1] * BLK, BLK)
            picks[tile] = group, other, start_i, listing[entry + 1]
            high_j, low_j = high[column, pl.ds(start_j, BLK), :], low[column, pl.ds(start_j, BLK), :]
            high_i, low_i = high[place, pl.ds(start_i, BLK), :], low[place, pl.ds(start_i, BLK), :]
            grams[tile] = nt_dot(high_j, low_i) + nt_dot(low_j, high_i) + nt_dot(high_j, high_i)
        for tile, (_, column, shift) in tiles:
            group, other, start_i, col_pick = picks[tile]
            params_i = packs[place][RHO : RHO + 8, pl.ds(start_i, BLK)]
            rho_i, sigma_i, square_i = params_i[0:1], params_i[1:2], params_i[2:3]
            params_j = col_params[column, col_pick]
            rho_j, sigma_j, square_j = params_j[:, 0:1], params_j[:, 1:2], params_j[:, 2:3]
            total = square_j + square_i - 2.0 * grams[tile]
            distance = jnp.sqrt(jnp.maximum(total, 1.0))
            seed = seeds[group * row_count + other]
            seed_back = seeds_back[shift * col_count + group]
            ahead = hash_bits(seed, positions_i, positions_j) * jnp.exp(
                jnp.maximum(distance - rho_i, 0.0) * (-1.0 / sigma_i)
            )
            behind = hash_bits(seed_back, positions_j, positions_i) * jnp.exp(
                jnp.maximum(distance - rho_j, 0.0) * (-1.0 / sigma_j)
            )
            weights = (ahead + behind - ahead * behind).astype(BF16)
            if shift == 0:
                weights = (weights.astype(F32) * jnp.where(group == col, 0.5, 1.0)).astype(BF16)
            out[tile] = weights


def pair_weights(sizes, plan, row_spans, col_spans, meta, listing, seeds, seeds_back, arrays, packs):
    depth = arrays[0].shape[-1]
    smem = pl.BlockSpec(memory_space=pltpu.SMEM)
    vmem = pl.BlockSpec(memory_space=pltpu.VMEM)
    tiles, count = len(plan), len(row_spans) + len(col_spans)
    return pl.pallas_call(
        functools.partial(weights_kernel, sizes, plan, (row_spans, col_spans)),
        in_specs=[smem] * 4 + [pl.BlockSpec(memory_space=pl.ANY)] * len(arrays) + [vmem] * count,
        out_specs=vmem,
        out_shape=jax.ShapeDtypeStruct((tiles, BLK, BLK), BF16),
        scratch_shapes=[
            pltpu.VMEM((count, SPAN, depth), F32),
            pltpu.VMEM((count, SPAN, depth), BF16),
            pltpu.VMEM((count, SPAN, depth), BF16),
            pltpu.VMEM((len(col_spans), CB, BLK, 8), F32),
            pltpu.VMEM((tiles, BLK, BLK), F32),
            pltpu.SemaphoreType.DMA((count,)),
        ],
        compiler_params=pltpu.CompilerParams(vmem_limit_bytes=VMEM_LIMIT),
        cost_estimate=pl.CostEstimate(
            flops=tiles * 6 * BLK * BLK * depth,
            bytes_accessed=count * SPAN * depth * 4,
            transcendentals=tiles * 3 * BLK * BLK,
        ),
        name="weights",
    )(meta, listing, seeds, seeds_back, *arrays, *packs)


def force_kernel(row_count, col_count, meta, listing, neg_rows, neg_cols, weights, row_y, *rest):
    shifts = row_count // 2 + 1
    col_y = rest[:row_count]
    row_force, col_force = rest[row_count], rest[row_count + 1 : 2 * row_count + 1]
    left_gram, right_gram, left_pull, right_pull, left_acc, right_acc, held_v, held_h = rest[2 * row_count + 1 :]
    row, col, live = meta[0], meta[1], meta[2]
    iota = lax.broadcasted_iota(I32, (D_EMB, BLK), 0)
    ones = jnp.ones((16, BLK), BF16)
    blank = jnp.zeros((D_EMB, BLK), BF16)

    def norm_rows(value, first):
        norm = jnp.sum(value * value, axis=0, keepdims=True)
        high, rest_ = split(norm)
        left_over = norm - high.astype(F32) - rest_.astype(F32)
        high, middle = high.astype(F32), rest_.astype(F32)
        return jnp.where(
            iota == first,
            high,
            jnp.where(iota == first + 1, middle, jnp.where(iota == first + 2, left_over, 0.0)),
        )

    def pulls(high, low):
        top = jnp.concatenate([high, ones, low], axis=0)
        bottom = jnp.concatenate([high, ones, blank], axis=0)
        return jnp.concatenate([top, bottom], axis=1)

    def left_block(index, value):
        high, low = split(value)
        extra = norm_rows(value, 0) + jnp.where((iota >= 3) & (iota < 7), 1.0, 0.0)
        left_gram[index] = jnp.concatenate([high, low, high, extra.astype(BF16)], axis=0)
        left_pull[index] = pulls(high, low)
        left_acc[index] = jnp.zeros((PULL, BLK), F32)

    def right_block(index, value):
        high, low = split(value)
        extra = norm_rows(value, 3) + jnp.where((iota < 3) | (iota == 6), 1.0, 0.0)
        twice_high, twice_low = -2.0 * high.astype(F32), -2.0 * low.astype(F32)
        stack = jnp.concatenate([twice_high, twice_high, twice_low, extra], axis=0)
        right_gram[index] = stack.T.astype(BF16)
        right_pull[index] = pulls(high, low)
        right_acc[index] = jnp.zeros((PULL, BLK), F32)

    @pl.loop(0, col_count)
    def _(group):
        for block in range(CB):
            left_block(group * CB + block, row_y[group, :D_EMB, block * BLK : (block + 1) * BLK])

    for shift in range(row_count):
        for block in range(CB):
            right_block(shift * CB + block, col_y[shift][:D_EMB, block * BLK : (block + 1) * BLK])

    def kernel_of(left, right):
        return 1.0 / nn_dot(right_gram[right], left_gram[left])

    def apply_all(tiles_):
        for lane, (left, right, coefficient) in enumerate(tiles_):
            high, low = split(coefficient())
            held_v[lane, :BLK], held_v[lane, BLK:] = high, low
            held_h[lane, :, :BLK], held_h[lane, :, BLK:] = high, low
        for lane, (left, right, _) in enumerate(tiles_):
            left_acc[left] += nn_dot(right_pull[right], held_v[lane])
        for lane, (left, right, _) in enumerate(tiles_):
            right_acc[right] += nt_dot(left_pull[left], held_h[lane])

    def near_active(group):
        offset = lax.rem(group - col + col_count, col_count)
        return (2 * offset < col_count) | ((2 * offset == col_count) & (2 * col < col_count))

    near = col_count // 2 + 1
    tiles = near + col_count * (shifts - 1)
    last = jnp.where(takes_shift(shifts - 1, row, row_count), tiles, tiles - col_count)

    @pl.loop(0, lax.div(last + UNROLL - 1, UNROLL))
    def _(step):
        batch = []
        for lane in range(UNROLL):
            index = step * UNROLL + lane
            far = jnp.maximum(index - near, 0)
            shift = jnp.where(index < near, 0, 1 + lax.div(far, col_count))
            group = jnp.where(index < near, lax.rem(col + index, col_count), lax.rem(far, col_count))
            inside = index < last
            shift = jnp.where(inside, shift, 0)
            inside &= (shift > 0) | near_active(group)
            slot = shift * col_count + group
            entry = (group * row_count + lax.rem(row + shift, row_count)) * 2
            left = group * CB + listing[entry]
            right = shift * CB + listing[entry + 1]

            def pull(left=left, right=right, slot=slot, inside=inside):
                return weights[slot].astype(F32) * (kernel_of(left, right) * jnp.where(inside, 1.0, 0.0))

            batch.append((left, right, pull))
        apply_all(batch)

    @pl.loop(0, lax.div(live + UNROLL - 1, UNROLL))
    def _(step):
        batch = []
        for lane in range(UNROLL):
            index = step * UNROLL + lane
            strength = jnp.where(index < live, -REPULSION, 0.0)
            place = jnp.minimum(index, live - 1)
            left = neg_rows[place]
            other = neg_cols[place]
            shift = lax.rem(lax.div(other, CB) - row + row_count, row_count)
            right = shift * CB + lax.rem(other, CB)
            def push(left=left, right=right, strength=strength):
                kernel = kernel_of(left, right)
                return strength * kernel * kernel
            batch.append((left, right, push))
        apply_all(batch)

    def force_of(acc, value):
        return acc[:D_EMB] + acc[D_EMB + 16 :] - value * acc[D_EMB : D_EMB + 1]

    @pl.loop(0, col_count)
    def _(group):
        for block in range(CB):
            lanes = slice(block * BLK, (block + 1) * BLK)
            row_force[group, :, lanes] = force_of(left_acc[group * CB + block], row_y[group, :D_EMB, lanes])

    for shift in range(row_count):
        for block in range(CB):
            lanes = slice(block * BLK, (block + 1) * BLK)
            col_force[shift][:, lanes] = force_of(right_acc[shift * CB + block], col_y[shift][:D_EMB, lanes])


def pair_forces(row_count, col_count, meta, listing, neg_rows, neg_cols, weights, row_y, col_y):
    smem = pl.BlockSpec(memory_space=pltpu.SMEM)
    vmem = pl.BlockSpec(memory_space=pltpu.VMEM)
    lefts, rights = col_count * CB, row_count * CB
    tiles = col_count * 2 + 48
    outs = pl.pallas_call(
        functools.partial(force_kernel, row_count, col_count),
        in_specs=[smem] * 4 + [vmem] * (2 + row_count),
        out_specs=[vmem] * (1 + row_count),
        out_shape=[jax.ShapeDtypeStruct((col_count, D_EMB, SPAN), F32)]
        + [jax.ShapeDtypeStruct((D_EMB, SPAN), F32)] * row_count,
        scratch_shapes=[
            pltpu.VMEM((lefts, STACK, BLK), BF16),
            pltpu.VMEM((rights, BLK, STACK), BF16),
            pltpu.VMEM((lefts, PULL, 2 * BLK), BF16),
            pltpu.VMEM((rights, PULL, 2 * BLK), BF16),
            pltpu.VMEM((lefts, PULL, BLK), F32),
            pltpu.VMEM((rights, PULL, BLK), F32),
            pltpu.VMEM((UNROLL, 2 * BLK, BLK), BF16),
            pltpu.VMEM((UNROLL, BLK, 2 * BLK), BF16),
        ],
        compiler_params=pltpu.CompilerParams(vmem_limit_bytes=VMEM_LIMIT),
        cost_estimate=pl.CostEstimate(
            flops=tiles * 2 * BLK * BLK * (STACK + 4 * PULL),
            bytes_accessed=4 * D_EMB * SPAN * 2 * (col_count + row_count),
            transcendentals=tiles * BLK * BLK,
        ),
        name="forces",
    )(meta, listing, neg_rows, neg_cols, weights, row_y, *col_y)
    return outs[0], outs[1:]


def shards(inputs, rho, sigma, embed, knn_blocks, knn_seeds, neg_rows, neg_cols, neg_count):
    row_count = lax.axis_size("row")
    col_count = lax.axis_size("col")
    shifts = row_count // 2 + 1
    row, col = lax.axis_index("row"), lax.axis_index("col")
    listing = knn_blocks.reshape(-1)
    seeds = knn_seeds.reshape(-1)
    row_list, col_list = neg_rows.reshape(-1), neg_cols.reshape(-1)
    meta = jnp.stack([row, col, neg_count[0, 0]]).astype(I32)

    def from_shift(value, shift):
        pairs = [((r + shift) % row_count, r) for r in range(row_count)]
        return lax.ppermute(value, "row", pairs)

    def from_half(value):
        half = row_count // 2
        pairs = [(r + half, r) if r % 2 == 0 else (r, r + half) for r in range(half)]
        return lax.ppermute(value, "row", pairs)

    def to_shift(value, shift):
        pairs = [(r, (r + shift) % row_count) for r in range(row_count)]
        return lax.ppermute(value, "row", pairs)

    row_x = lax.all_gather(inputs, "col", axis=0, tiled=False)
    col_x = [inputs]
    for shift in range(1, shifts):
        col_x.append(from_half(inputs) if 2 * shift == row_count else from_shift(inputs, shift))

    squares = jnp.sum(inputs * inputs, axis=1)
    seed_row = jnp.zeros((SPAN,), F32).at[: seeds.shape[0]].set(seeds.astype(F32))
    params = jnp.stack([rho, sigma, squares, seed_row])
    pack = jnp.concatenate([embed, params, jnp.zeros((PACK - D_EMB - 4, SPAN), F32)], axis=0)
    row_pack = lax.all_gather(pack, "col", axis=0, tiled=False)
    col_pack = [pack] + [from_shift(pack, shift) for shift in range(1, row_count)]

    plane_seeds = row_pack[:, SEEDS, : seeds.shape[0]].reshape(col_count, col_count, row_count)
    own_column = lax.dynamic_index_in_dim(plane_seeds, col, 1, keepdims=False)
    seeds_back = []
    for shift in range(shifts):
        wanted = lax.dynamic_index_in_dim(own_column, (row - shift) % row_count, 1, keepdims=False)
        seeds_back.append(from_shift(wanted, shift) if shift else wanted)
    seeds_back = jnp.concatenate(seeds_back).astype(I32)

    sizes = row_count, col_count
    plan = [(group, shift, shift) for shift in range(shifts) for group in range(col_count)]
    row_spans = [(0, group) for group in range(col_count)]
    col_spans = [(1 + shift, None) for shift in range(shifts)]
    row_packs = [row_pack[group] for group in range(col_count)]
    weights = pair_weights(
        sizes,
        plan,
        row_spans,
        col_spans,
        jnp.concatenate([meta, jnp.arange(col_count, dtype=I32)]),
        listing,
        seeds,
        seeds_back,
        [row_x] + col_x,
        col_pack[:shifts] + row_packs,
    )

    row_y, col_y = row_pack, col_pack
    for step in range(STEPS):
        if step:
            row_y = lax.all_gather(embed, "col", axis=0, tiled=False)
            col_y = [embed] + [from_shift(embed, shift) for shift in range(1, row_count)]
        row_force, col_force = pair_forces(
            row_count, col_count, meta, listing, row_list, col_list, weights, row_y, col_y
        )
        row_parts = lax.all_to_all(row_force, "col", split_axis=0, concat_axis=0, tiled=True)
        force = jnp.sum(row_parts, axis=0) + col_force[0]
        for shift in range(1, row_count):
            force = force + to_shift(col_force[shift], shift)
        embed = embed + STEP_SIZE * force
    return (embed, force * FORCE_SCALE)


def solution(mesh):
    in_specs = (
        P(("row", "col"), None),
        P(("row", "col")),
        P(("row", "col")),
        P(None, ("row", "col")),
        P("row", "col", None, None, None),
        P("row", "col", None, None),
        P("row", "col", None),
        P("row", "col", None),
        P("row", "col"),
    )
    out_specs = (P(None, ("row", "col")), P(None, ("row", "col")))
    return jax.shard_map(shards, mesh=mesh, in_specs=in_specs, out_specs=out_specs, check_vma=False)
```

```python
import functools

import jax
import jax.numpy as jnp
from jax import lax
from jax.experimental import pallas as pl
from jax.experimental.pallas import tpu as pltpu
from jax.sharding import PartitionSpec as P

D_EMB = 64
BLK = 128
CB = 2
SPAN = CB * BLK
STEPS = 2

STEP_SIZE = 0.0005
REPULSION = 2.0
FORCE_SCALE = 0.015625

RHO, SIGMA, SQUARES, SEEDS = D_EMB, D_EMB + 1, D_EMB + 2, D_EMB + 3
PACK = 72
STACK = 4 * D_EMB
PULL = 2 * D_EMB + 16
UNROLL = 12
F32, BF16, I32 = jnp.float32, jnp.bfloat16, jnp.int32
VMEM_LIMIT = 44 * 2**20


def split(value):
    high = value.astype(BF16)
    return high, (value - high.astype(F32)).astype(BF16)


def nt_dot(left, right):
    return lax.dot_general(left, right, (((1,), (1,)), ((), ())), preferred_element_type=F32)


def nn_dot(left, right):
    return lax.dot_general(left, right, (((1,), (0,)), ((), ())), preferred_element_type=F32)


def hash_bits(salt_value, first, second):
    mixed = first * 1103515245 + salt_value
    mixed = (mixed ^ second * 747796405) * 277803737
    return (mixed >> 17 & 1).astype(F32)


def takes_shift(shift, row, row_count):
    if 2 * shift != row_count:
        return True
    half = row_count // 2
    return jnp.where(row < half, row % 2 == 0, (row - half) % 2 == 1)


def weights_kernel(sizes, plan, spans, meta, listing, seeds, *rest):
    row_count, col_count = sizes
    col_spans, row_spans = spans
    count = row_spans + col_spans
    arrays, packs = rest[:count], rest[count : 2 * count]
    out, high, low, col_params, grams = rest[2 * count :]
    row, col = meta[0], meta[1]
    for place in range(col_spans):
        for block in range(CB):
            params = packs[place][RHO : RHO + 8, block * BLK : (block + 1) * BLK]
            col_params[place, block] = params.T
    positions_j = lax.broadcasted_iota(I32, (BLK, BLK), 0)
    positions_i = lax.broadcasted_iota(I32, (BLK, BLK), 1)
    wanted_seed = lax.broadcasted_iota(I32, (1, SPAN), 1) == col * row_count + row

    for place in range(col_spans):
        high[place], low[place] = split(arrays[place][...])
    for line in range(row_spans):
        place = col_spans + line
        high[place], low[place] = split(arrays[place][...])
        group = lax.bitwise_xor(col, line)
        tiles = [(tile, entry) for tile, entry in enumerate(plan) if entry[0] == line]
        picks = {}
        for tile, (_, column, shift) in tiles:
            other = lax.rem(row + shift, row_count)
            entry = (group * row_count + other) * 2
            start_i = pl.multiple_of(listing[entry] * BLK, BLK)
            start_j = pl.multiple_of(listing[entry + 1] * BLK, BLK)
            picks[tile] = other, start_i, listing[entry + 1]
            high_j, low_j = high[column, pl.ds(start_j, BLK), :], low[column, pl.ds(start_j, BLK), :]
            high_i, low_i = high[place, pl.ds(start_i, BLK), :], low[place, pl.ds(start_i, BLK), :]
            grams[tile] = nt_dot(high_j, low_i) + nt_dot(low_j, high_i) + nt_dot(high_j, high_i)
        for tile, (_, column, shift) in tiles:
            other, start_i, col_pick = picks[tile]
            params_i = packs[place][RHO : RHO + 8, pl.ds(start_i, BLK)]
            rho_i, sigma_i, square_i = params_i[0:1], params_i[1:2], params_i[2:3]
            params_j = col_params[column, col_pick]
            rho_j, sigma_j, square_j = params_j[:, 0:1], params_j[:, 1:2], params_j[:, 2:3]
            total = square_j + square_i - 2.0 * grams[tile]
            distance = jnp.sqrt(jnp.maximum(total, 1.0))
            seed = seeds[group * row_count + other]
            plane_seeds = packs[place][SEEDS + shift : SEEDS + shift + 1, :]
            seed_back = jnp.sum(jnp.where(wanted_seed, plane_seeds, 0.0), axis=1, keepdims=True).astype(I32)
            ahead = hash_bits(seed, positions_i, positions_j) * jnp.exp(
                jnp.maximum(distance - rho_i, 0.0) * (-1.0 / sigma_i)
            )
            behind = hash_bits(seed_back, positions_j, positions_i) * jnp.exp(
                jnp.maximum(distance - rho_j, 0.0) * (-1.0 / sigma_j)
            )
            weights = (ahead + behind - ahead * behind).astype(BF16)
            if shift == 0 and line == 0:
                weights = (weights.astype(F32) * 0.5).astype(BF16)
            out[tile] = weights


def pair_weights(sizes, plan, col_spans, meta, listing, seeds, arrays, packs):
    depth = arrays[0].shape[-1]
    smem = pl.BlockSpec(memory_space=pltpu.SMEM)
    vmem = pl.BlockSpec(memory_space=pltpu.VMEM)
    tiles, count = len(plan), len(arrays)
    return pl.pallas_call(
        functools.partial(weights_kernel, sizes, plan, (col_spans, count - col_spans)),
        in_specs=[smem] * 3 + [vmem] * (2 * count),
        out_specs=vmem,
        out_shape=jax.ShapeDtypeStruct((tiles, BLK, BLK), BF16),
        scratch_shapes=[
            pltpu.VMEM((count, SPAN, depth), BF16),
            pltpu.VMEM((count, SPAN, depth), BF16),
            pltpu.VMEM((col_spans, CB, BLK, 8), F32),
            pltpu.VMEM((tiles, BLK, BLK), F32),
        ],
        compiler_params=pltpu.CompilerParams(vmem_limit_bytes=VMEM_LIMIT),
        cost_estimate=pl.CostEstimate(
            flops=tiles * 6 * BLK * BLK * depth,
            bytes_accessed=count * SPAN * depth * 4,
            transcendentals=tiles * 3 * BLK * BLK,
        ),
        name="weights",
    )(meta, listing, seeds, *arrays, *packs)


def force_kernel(row_count, col_count, by_bits, meta, listing, neg_rows, neg_cols, weights, *rest):
    shifts = row_count // 2 + 1
    row_arrays, rest = (rest[:2], rest[2:]) if by_bits else (rest[:1], rest[1:])
    col_y = rest[:row_count]
    row_force, col_force = rest[row_count], rest[row_count + 1 : 2 * row_count + 1]
    left_gram, right_gram, left_pull, right_pull, left_acc, right_acc, held_v, held_h = rest[2 * row_count + 1 :]
    row, col, live = meta[0], meta[1], meta[2]
    iota = lax.broadcasted_iota(I32, (D_EMB, BLK), 0)
    ones = jnp.ones((16, BLK), BF16)
    blank = jnp.zeros((D_EMB, BLK), BF16)

    def norm_rows(value, first):
        norm = jnp.sum(value * value, axis=0, keepdims=True)
        high, rest_ = split(norm)
        left_over = norm - high.astype(F32) - rest_.astype(F32)
        high, middle = high.astype(F32), rest_.astype(F32)
        return jnp.where(
            iota == first,
            high,
            jnp.where(iota == first + 1, middle, jnp.where(iota == first + 2, left_over, 0.0)),
        )

    def pulls(high, low):
        top = jnp.concatenate([high, ones, low], axis=0)
        bottom = jnp.concatenate([high, ones, blank], axis=0)
        return jnp.concatenate([top, bottom], axis=1)

    def left_block(index, value):
        high, low = split(value)
        extra = norm_rows(value, 0) + jnp.where((iota >= 3) & (iota < 7), 1.0, 0.0)
        left_gram[index] = jnp.concatenate([high, low, high, extra.astype(BF16)], axis=0)
        left_pull[index] = pulls(high, low)
        left_acc[index] = jnp.zeros((PULL, BLK), F32)

    def right_block(index, value):
        high, low = split(value)
        extra = norm_rows(value, 3) + jnp.where((iota < 3) | (iota == 6), 1.0, 0.0)
        twice_high, twice_low = -2.0 * high.astype(F32), -2.0 * low.astype(F32)
        stack = jnp.concatenate([twice_high, twice_high, twice_low, extra], axis=0)
        right_gram[index] = stack.T.astype(BF16)
        right_pull[index] = pulls(high, low)
        right_acc[index] = jnp.zeros((PULL, BLK), F32)

    def row_y(line, block):
        lanes = slice(block * BLK, (block + 1) * BLK)
        if by_bits:
            return row_arrays[line % 2][line // 2, :D_EMB, lanes], lax.bitwise_xor(line, col)
        return row_arrays[0][line, :D_EMB, lanes], line

    for line in range(col_count):
        for block in range(CB):
            value, group = row_y(line, block)
            left_block(group * CB + block, value)

    for shift in range(row_count):
        for block in range(CB):
            right_block(shift * CB + block, col_y[shift][:D_EMB, block * BLK : (block + 1) * BLK])

    def kernel_of(left, right):
        return 1.0 / nn_dot(right_gram[right], left_gram[left])

    def apply_all(tiles_):
        for lane, (left, right, coefficient) in enumerate(tiles_):
            high, low = split(coefficient())
            held_v[lane, :BLK], held_v[lane, BLK:] = high, low
            held_h[lane, :, :BLK], held_h[lane, :, BLK:] = high, low
        for lane, (left, right, _) in enumerate(tiles_):
            left_acc[left] += nn_dot(right_pull[right], held_v[lane])
        for lane, (left, right, _) in enumerate(tiles_):
            right_acc[right] += nt_dot(left_pull[left], held_h[lane])

    def near_active(group):
        offset = lax.rem(group - col + col_count, col_count)
        return (2 * offset < col_count) | ((2 * offset == col_count) & (2 * col < col_count))

    near = col_count // 2 + 1
    tiles = near + col_count * (shifts - 1)
    last = jnp.where(takes_shift(shifts - 1, row, row_count), tiles, tiles - col_count)

    @pl.loop(0, lax.div(last + UNROLL - 1, UNROLL))
    def _(step):
        batch = []
        for lane in range(UNROLL):
            index = step * UNROLL + lane
            far = jnp.maximum(index - near, 0)
            shift = jnp.where(index < near, 0, 1 + lax.div(far, col_count))
            group = jnp.where(index < near, lax.rem(col + index, col_count), lax.rem(far, col_count))
            inside = index < last
            shift = jnp.where(inside, shift, 0)
            inside &= (shift > 0) | near_active(group)
            slot = shift * col_count + lax.bitwise_xor(group, col)
            entry = (group * row_count + lax.rem(row + shift, row_count)) * 2
            left = group * CB + listing[entry]
            right = shift * CB + listing[entry + 1]

            def pull(left=left, right=right, slot=slot, inside=inside):
                return weights[slot].astype(F32) * (kernel_of(left, right) * jnp.where(inside, 1.0, 0.0))

            batch.append((left, right, pull))
        apply_all(batch)

    @pl.loop(0, lax.div(live + UNROLL - 1, UNROLL))
    def _(step):
        batch = []
        for lane in range(UNROLL):
            index = step * UNROLL + lane
            strength = jnp.where(index < live, -REPULSION, 0.0)
            place = jnp.minimum(index, live - 1)
            left = neg_rows[place]
            other = neg_cols[place]
            shift = lax.rem(lax.div(other, CB) - row + row_count, row_count)
            right = shift * CB + lax.rem(other, CB)
            def push(left=left, right=right, strength=strength):
                kernel = kernel_of(left, right)
                return strength * kernel * kernel
            batch.append((left, right, push))
        apply_all(batch)

    def force_of(acc, value):
        return acc[:D_EMB] + acc[D_EMB + 16 :] - value * acc[D_EMB : D_EMB + 1]

    for line in range(col_count):
        for block in range(CB):
            value, group = row_y(line, block)
            lanes = slice(block * BLK, (block + 1) * BLK)
            row_force[group, :, lanes] = force_of(left_acc[group * CB + block], value)

    for shift in range(row_count):
        for block in range(CB):
            lanes = slice(block * BLK, (block + 1) * BLK)
            col_force[shift][:, lanes] = force_of(right_acc[shift * CB + block], col_y[shift][:D_EMB, lanes])


def pair_forces(sizes, meta, listing, neg_rows, neg_cols, weights, row_y, col_y):
    row_count, col_count = sizes
    smem = pl.BlockSpec(memory_space=pltpu.SMEM)
    vmem = pl.BlockSpec(memory_space=pltpu.VMEM)
    lefts, rights = col_count * CB, row_count * CB
    tiles = col_count * 2 + 48
    outs = pl.pallas_call(
        functools.partial(force_kernel, row_count, col_count, len(row_y) > 1),
        in_specs=[smem] * 4 + [vmem] * (1 + len(row_y) + row_count),
        out_specs=[vmem] * (1 + row_count),
        out_shape=[jax.ShapeDtypeStruct((col_count, D_EMB, SPAN), F32)]
        + [jax.ShapeDtypeStruct((D_EMB, SPAN), F32)] * row_count,
        scratch_shapes=[
            pltpu.VMEM((lefts, STACK, BLK), BF16),
            pltpu.VMEM((rights, BLK, STACK), BF16),
            pltpu.VMEM((lefts, PULL, 2 * BLK), BF16),
            pltpu.VMEM((rights, PULL, 2 * BLK), BF16),
            pltpu.VMEM((lefts, PULL, BLK), F32),
            pltpu.VMEM((rights, PULL, BLK), F32),
            pltpu.VMEM((UNROLL, 2 * BLK, BLK), BF16),
            pltpu.VMEM((UNROLL, BLK, 2 * BLK), BF16),
        ],
        compiler_params=pltpu.CompilerParams(vmem_limit_bytes=VMEM_LIMIT),
        cost_estimate=pl.CostEstimate(
            flops=tiles * 2 * BLK * BLK * (STACK + 4 * PULL),
            bytes_accessed=4 * D_EMB * SPAN * 2 * (col_count + row_count),
            transcendentals=tiles * BLK * BLK,
        ),
        name="forces",
    )(meta, listing, neg_rows, neg_cols, weights, *row_y, *col_y)
    return outs[0], outs[1:]


def shards(inputs, rho, sigma, embed, knn_blocks, knn_seeds, neg_rows, neg_cols, neg_count):
    row_count = lax.axis_size("row")
    col_count = lax.axis_size("col")
    shifts = row_count // 2 + 1
    row, col = lax.axis_index("row"), lax.axis_index("col")
    listing = knn_blocks.reshape(-1)
    seeds = knn_seeds.reshape(-1)
    row_list, col_list = neg_rows.reshape(-1), neg_cols.reshape(-1)
    meta = jnp.stack([row, col, neg_count[0, 0]]).astype(I32)

    def from_shift(value, shift):
        pairs = [((r + shift) % row_count, r) for r in range(row_count)]
        return lax.ppermute(value, "row", pairs)

    def from_half(value):
        half = row_count // 2
        pairs = [(r + half, r) if r % 2 == 0 else (r, r + half) for r in range(half)]
        return lax.ppermute(value, "row", pairs)

    def to_shift(value, shift):
        pairs = [(r, (r + shift) % row_count) for r in range(row_count)]
        return lax.ppermute(value, "row", pairs)

    def from_bits(value, bits):
        pairs = [(c ^ bits, c) for c in range(col_count)]
        return lax.ppermute(value, "col", pairs)

    sizes = row_count, col_count
    squares = jnp.sum(inputs * inputs, axis=1)
    seed_row = jnp.zeros((SPAN,), F32).at[: seeds.shape[0]].set(seeds.astype(F32))
    params = jnp.stack([rho, sigma, squares, seed_row])
    pack = jnp.concatenate([embed, params, jnp.zeros((PACK - D_EMB - 4, SPAN), F32)], axis=0)

    def after(value, *others):
        return lax.optimization_barrier((value, *others))[0]

    row_x = {0: inputs}
    bits = 2
    while bits < col_count:
        row_x[bits] = from_bits(inputs, bits)
        bits *= 2
    col_x = [inputs]
    for shift in range(1, shifts):
        if 2 * shift < row_count:
            col_x.append(from_shift(inputs, shift))
    row_x[1] = from_bits(after(inputs, pack), 1)
    col_pack = [pack] + [from_shift(pack, shift) for shift in range(1, shifts)]
    first = [row_x[2], row_x[4], *col_x[1:], *col_pack[1:]]
    if row_count % 2 == 0:
        col_x.append(from_half(after(inputs, *first)))
    for bits in range(2, col_count, 2):
        if bits not in row_x:
            row_x[bits] = from_bits(after(inputs, *first), bits)
    for bits in range(2, col_count, 2):
        row_x[bits + 1] = from_bits(row_x[bits], 1)
    swapped = [row_x[3], row_x[5]]
    col_pack += [from_shift(after(pack, *swapped), shift) for shift in range(shifts, row_count)]

    own_pack = jnp.concatenate(
        [pack[: SEEDS + 1]]
        + [col_pack[shift][SEEDS : SEEDS + 1] for shift in range(1, shifts)]
        + [pack[SEEDS + shifts :]],
        axis=0,
    )
    own_pack = after(own_pack, *swapped)
    even_packs = jnp.stack([own_pack] + [from_bits(own_pack, bits) for bits in range(2, col_count, 2)])
    odd_packs = from_bits(even_packs, 1)
    row_packs = [(even_packs, odd_packs)[bits % 2][bits // 2] for bits in range(col_count)]

    plan = [(bits, shift, shift) for shift in range(shifts) for bits in range(col_count)]
    weights = pair_weights(
        sizes,
        plan,
        shifts,
        meta,
        listing,
        seeds,
        col_x + [row_x[bits] for bits in range(col_count)],
        col_pack[:shifts] + row_packs,
    )

    row_y, col_y = (even_packs, odd_packs), col_pack
    for step in range(STEPS):
        if step:
            row_y = (lax.all_gather(embed, "col", axis=0, tiled=False),)
            col_y = [embed] + [from_shift(embed, shift) for shift in range(1, row_count)]
        row_force, col_force = pair_forces(sizes, meta, listing, row_list, col_list, weights, row_y, col_y)
        row_parts = lax.all_to_all(row_force, "col", split_axis=0, concat_axis=0, tiled=True)
        force = jnp.sum(row_parts, axis=0) + col_force[0]
        for shift in range(1, row_count):
            force = force + to_shift(col_force[shift], shift)
        embed = embed + STEP_SIZE * force
    return (embed, force * FORCE_SCALE)


def solution(mesh):
    in_specs = (
        P(("row", "col"), None),
        P(("row", "col")),
        P(("row", "col")),
        P(None, ("row", "col")),
        P("row", "col", None, None, None),
        P("row", "col", None, None),
        P("row", "col", None),
        P("row", "col", None),
        P("row", "col"),
    )
    out_specs = (P(None, ("row", "col")), P(None, ("row", "col")))
    return jax.shard_map(shards, mesh=mesh, in_specs=in_specs, out_specs=out_specs, check_vma=False)
```

```python
import functools

import jax
import jax.numpy as jnp
from jax import lax
from jax.experimental import pallas as pl
from jax.experimental.pallas import tpu as pltpu
from jax.sharding import PartitionSpec as P

D_EMB = 64
BLK = 128
CB = 2
SPAN = CB * BLK
STEPS = 2

STEP_SIZE = 0.0005
REPULSION = 2.0
FORCE_SCALE = 0.015625

RHO, SIGMA, SQUARES, SEEDS = D_EMB, D_EMB + 1, D_EMB + 2, D_EMB + 3
PACK = 72
STACK = 4 * D_EMB
PULL = 2 * D_EMB + 16
UNROLL = 12
F32, BF16, I32 = jnp.float32, jnp.bfloat16, jnp.int32
VMEM_LIMIT = 44 * 2**20


def split(value):
    high = value.astype(BF16)
    return high, (value - high.astype(F32)).astype(BF16)


def nt_dot(left, right):
    return lax.dot_general(left, right, (((1,), (1,)), ((), ())), preferred_element_type=F32)


def nn_dot(left, right):
    return lax.dot_general(left, right, (((1,), (0,)), ((), ())), preferred_element_type=F32)


def hash_bits(salt_value, first, second):
    mixed = first * 1103515245 + salt_value
    mixed = (mixed ^ second * 747796405) * 277803737
    return (mixed >> 17 & 1).astype(F32)


def takes_shift(shift, row, row_count):
    if 2 * shift != row_count:
        return True
    half = row_count // 2
    return jnp.where(row < half, row % 2 == 0, (row - half) % 2 == 1)


def each(count, body):
    if count <= 8:
        for index in range(count):
            body(index)
    else:
        pl.loop(0, count)(body)


def pick_of(sizes, meta, listing, bits, shift):
    row_count, _ = sizes
    place = lax.bitwise_xor(meta[1], bits) * row_count + lax.rem(meta[0] + shift, row_count)
    start_i = pl.multiple_of(listing[2 * place] * BLK, BLK)
    start_j = pl.multiple_of(listing[2 * place + 1] * BLK, BLK)
    return start_i, start_j, place


def gram_of(high_j, low_j, high_i, low_i):
    return nt_dot(high_j, low_i) + nt_dot(low_j, high_i) + nt_dot(high_j, high_i)


def grams_kernel(sizes, counts, meta, listing, *rest):
    shifts_early, rows_early = counts
    row_count, _ = sizes
    columns, rows = rest[:shifts_early], rest[shifts_early : shifts_early + rows_early - 1]
    grams, high_c, low_c, high_last, low_last, high_r, low_r = rest[shifts_early + rows_early - 1 :]
    for shift in range(shifts_early):
        high_c[shift], low_c[shift] = split(columns[shift][:SPAN])
    high_r[0], low_r[0] = high_c[0], low_c[0]
    for line in range(1, rows_early):
        high_r[line], low_r[line] = split(rows[line - 1][...])

    def row_span(line):
        bits = meta[3 + line]
        for shift in range(shifts_early):
            start_i, start_j, _ = pick_of(sizes, meta, listing, bits, shift)
            span_i, span_j = pl.ds(start_i, BLK), pl.ds(start_j, BLK)
            grams[line, shift] = gram_of(
                high_c[shift, span_j, :], low_c[shift, span_j, :], high_r[line, span_i, :], low_r[line, span_i, :]
            )
        start_i, _, _ = pick_of(sizes, meta, listing, bits, shifts_early)
        high_last[line] = high_r[line, pl.ds(start_i, BLK), :]
        low_last[line] = low_r[line, pl.ds(start_i, BLK), :]

    each(rows_early, row_span)


def early_grams(sizes, meta, listing, columns, rows):
    shifts_early, rows_early, depth = len(columns), len(rows) + 1, rows[0].shape[-1]
    smem = pl.BlockSpec(memory_space=pltpu.SMEM)
    vmem = pl.BlockSpec(memory_space=pltpu.VMEM)
    tiles = shifts_early * rows_early
    return pl.pallas_call(
        functools.partial(grams_kernel, sizes, (shifts_early, rows_early)),
        in_specs=[smem] * 2 + [vmem] * (len(columns) + len(rows)),
        out_specs=[vmem] * 5,
        out_shape=[
            jax.ShapeDtypeStruct((rows_early, shifts_early, BLK, BLK), F32),
            jax.ShapeDtypeStruct((shifts_early, SPAN, depth), BF16),
            jax.ShapeDtypeStruct((shifts_early, SPAN, depth), BF16),
            jax.ShapeDtypeStruct((rows_early, BLK, depth), BF16),
            jax.ShapeDtypeStruct((rows_early, BLK, depth), BF16),
        ],
        scratch_shapes=[pltpu.VMEM((rows_early, SPAN, depth), BF16)] * 2,
        compiler_params=pltpu.CompilerParams(vmem_limit_bytes=VMEM_LIMIT),
        cost_estimate=pl.CostEstimate(
            flops=tiles * 6 * BLK * BLK * depth,
            bytes_accessed=(shifts_early + rows_early) * SPAN * depth * 4,
            transcendentals=0,
        ),
        name="grams",
    )(meta, listing, *columns, *rows)


def weights_kernel(sizes, counts, meta, listing, seeds, grams, high_c, low_c, high_last, low_last, *rest):
    row_count, col_count = sizes
    shifts_early, rows_early = counts
    shifts, rows_late = shifts_early + 1, col_count - rows_early
    columns, late, packs = rest[:shifts], rest[shifts : shifts + rows_late], rest[shifts + rows_late :][:3]
    out, high_l, low_l, high_r, low_r, late_grams, col_params, row_params = rest[shifts + rows_late + 3 :]
    own_pack, even_packs, odd_packs = packs
    row, col = meta[0], meta[1]

    high_l[...], low_l[...] = split(columns[shifts_early][:SPAN])
    for shift in range(shifts):
        for block in range(CB):
            lanes = slice(block * BLK, (block + 1) * BLK)
            if shift == 0:
                params = own_pack[RHO : RHO + 8, lanes]
            else:
                params = columns[shift][SPAN + 16 : SPAN + 24, 2 * SPAN :][:, lanes]
            col_params[shift, block] = params.T
    for bits in range(col_count):
        row_params[bits] = (even_packs, odd_packs)[bits % 2][bits // 2, RHO : RHO + 8, :]
    for line in range(rows_late):
        high_r[line], low_r[line] = split(late[line][...])

    def early_last(line):
        _, start_j, _ = pick_of(sizes, meta, listing, meta[3 + line], shifts_early)
        span_j = pl.ds(start_j, BLK)
        late_grams[shifts_early, meta[3 + line]] = gram_of(
            high_l[span_j, :], low_l[span_j, :], high_last[line], low_last[line]
        )

    each(rows_early, early_last)

    def late_row(line):
        bits = meta[3 + rows_early + line]
        for shift in range(shifts):
            start_i, start_j, _ = pick_of(sizes, meta, listing, bits, shift)
            span_i, span_j = pl.ds(start_i, BLK), pl.ds(start_j, BLK)
            if shift == shifts_early:
                high_j, low_j = high_l[span_j, :], low_l[span_j, :]
            else:
                high_j, low_j = high_c[shift, span_j, :], low_c[shift, span_j, :]
            late_grams[shift, bits] = gram_of(high_j, low_j, high_r[line, span_i, :], low_r[line, span_i, :])

    each(rows_late, late_row)

    positions_j = lax.broadcasted_iota(I32, (BLK, BLK), 0)
    positions_i = lax.broadcasted_iota(I32, (BLK, BLK), 1)
    wanted_seed = lax.broadcasted_iota(I32, (1, SPAN), 1) == col * row_count + row

    def finish(bits, shift, gram):
        start_i, start_j, place = pick_of(sizes, meta, listing, bits, shift)
        params_i = row_params[bits, :, pl.ds(start_i, BLK)]
        rho_i, sigma_i, square_i = params_i[0:1], params_i[1:2], params_i[2:3]
        params_j = col_params[shift, lax.div(start_j, BLK)]
        rho_j, sigma_j, square_j = params_j[:, 0:1], params_j[:, 1:2], params_j[:, 2:3]
        distance = jnp.sqrt(jnp.maximum(square_j + square_i - 2.0 * gram, 1.0))
        plane_seeds = row_params[bits, SEEDS - RHO + shift : SEEDS - RHO + shift + 1, :]
        seed_back = jnp.sum(jnp.where(wanted_seed, plane_seeds, 0.0), axis=1, keepdims=True).astype(I32)
        ahead = hash_bits(seeds[place], positions_i, positions_j) * jnp.exp(
            jnp.maximum(distance - rho_i, 0.0) * (-1.0 / sigma_i)
        )
        behind = hash_bits(seed_back, positions_j, positions_i) * jnp.exp(
            jnp.maximum(distance - rho_j, 0.0) * (-1.0 / sigma_j)
        )
        weights = (ahead + behind - ahead * behind).astype(BF16)
        if shift == 0:
            weights = (weights.astype(F32) * jnp.where(bits == 0, 0.5, 1.0)).astype(BF16)
        out[shift * col_count + bits] = weights

    def early_rows(line):
        bits = meta[3 + line]
        for shift in range(shifts):
            finish(bits, shift, grams[line, shift] if shift < shifts_early else late_grams[shift, bits])

    def late_rows(line):
        bits = meta[3 + rows_early + line]
        for shift in range(shifts):
            finish(bits, shift, late_grams[shift, bits])

    each(rows_early, early_rows)
    each(rows_late, late_rows)


def pair_weights(sizes, meta, listing, seeds, early, columns, late, packs):
    _, col_count = sizes
    shifts, depth = len(columns), late[0].shape[-1]
    rows_late = len(late)
    smem = pl.BlockSpec(memory_space=pltpu.SMEM)
    vmem = pl.BlockSpec(memory_space=pltpu.VMEM)
    tiles = shifts * col_count
    return pl.pallas_call(
        functools.partial(weights_kernel, sizes, (shifts - 1, col_count - rows_late)),
        in_specs=[smem] * 3 + [vmem] * (5 + shifts + rows_late + 3),
        out_specs=vmem,
        out_shape=jax.ShapeDtypeStruct((tiles, BLK, BLK), BF16),
        scratch_shapes=[
            pltpu.VMEM((SPAN, depth), BF16),
            pltpu.VMEM((SPAN, depth), BF16),
            pltpu.VMEM((rows_late, SPAN, depth), BF16),
            pltpu.VMEM((rows_late, SPAN, depth), BF16),
            pltpu.VMEM((shifts, col_count, BLK, BLK), F32),
            pltpu.VMEM((shifts, CB, BLK, 8), F32),
            pltpu.VMEM((col_count, 8, SPAN), F32),
        ],
        compiler_params=pltpu.CompilerParams(vmem_limit_bytes=VMEM_LIMIT),
        cost_estimate=pl.CostEstimate(
            flops=tiles * 3 * BLK * BLK * depth,
            bytes_accessed=(shifts + rows_late) * SPAN * depth * 4,
            transcendentals=tiles * 3 * BLK * BLK,
        ),
        name="weights",
    )(meta, listing, seeds, *early, *columns, *late, *packs)


def force_kernel(row_count, col_count, by_bits, meta, listing, neg_rows, neg_cols, weights, *rest):
    shifts = row_count // 2 + 1
    row_arrays, rest = (rest[:2], rest[2:]) if by_bits else (rest[:1], rest[1:])
    col_y = rest[:row_count]
    row_force, col_force = rest[row_count], rest[row_count + 1 : 2 * row_count + 1]
    left_gram, right_gram, left_pull, right_pull, left_acc, right_acc, held_v, held_h = rest[2 * row_count + 1 :]
    row, col, live = meta[0], meta[1], meta[2]
    iota = lax.broadcasted_iota(I32, (D_EMB, BLK), 0)
    ones = jnp.ones((16, BLK), BF16)
    blank = jnp.zeros((D_EMB, BLK), BF16)

    def norm_rows(value, first):
        norm = jnp.sum(value * value, axis=0, keepdims=True)
        high, rest_ = split(norm)
        left_over = norm - high.astype(F32) - rest_.astype(F32)
        high, middle = high.astype(F32), rest_.astype(F32)
        return jnp.where(
            iota == first,
            high,
            jnp.where(iota == first + 1, middle, jnp.where(iota == first + 2, left_over, 0.0)),
        )

    def pulls(high, low):
        top = jnp.concatenate([high, ones, low], axis=0)
        bottom = jnp.concatenate([high, ones, blank], axis=0)
        return jnp.concatenate([top, bottom], axis=1)

    def left_block(index, value):
        high, low = split(value)
        extra = norm_rows(value, 0) + jnp.where((iota >= 3) & (iota < 7), 1.0, 0.0)
        left_gram[index] = jnp.concatenate([high, low, high, extra.astype(BF16)], axis=0)
        left_pull[index] = pulls(high, low)
        left_acc[index] = jnp.zeros((PULL, BLK), F32)

    def right_block(index, value):
        high, low = split(value)
        extra = norm_rows(value, 3) + jnp.where((iota < 3) | (iota == 6), 1.0, 0.0)
        twice_high, twice_low = -2.0 * high.astype(F32), -2.0 * low.astype(F32)
        stack = jnp.concatenate([twice_high, twice_high, twice_low, extra], axis=0)
        right_gram[index] = stack.T.astype(BF16)
        right_pull[index] = pulls(high, low)
        right_acc[index] = jnp.zeros((PULL, BLK), F32)

    def row_y(pair, side, block):
        lanes = slice(block * BLK, (block + 1) * BLK)
        line = pair * 2 + side
        if by_bits:
            return row_arrays[side][pair, :D_EMB, lanes], lax.bitwise_xor(line, col)
        return row_arrays[0][line, :D_EMB, lanes], line

    @pl.loop(0, col_count // 2)
    def _(pair):
        for side in range(2):
            for block in range(CB):
                value, group = row_y(pair, side, block)
                left_block(group * CB + block, value)

    for shift in range(row_count):
        for block in range(CB):
            right_block(shift * CB + block, col_y[shift][:D_EMB, block * BLK : (block + 1) * BLK])

    def kernel_of(left, right):
        return 1.0 / nn_dot(right_gram[right], left_gram[left])

    def apply_all(tiles_):
        for lane, (left, right, coefficient) in enumerate(tiles_):
            high, low = split(coefficient())
            held_v[lane, :BLK], held_v[lane, BLK:] = high, low
            held_h[lane, :, :BLK], held_h[lane, :, BLK:] = high, low
        for lane, (left, right, _) in enumerate(tiles_):
            left_acc[left] += nn_dot(right_pull[right], held_v[lane])
        for lane, (left, right, _) in enumerate(tiles_):
            right_acc[right] += nt_dot(left_pull[left], held_h[lane])

    def near_active(group):
        offset = lax.rem(group - col + col_count, col_count)
        return (2 * offset < col_count) | ((2 * offset == col_count) & (2 * col < col_count))

    near = col_count // 2 + 1
    tiles = near + col_count * (shifts - 1)
    last = jnp.where(takes_shift(shifts - 1, row, row_count), tiles, tiles - col_count)

    @pl.loop(0, lax.div(last + UNROLL - 1, UNROLL))
    def _(step):
        batch = []
        for lane in range(UNROLL):
            index = step * UNROLL + lane
            far = jnp.maximum(index - near, 0)
            shift = jnp.where(index < near, 0, 1 + lax.div(far, col_count))
            group = jnp.where(index < near, lax.rem(col + index, col_count), lax.rem(far, col_count))
            inside = index < last
            shift = jnp.where(inside, shift, 0)
            inside &= (shift > 0) | near_active(group)
            slot = shift * col_count + lax.bitwise_xor(group, col)
            entry = (group * row_count + lax.rem(row + shift, row_count)) * 2
            left = group * CB + listing[entry]
            right = shift * CB + listing[entry + 1]

            def pull(left=left, right=right, slot=slot, inside=inside):
                return weights[slot].astype(F32) * (kernel_of(left, right) * jnp.where(inside, 1.0, 0.0))

            batch.append((left, right, pull))
        apply_all(batch)

    @pl.loop(0, lax.div(live + UNROLL - 1, UNROLL))
    def _(step):
        batch = []
        for lane in range(UNROLL):
            index = step * UNROLL + lane
            strength = jnp.where(index < live, -REPULSION, 0.0)
            place = jnp.minimum(index, live - 1)
            left = neg_rows[place]
            other = neg_cols[place]
            shift = lax.rem(lax.div(other, CB) - row + row_count, row_count)
            right = shift * CB + lax.rem(other, CB)
            def push(left=left, right=right, strength=strength):
                kernel = kernel_of(left, right)
                return strength * kernel * kernel
            batch.append((left, right, push))
        apply_all(batch)

    def force_of(acc, value):
        return acc[:D_EMB] + acc[D_EMB + 16 :] - value * acc[D_EMB : D_EMB + 1]

    @pl.loop(0, col_count // 2)
    def _(pair):
        for side in range(2):
            for block in range(CB):
                value, group = row_y(pair, side, block)
                lanes = slice(block * BLK, (block + 1) * BLK)
                row_force[group, :, lanes] = force_of(left_acc[group * CB + block], value)

    for shift in range(row_count):
        for block in range(CB):
            lanes = slice(block * BLK, (block + 1) * BLK)
            col_force[shift][:, lanes] = force_of(right_acc[shift * CB + block], col_y[shift][:D_EMB, lanes])


def pair_forces(sizes, meta, listing, neg_rows, neg_cols, weights, row_y, col_y):
    row_count, col_count = sizes
    smem = pl.BlockSpec(memory_space=pltpu.SMEM)
    vmem = pl.BlockSpec(memory_space=pltpu.VMEM)
    lefts, rights = col_count * CB, row_count * CB
    tiles = col_count * 2 + 48
    outs = pl.pallas_call(
        functools.partial(force_kernel, row_count, col_count, len(row_y) > 1),
        in_specs=[smem] * 4 + [vmem] * (1 + len(row_y) + row_count),
        out_specs=[vmem] * (1 + row_count),
        out_shape=[jax.ShapeDtypeStruct((col_count, D_EMB, SPAN), F32)]
        + [jax.ShapeDtypeStruct((D_EMB, SPAN), F32)] * row_count,
        scratch_shapes=[
            pltpu.VMEM((lefts, STACK, BLK), BF16),
            pltpu.VMEM((rights, BLK, STACK), BF16),
            pltpu.VMEM((lefts, PULL, 2 * BLK), BF16),
            pltpu.VMEM((rights, PULL, 2 * BLK), BF16),
            pltpu.VMEM((lefts, PULL, BLK), F32),
            pltpu.VMEM((rights, PULL, BLK), F32),
            pltpu.VMEM((UNROLL, 2 * BLK, BLK), BF16),
            pltpu.VMEM((UNROLL, BLK, 2 * BLK), BF16),
        ],
        compiler_params=pltpu.CompilerParams(vmem_limit_bytes=VMEM_LIMIT),
        cost_estimate=pl.CostEstimate(
            flops=tiles * 2 * BLK * BLK * (STACK + 4 * PULL),
            bytes_accessed=4 * D_EMB * SPAN * 2 * (col_count + row_count),
            transcendentals=tiles * BLK * BLK,
        ),
        name="forces",
    )(meta, listing, neg_rows, neg_cols, weights, *row_y, *col_y)
    return outs[0], outs[1:]


def shards(inputs, rho, sigma, embed, knn_blocks, knn_seeds, neg_rows, neg_cols, neg_count):
    row_count = lax.axis_size("row")
    col_count = lax.axis_size("col")
    shifts = row_count // 2 + 1
    row, col = lax.axis_index("row"), lax.axis_index("col")
    listing = knn_blocks.reshape(-1)
    seeds = knn_seeds.reshape(-1)
    row_list, col_list = neg_rows.reshape(-1), neg_cols.reshape(-1)
    meta = jnp.stack([row, col, neg_count[0, 0]]).astype(I32)

    def from_shift(value, shift):
        pairs = [((r + shift) % row_count, r) for r in range(row_count)]
        return lax.ppermute(value, "row", pairs)

    def from_half(value):
        half = row_count // 2
        pairs = [(r + half, r) if r % 2 == 0 else (r, r + half) for r in range(half)]
        return lax.ppermute(value, "row", pairs)

    def to_shift(value, shift):
        pairs = [(r, (r + shift) % row_count) for r in range(row_count)]
        return lax.ppermute(value, "row", pairs)

    def from_bits(value, bits):
        pairs = [(c ^ bits, c) for c in range(col_count)]
        return lax.ppermute(value, "col", pairs)

    sizes = row_count, col_count
    single = [1 << place for place in range(1, (col_count - 1).bit_length())]
    early_bits = [0, 1] + [bits + core for bits in single for core in range(2)]
    late_bits = [bits for bits in range(col_count) if bits not in early_bits]
    meta = jnp.concatenate([meta, jnp.array(early_bits + late_bits, I32)])

    def after(value, *others):
        return lax.optimization_barrier((value, *others))[0]

    row_x = {0: inputs}
    for bits in single:
        row_x[bits] = from_bits(inputs, bits)
    far_seeds = [from_shift(seeds, shift) for shift in range(1, shifts)]

    squares = jnp.sum(inputs * inputs, axis=1)
    params = jnp.stack([rho, sigma, squares])
    pack = jnp.concatenate([embed, params, jnp.zeros((PACK - SEEDS, SPAN), F32)], axis=0)
    third = PACK // 3
    below = jnp.concatenate([pack[:third], pack[third : 2 * third], pack[2 * third :]], axis=1)
    with_pack = jnp.concatenate([inputs, after(below, *far_seeds)], axis=0)
    col_x = [inputs] + [from_shift(with_pack, shift) for shift in range(1, shifts - 1)]
    for bits in late_bits:
        if bits % 2 == 0:
            row_x[bits] = from_bits(after(inputs, with_pack), bits)
    row_x[1] = from_bits(after(inputs, with_pack), 1)
    near = [row_x[bits] for bits in single] + col_x[1:]
    for bits in single:
        row_x[bits + 1] = from_bits(after(row_x[bits], *near), 1)
    col_x.append(from_half(after(with_pack, row_x[1])))

    seed_rows = jnp.pad(
        jnp.stack([seeds, *far_seeds]).astype(F32), ((0, PACK - SEEDS - shifts), (0, SPAN - seeds.shape[0]))
    )
    own_pack = jnp.concatenate([embed, params, seed_rows], axis=0)
    early = early_grams(sizes, meta, listing, col_x[:-1], [row_x[bits] for bits in early_bits[1:]])
    own_pack = after(own_pack, *[row_x[bits + 1] for bits in single])
    even_packs = jnp.stack([own_pack] + [from_bits(own_pack, bits) for bits in range(2, col_count, 2)])
    even_packs = after(even_packs, early[0])
    odd_packs = from_bits(even_packs, 1)
    for bits in late_bits:
        if bits % 2 == 0:
            row_x[bits + 1] = from_bits(after(row_x[bits], even_packs), 1)

    col_y = [embed]
    for shift in range(1, shifts - 1):
        packed = col_x[shift][SPAN:]
        col_y.append(
            jnp.concatenate(
                [packed[:, :SPAN], packed[:, SPAN : 2 * SPAN], packed[: D_EMB - 2 * third, 2 * SPAN :]], axis=0
            )
        )
    held = after(embed, *[row_x[bits] for bits in late_bits if bits % 2 == 0])
    col_y += [from_shift(held, shift) for shift in range(shifts - 1, row_count)]

    weights = pair_weights(
        sizes,
        meta,
        listing,
        seeds,
        early,
        col_x,
        [row_x[bits] for bits in late_bits],
        [own_pack, even_packs, odd_packs],
    )

    row_y = (even_packs, odd_packs)
    for step in range(STEPS):
        if step:
            row_y = (lax.all_gather(embed, "col", axis=0, tiled=False),)
            col_y = [embed] + [from_shift(embed, shift) for shift in range(1, row_count)]
        row_force, col_force = pair_forces(sizes, meta, listing, row_list, col_list, weights, row_y, col_y)
        row_parts = lax.all_to_all(row_force, "col", split_axis=0, concat_axis=0, tiled=True)
        force = jnp.sum(row_parts, axis=0) + col_force[0]
        for shift in range(1, row_count):
            force = force + to_shift(col_force[shift], shift)
        embed = embed + STEP_SIZE * force
    return (embed, force * FORCE_SCALE)


def solution(mesh):
    in_specs = (
        P(("row", "col"), None),
        P(("row", "col")),
        P(("row", "col")),
        P(None, ("row", "col")),
        P("row", "col", None, None, None),
        P("row", "col", None, None),
        P("row", "col", None),
        P("row", "col", None),
        P("row", "col"),
    )
    out_specs = (P(None, ("row", "col")), P(None, ("row", "col")))
    return jax.shard_map(shards, mesh=mesh, in_specs=in_specs, out_specs=out_specs, check_vma=False)
```

```python
import functools

import jax
import jax.numpy as jnp
from jax import lax
from jax.experimental import pallas as pl
from jax.experimental.pallas import tpu as pltpu
from jax.sharding import PartitionSpec as P

D_EMB = 64
BLK = 128
CB = 2
SPAN = CB * BLK
STEPS = 2

STEP_SIZE = 0.0005
REPULSION = 2.0
FORCE_SCALE = 0.015625

RHO, SIGMA, SQUARES, SEEDS = D_EMB, D_EMB + 1, D_EMB + 2, D_EMB + 3
PACK = 72
STACK = 4 * D_EMB
PULL = 2 * D_EMB + 16
UNROLL = 12
F32, BF16, I32 = jnp.float32, jnp.bfloat16, jnp.int32
VMEM_LIMIT = 44 * 2**20


def split(value):
    high = value.astype(BF16)
    return high, (value - high.astype(F32)).astype(BF16)


def nt_dot(left, right):
    return lax.dot_general(left, right, (((1,), (1,)), ((), ())), preferred_element_type=F32)


def nn_dot(left, right):
    return lax.dot_general(left, right, (((1,), (0,)), ((), ())), preferred_element_type=F32)


def hash_bits(salt_value, first, second):
    mixed = first * 1103515245 + salt_value
    mixed = (mixed ^ second * 747796405) * 277803737
    return (mixed >> 17 & 1).astype(F32)


def takes_shift(shift, row, row_count):
    if 2 * shift != row_count:
        return True
    half = row_count // 2
    return jnp.where(row < half, row % 2 == 0, (row - half) % 2 == 1)


def each(count, body):
    if count <= 8:
        for index in range(count):
            body(index)
    else:
        pl.loop(0, count)(body)


def pick_of(sizes, meta, listing, bits, shift):
    row_count, _ = sizes
    place = lax.bitwise_xor(meta[1], bits) * row_count + lax.rem(meta[0] + shift, row_count)
    start_i = pl.multiple_of(listing[2 * place] * BLK, BLK)
    start_j = pl.multiple_of(listing[2 * place + 1] * BLK, BLK)
    return start_i, start_j, place


def gram_of(high_j, low_j, high_i, low_i):
    return nt_dot(high_j, low_i) + nt_dot(low_j, high_i) + nt_dot(high_j, high_i)


def grams_kernel(sizes, counts, meta, listing, *rest):
    shifts_early, rows_early = counts
    row_count, _ = sizes
    columns, rows = rest[:shifts_early], rest[shifts_early : shifts_early + rows_early - 1]
    grams, high_c, low_c, high_last, low_last, high_r, low_r = rest[shifts_early + rows_early - 1 :]
    for shift in range(shifts_early):
        high_c[shift], low_c[shift] = split(columns[shift][...])
    high_r[0], low_r[0] = high_c[0], low_c[0]
    for line in range(1, rows_early):
        high_r[line], low_r[line] = split(rows[line - 1][...])

    def row_span(line):
        bits = meta[3 + line]
        for shift in range(shifts_early):
            start_i, start_j, _ = pick_of(sizes, meta, listing, bits, shift)
            span_i, span_j = pl.ds(start_i, BLK), pl.ds(start_j, BLK)
            grams[line, shift] = gram_of(
                high_c[shift, span_j, :], low_c[shift, span_j, :], high_r[line, span_i, :], low_r[line, span_i, :]
            )
        start_i, _, _ = pick_of(sizes, meta, listing, bits, shifts_early)
        high_last[line] = high_r[line, pl.ds(start_i, BLK), :]
        low_last[line] = low_r[line, pl.ds(start_i, BLK), :]

    each(rows_early, row_span)


def early_grams(sizes, meta, listing, columns, rows):
    shifts_early, rows_early, depth = len(columns), len(rows) + 1, rows[0].shape[-1]
    smem = pl.BlockSpec(memory_space=pltpu.SMEM)
    vmem = pl.BlockSpec(memory_space=pltpu.VMEM)
    tiles = shifts_early * rows_early
    return pl.pallas_call(
        functools.partial(grams_kernel, sizes, (shifts_early, rows_early)),
        in_specs=[smem] * 2 + [vmem] * (len(columns) + len(rows)),
        out_specs=[vmem] * 5,
        out_shape=[
            jax.ShapeDtypeStruct((rows_early, shifts_early, BLK, BLK), F32),
            jax.ShapeDtypeStruct((shifts_early, SPAN, depth), BF16),
            jax.ShapeDtypeStruct((shifts_early, SPAN, depth), BF16),
            jax.ShapeDtypeStruct((rows_early, BLK, depth), BF16),
            jax.ShapeDtypeStruct((rows_early, BLK, depth), BF16),
        ],
        scratch_shapes=[pltpu.VMEM((rows_early, SPAN, depth), BF16)] * 2,
        compiler_params=pltpu.CompilerParams(vmem_limit_bytes=VMEM_LIMIT),
        cost_estimate=pl.CostEstimate(
            flops=tiles * 6 * BLK * BLK * depth,
            bytes_accessed=(shifts_early + rows_early) * SPAN * depth * 4,
            transcendentals=0,
        ),
        name="grams",
    )(meta, listing, *columns, *rows)


def weights_kernel(sizes, counts, meta, listing, seeds, grams, high_c, low_c, high_last, low_last, *rest):
    row_count, col_count = sizes
    shifts_early, rows_early = counts
    shifts, rows_late = shifts_early + 1, col_count - rows_early
    last, late, col_packs = rest[0], rest[1 : 1 + rows_late], rest[1 + rows_late :][:shifts]
    even_packs, odd_packs = rest[1 + rows_late + shifts :][:2]
    out, high_l, low_l, high_r, low_r, late_grams, col_params, row_params = rest[3 + rows_late + shifts :]
    row, col = meta[0], meta[1]

    high_l[...], low_l[...] = split(last[...])
    for shift in range(shifts):
        for block in range(CB):
            lanes = slice(block * BLK, (block + 1) * BLK)
            col_params[shift, block] = col_packs[shift][RHO : RHO + 8, lanes].T
    for bits in range(col_count):
        row_params[bits] = (even_packs, odd_packs)[bits % 2][bits // 2, RHO : RHO + 8, :]
    for line in range(rows_late):
        high_r[line], low_r[line] = split(late[line][...])

    def early_last(line):
        _, start_j, _ = pick_of(sizes, meta, listing, meta[3 + line], shifts_early)
        span_j = pl.ds(start_j, BLK)
        late_grams[shifts_early, meta[3 + line]] = gram_of(
            high_l[span_j, :], low_l[span_j, :], high_last[line], low_last[line]
        )

    each(rows_early, early_last)

    def late_row(line):
        bits = meta[3 + rows_early + line]
        for shift in range(shifts):
            start_i, start_j, _ = pick_of(sizes, meta, listing, bits, shift)
            span_i, span_j = pl.ds(start_i, BLK), pl.ds(start_j, BLK)
            if shift == shifts_early:
                high_j, low_j = high_l[span_j, :], low_l[span_j, :]
            else:
                high_j, low_j = high_c[shift, span_j, :], low_c[shift, span_j, :]
            late_grams[shift, bits] = gram_of(high_j, low_j, high_r[line, span_i, :], low_r[line, span_i, :])

    each(rows_late, late_row)

    positions_j = lax.broadcasted_iota(I32, (BLK, BLK), 0)
    positions_i = lax.broadcasted_iota(I32, (BLK, BLK), 1)
    wanted_seed = lax.broadcasted_iota(I32, (1, SPAN), 1) == col * row_count + row

    def finish(bits, shift, gram):
        start_i, start_j, place = pick_of(sizes, meta, listing, bits, shift)
        params_i = row_params[bits, :, pl.ds(start_i, BLK)]
        rho_i, sigma_i, square_i = params_i[0:1], params_i[1:2], params_i[2:3]
        params_j = col_params[shift, lax.div(start_j, BLK)]
        rho_j, sigma_j, square_j = params_j[:, 0:1], params_j[:, 1:2], params_j[:, 2:3]
        distance = jnp.sqrt(jnp.maximum(square_j + square_i - 2.0 * gram, 1.0))
        plane_seeds = row_params[bits, SEEDS - RHO + shift : SEEDS - RHO + shift + 1, :]
        seed_back = jnp.sum(jnp.where(wanted_seed, plane_seeds, 0.0), axis=1, keepdims=True).astype(I32)
        ahead = hash_bits(seeds[place], positions_i, positions_j) * jnp.exp(
            jnp.maximum(distance - rho_i, 0.0) * (-1.0 / sigma_i)
        )
        behind = hash_bits(seed_back, positions_j, positions_i) * jnp.exp(
            jnp.maximum(distance - rho_j, 0.0) * (-1.0 / sigma_j)
        )
        weights = (ahead + behind - ahead * behind).astype(BF16)
        if shift == 0:
            weights = (weights.astype(F32) * jnp.where(bits == 0, 0.5, 1.0)).astype(BF16)
        out[shift * col_count + bits] = weights

    def early_rows(line):
        bits = meta[3 + line]
        for shift in range(shifts):
            finish(bits, shift, grams[line, shift] if shift < shifts_early else late_grams[shift, bits])

    def late_rows(line):
        bits = meta[3 + rows_early + line]
        for shift in range(shifts):
            finish(bits, shift, late_grams[shift, bits])

    each(rows_early, early_rows)
    each(rows_late, late_rows)


def pair_weights(sizes, meta, listing, seeds, early, last, late, packs):
    _, col_count = sizes
    shifts, depth = len(packs) - 2, late[0].shape[-1]
    rows_late = len(late)
    smem = pl.BlockSpec(memory_space=pltpu.SMEM)
    vmem = pl.BlockSpec(memory_space=pltpu.VMEM)
    tiles = shifts * col_count
    return pl.pallas_call(
        functools.partial(weights_kernel, sizes, (shifts - 1, col_count - rows_late)),
        in_specs=[smem] * 3 + [vmem] * (5 + 1 + rows_late + len(packs)),
        out_specs=vmem,
        out_shape=jax.ShapeDtypeStruct((tiles, BLK, BLK), BF16),
        scratch_shapes=[
            pltpu.VMEM((SPAN, depth), BF16),
            pltpu.VMEM((SPAN, depth), BF16),
            pltpu.VMEM((rows_late, SPAN, depth), BF16),
            pltpu.VMEM((rows_late, SPAN, depth), BF16),
            pltpu.VMEM((shifts, col_count, BLK, BLK), F32),
            pltpu.VMEM((shifts, CB, BLK, 8), F32),
            pltpu.VMEM((col_count, 8, SPAN), F32),
        ],
        compiler_params=pltpu.CompilerParams(vmem_limit_bytes=VMEM_LIMIT),
        cost_estimate=pl.CostEstimate(
            flops=tiles * 3 * BLK * BLK * depth,
            bytes_accessed=(1 + rows_late) * SPAN * depth * 4,
            transcendentals=tiles * 3 * BLK * BLK,
        ),
        name="weights",
    )(meta, listing, seeds, *early, last, *late, *packs)


def force_kernel(row_count, col_count, by_bits, meta, listing, neg_rows, neg_cols, weights, *rest):
    shifts = row_count // 2 + 1
    row_arrays, rest = (rest[:2], rest[2:]) if by_bits else (rest[:1], rest[1:])
    col_y = rest[:row_count]
    row_force, col_force = rest[row_count], rest[row_count + 1 : 2 * row_count + 1]
    left_gram, right_gram, left_pull, right_pull, left_acc, right_acc, held_v, held_h = rest[2 * row_count + 1 :]
    row, col, live = meta[0], meta[1], meta[2]
    iota = lax.broadcasted_iota(I32, (D_EMB, BLK), 0)
    ones = jnp.ones((16, BLK), BF16)
    blank = jnp.zeros((D_EMB, BLK), BF16)

    def norm_rows(value, first):
        norm = jnp.sum(value * value, axis=0, keepdims=True)
        high, rest_ = split(norm)
        left_over = norm - high.astype(F32) - rest_.astype(F32)
        high, middle = high.astype(F32), rest_.astype(F32)
        return jnp.where(
            iota == first,
            high,
            jnp.where(iota == first + 1, middle, jnp.where(iota == first + 2, left_over, 0.0)),
        )

    def pulls(high, low):
        top = jnp.concatenate([high, ones, low], axis=0)
        bottom = jnp.concatenate([high, ones, blank], axis=0)
        return jnp.concatenate([top, bottom], axis=1)

    def left_block(index, value):
        high, low = split(value)
        extra = norm_rows(value, 0) + jnp.where((iota >= 3) & (iota < 7), 1.0, 0.0)
        left_gram[index] = jnp.concatenate([high, low, high, extra.astype(BF16)], axis=0)
        left_pull[index] = pulls(high, low)
        left_acc[index] = jnp.zeros((PULL, BLK), F32)

    def right_block(index, value):
        high, low = split(value)
        extra = norm_rows(value, 3) + jnp.where((iota < 3) | (iota == 6), 1.0, 0.0)
        twice_high, twice_low = -2.0 * high.astype(F32), -2.0 * low.astype(F32)
        stack = jnp.concatenate([twice_high, twice_high, twice_low, extra], axis=0)
        right_gram[index] = stack.T.astype(BF16)
        right_pull[index] = pulls(high, low)
        right_acc[index] = jnp.zeros((PULL, BLK), F32)

    def row_y(pair, side, block):
        lanes = slice(block * BLK, (block + 1) * BLK)
        line = pair * 2 + side
        if by_bits:
            return row_arrays[side][pair, :D_EMB, lanes], lax.bitwise_xor(line, col)
        return row_arrays[0][line, :D_EMB, lanes], line

    @pl.loop(0, col_count // 2)
    def _(pair):
        for side in range(2):
            for block in range(CB):
                value, group = row_y(pair, side, block)
                left_block(group * CB + block, value)

    for shift in range(row_count):
        for block in range(CB):
            right_block(shift * CB + block, col_y[shift][:D_EMB, block * BLK : (block + 1) * BLK])

    def kernel_of(left, right):
        return 1.0 / nn_dot(right_gram[right], left_gram[left])

    def apply_all(tiles_):
        for lane, (left, right, coefficient) in enumerate(tiles_):
            high, low = split(coefficient())
            held_v[lane, :BLK], held_v[lane, BLK:] = high, low
            held_h[lane, :, :BLK], held_h[lane, :, BLK:] = high, low
        for lane, (left, right, _) in enumerate(tiles_):
            left_acc[left] += nn_dot(right_pull[right], held_v[lane])
        for lane, (left, right, _) in enumerate(tiles_):
            right_acc[right] += nt_dot(left_pull[left], held_h[lane])

    def near_active(group):
        offset = lax.rem(group - col + col_count, col_count)
        return (2 * offset < col_count) | ((2 * offset == col_count) & (2 * col < col_count))

    near = col_count // 2 + 1
    tiles = near + col_count * (shifts - 1)
    last = jnp.where(takes_shift(shifts - 1, row, row_count), tiles, tiles - col_count)

    @pl.loop(0, lax.div(last + UNROLL - 1, UNROLL))
    def _(step):
        batch = []
        for lane in range(UNROLL):
            index = step * UNROLL + lane
            far = jnp.maximum(index - near, 0)
            shift = jnp.where(index < near, 0, 1 + lax.div(far, col_count))
            group = jnp.where(index < near, lax.rem(col + index, col_count), lax.rem(far, col_count))
            inside = index < last
            shift = jnp.where(inside, shift, 0)
            inside &= (shift > 0) | near_active(group)
            slot = shift * col_count + lax.bitwise_xor(group, col)
            entry = (group * row_count + lax.rem(row + shift, row_count)) * 2
            left = group * CB + listing[entry]
            right = shift * CB + listing[entry + 1]

            def pull(left=left, right=right, slot=slot, inside=inside):
                return weights[slot].astype(F32) * (kernel_of(left, right) * jnp.where(inside, 1.0, 0.0))

            batch.append((left, right, pull))
        apply_all(batch)

    @pl.loop(0, lax.div(live + UNROLL - 1, UNROLL))
    def _(step):
        batch = []
        for lane in range(UNROLL):
            index = step * UNROLL + lane
            strength = jnp.where(index < live, -REPULSION, 0.0)
            place = jnp.minimum(index, live - 1)
            left = neg_rows[place]
            other = neg_cols[place]
            shift = lax.rem(lax.div(other, CB) - row + row_count, row_count)
            right = shift * CB + lax.rem(other, CB)
            def push(left=left, right=right, strength=strength):
                kernel = kernel_of(left, right)
                return strength * kernel * kernel
            batch.append((left, right, push))
        apply_all(batch)

    def force_of(acc, value):
        return acc[:D_EMB] + acc[D_EMB + 16 :] - value * acc[D_EMB : D_EMB + 1]

    @pl.loop(0, col_count // 2)
    def _(pair):
        for side in range(2):
            for block in range(CB):
                value, group = row_y(pair, side, block)
                lanes = slice(block * BLK, (block + 1) * BLK)
                row_force[group, :, lanes] = force_of(left_acc[group * CB + block], value)

    for shift in range(row_count):
        for block in range(CB):
            lanes = slice(block * BLK, (block + 1) * BLK)
            col_force[shift][:, lanes] = force_of(right_acc[shift * CB + block], col_y[shift][:D_EMB, lanes])


def pair_forces(sizes, meta, listing, neg_rows, neg_cols, weights, row_y, col_y):
    row_count, col_count = sizes
    smem = pl.BlockSpec(memory_space=pltpu.SMEM)
    vmem = pl.BlockSpec(memory_space=pltpu.VMEM)
    lefts, rights = col_count * CB, row_count * CB
    tiles = col_count * 2 + 48
    outs = pl.pallas_call(
        functools.partial(force_kernel, row_count, col_count, len(row_y) > 1),
        in_specs=[smem] * 4 + [vmem] * (1 + len(row_y) + row_count),
        out_specs=[vmem] * (1 + row_count),
        out_shape=[jax.ShapeDtypeStruct((col_count, D_EMB, SPAN), F32)]
        + [jax.ShapeDtypeStruct((D_EMB, SPAN), F32)] * row_count,
        scratch_shapes=[
            pltpu.VMEM((lefts, STACK, BLK), BF16),
            pltpu.VMEM((rights, BLK, STACK), BF16),
            pltpu.VMEM((lefts, PULL, 2 * BLK), BF16),
            pltpu.VMEM((rights, PULL, 2 * BLK), BF16),
            pltpu.VMEM((lefts, PULL, BLK), F32),
            pltpu.VMEM((rights, PULL, BLK), F32),
            pltpu.VMEM((UNROLL, 2 * BLK, BLK), BF16),
            pltpu.VMEM((UNROLL, BLK, 2 * BLK), BF16),
        ],
        compiler_params=pltpu.CompilerParams(vmem_limit_bytes=VMEM_LIMIT),
        cost_estimate=pl.CostEstimate(
            flops=tiles * 2 * BLK * BLK * (STACK + 4 * PULL),
            bytes_accessed=4 * D_EMB * SPAN * 2 * (col_count + row_count),
            transcendentals=tiles * BLK * BLK,
        ),
        name="forces",
    )(meta, listing, neg_rows, neg_cols, weights, *row_y, *col_y)
    return outs[0], outs[1:]


def shards(inputs, rho, sigma, embed, knn_blocks, knn_seeds, neg_rows, neg_cols, neg_count):
    row_count = lax.axis_size("row")
    col_count = lax.axis_size("col")
    shifts = row_count // 2 + 1
    row, col = lax.axis_index("row"), lax.axis_index("col")
    listing = knn_blocks.reshape(-1)
    seeds = knn_seeds.reshape(-1)
    row_list, col_list = neg_rows.reshape(-1), neg_cols.reshape(-1)
    meta = jnp.stack([row, col, neg_count[0, 0]]).astype(I32)

    def from_shift(value, shift):
        pairs = [((r + shift) % row_count, r) for r in range(row_count)]
        return lax.ppermute(value, "row", pairs)

    def from_half(value):
        half = row_count // 2
        pairs = [(r + half, r) if r % 2 == 0 else (r, r + half) for r in range(half)]
        return lax.ppermute(value, "row", pairs)

    def to_shift(value, shift):
        pairs = [(r, (r + shift) % row_count) for r in range(row_count)]
        return lax.ppermute(value, "row", pairs)

    def from_bits(value, bits):
        pairs = [(c ^ bits, c) for c in range(col_count)]
        return lax.ppermute(value, "col", pairs)

    sizes = row_count, col_count
    single = [1 << place for place in range(1, (col_count - 1).bit_length())]
    early_bits = [0, 1] + [bits + core for bits in single for core in range(2)]
    late_bits = [bits for bits in range(col_count) if bits not in early_bits]
    meta = jnp.concatenate([meta, jnp.array(early_bits + late_bits, I32)])

    def after(value, *others):
        return lax.optimization_barrier((value, *others))[0]

    row_x = {0: inputs}
    for bits in single:
        row_x[bits] = from_bits(inputs, bits)
    col_x = [inputs] + [from_shift(inputs, shift) for shift in range(1, shifts - 1)]
    near = [row_x[bits] for bits in single] + col_x[1:]
    for bits in late_bits:
        if bits % 2 == 0:
            row_x[bits] = from_bits(inputs, bits)
    far_seeds = [from_shift(seeds, shift) for shift in range(1, shifts)]
    row_x[1] = from_bits(after(inputs, *far_seeds), 1)
    for bits in single:
        row_x[bits + 1] = from_bits(after(row_x[bits], *near), 1)
    col_x.append(from_half(after(inputs, row_x[1])))

    squares = jnp.sum(inputs * inputs, axis=1)
    seed_rows = jnp.pad(
        jnp.stack([seeds, *far_seeds]).astype(F32), ((0, PACK - SEEDS - shifts), (0, SPAN - seeds.shape[0]))
    )
    own_pack = jnp.concatenate([embed, jnp.stack([rho, sigma, squares]), seed_rows], axis=0)
    own_pack = after(own_pack, *[row_x[bits + 1] for bits in single])
    early = early_grams(sizes, meta, listing, col_x[:-1], [row_x[bits] for bits in early_bits[1:]])
    even_packs = jnp.stack([own_pack] + [from_bits(own_pack, bits) for bits in range(2, col_count, 2)])
    even_packs = after(even_packs, early[0])
    odd_packs = from_bits(even_packs, 1)
    for bits in late_bits:
        if bits % 2 == 0:
            row_x[bits + 1] = from_bits(after(row_x[bits], even_packs), 1)
    held = after(own_pack, *[row_x[bits] for bits in late_bits if bits % 2 == 0])
    col_packs = [own_pack] + [from_shift(held, shift) for shift in range(1, row_count)]
    col_y = col_packs

    weights = pair_weights(
        sizes,
        meta,
        listing,
        seeds,
        early,
        col_x[-1],
        [row_x[bits] for bits in late_bits],
        col_packs[:shifts] + [even_packs, odd_packs],
    )

    row_y = (even_packs, odd_packs)
    for step in range(STEPS):
        if step:
            row_y = (lax.all_gather(embed, "col", axis=0, tiled=False),)
            col_y = [embed] + [from_shift(embed, shift) for shift in range(1, row_count)]
        row_force, col_force = pair_forces(sizes, meta, listing, row_list, col_list, weights, row_y, col_y)
        row_parts = lax.all_to_all(row_force, "col", split_axis=0, concat_axis=0, tiled=True)
        force = jnp.sum(row_parts, axis=0) + col_force[0]
        for shift in range(1, row_count):
            force = force + to_shift(col_force[shift], shift)
        embed = embed + STEP_SIZE * force
    return (embed, force * FORCE_SCALE)


def solution(mesh):
    in_specs = (
        P(("row", "col"), None),
        P(("row", "col")),
        P(("row", "col")),
        P(None, ("row", "col")),
        P("row", "col", None, None, None),
        P("row", "col", None, None),
        P("row", "col", None),
        P("row", "col", None),
        P("row", "col"),
    )
    out_specs = (P(None, ("row", "col")), P(None, ("row", "col")))
    return jax.shard_map(shards, mesh=mesh, in_specs=in_specs, out_specs=out_specs, check_vma=False)
```

```python
import functools

import jax
import jax.numpy as jnp
from jax import lax
from jax.experimental import pallas as pl
from jax.experimental.pallas import tpu as pltpu
from jax.sharding import PartitionSpec as P

D_EMB = 64
BLK = 128
CB = 2
SPAN = CB * BLK
STEPS = 2

STEP_SIZE = 0.0005
REPULSION = 2.0
FORCE_SCALE = 0.015625

RHO, SIGMA, SQUARES, SEEDS = D_EMB, D_EMB + 1, D_EMB + 2, D_EMB + 3
PACK = 72
STACK = 4 * D_EMB
PULL = 2 * D_EMB + 16
UNROLL = 12
F32, BF16, I32 = jnp.float32, jnp.bfloat16, jnp.int32
VMEM_LIMIT = 44 * 2**20


def split(value):
    high = value.astype(BF16)
    return high, (value - high.astype(F32)).astype(BF16)


def nt_dot(left, right):
    return lax.dot_general(left, right, (((1,), (1,)), ((), ())), preferred_element_type=F32)


def nn_dot(left, right):
    return lax.dot_general(left, right, (((1,), (0,)), ((), ())), preferred_element_type=F32)


def hash_bits(salt_value, first, second):
    mixed = first * 1103515245 + salt_value
    mixed = (mixed ^ second * 747796405) * 277803737
    return (mixed >> 17 & 1).astype(F32)


def takes_shift(shift, row, row_count):
    if 2 * shift != row_count:
        return True
    half = row_count // 2
    return jnp.where(row < half, row % 2 == 0, (row - half) % 2 == 1)


def each(count, body):
    if count <= 8:
        for index in range(count):
            body(index)
    else:
        pl.loop(0, count)(body)


def pick_of(sizes, meta, listing, bits, shift):
    row_count, _ = sizes
    place = lax.bitwise_xor(meta[1], bits) * row_count + lax.rem(meta[0] + shift, row_count)
    start_i = pl.multiple_of(listing[2 * place] * BLK, BLK)
    start_j = pl.multiple_of(listing[2 * place + 1] * BLK, BLK)
    return start_i, start_j, place


def gram_of(high_j, low_j, high_i, low_i):
    return nt_dot(high_j, low_i) + nt_dot(low_j, high_i) + nt_dot(high_j, high_i)


def grams_kernel(sizes, counts, meta, listing, *rest):
    shifts_early, rows_early = counts
    row_count, _ = sizes
    columns, rows = rest[:shifts_early], rest[shifts_early : shifts_early + rows_early - 1]
    grams, high_c, low_c, high_last, low_last, squares, high_r, low_r = rest[shifts_early + rows_early - 1 :]
    for shift in range(shifts_early):
        value = columns[shift][...]
        high_c[shift], low_c[shift] = split(value)
        squares[shift] = jnp.sum(value * value, axis=1, keepdims=True)
    high_r[0], low_r[0] = high_c[0], low_c[0]
    for line in range(1, rows_early):
        high_r[line], low_r[line] = split(rows[line - 1][...])

    def row_span(line):
        bits = meta[3 + line]
        for shift in range(shifts_early):
            start_i, start_j, _ = pick_of(sizes, meta, listing, bits, shift)
            span_i, span_j = pl.ds(start_i, BLK), pl.ds(start_j, BLK)
            grams[line, shift] = gram_of(
                high_c[shift, span_j, :], low_c[shift, span_j, :], high_r[line, span_i, :], low_r[line, span_i, :]
            )
        start_i, _, _ = pick_of(sizes, meta, listing, bits, shifts_early)
        high_last[line] = high_r[line, pl.ds(start_i, BLK), :]
        low_last[line] = low_r[line, pl.ds(start_i, BLK), :]

    each(rows_early, row_span)


def early_grams(sizes, meta, listing, columns, rows):
    shifts_early, rows_early, depth = len(columns), len(rows) + 1, rows[0].shape[-1]
    smem = pl.BlockSpec(memory_space=pltpu.SMEM)
    vmem = pl.BlockSpec(memory_space=pltpu.VMEM)
    tiles = shifts_early * rows_early
    return pl.pallas_call(
        functools.partial(grams_kernel, sizes, (shifts_early, rows_early)),
        in_specs=[smem] * 2 + [vmem] * (len(columns) + len(rows)),
        out_specs=[vmem] * 6,
        out_shape=[
            jax.ShapeDtypeStruct((rows_early, shifts_early, BLK, BLK), F32),
            jax.ShapeDtypeStruct((shifts_early, SPAN, depth), BF16),
            jax.ShapeDtypeStruct((shifts_early, SPAN, depth), BF16),
            jax.ShapeDtypeStruct((rows_early, BLK, depth), BF16),
            jax.ShapeDtypeStruct((rows_early, BLK, depth), BF16),
            jax.ShapeDtypeStruct((shifts_early, SPAN, 1), F32),
        ],
        scratch_shapes=[pltpu.VMEM((rows_early, SPAN, depth), BF16)] * 2,
        compiler_params=pltpu.CompilerParams(vmem_limit_bytes=VMEM_LIMIT),
        cost_estimate=pl.CostEstimate(
            flops=tiles * 6 * BLK * BLK * depth,
            bytes_accessed=(shifts_early + rows_early) * SPAN * depth * 4,
            transcendentals=0,
        ),
        name="grams",
    )(meta, listing, *columns, *rows)


def weights_kernel(sizes, counts, meta, listing, seeds, grams, high_c, low_c, high_last, low_last, squares, *rest):
    row_count, col_count = sizes
    shifts_early, rows_early = counts
    shifts, rows_late = shifts_early + 1, col_count - rows_early
    last, late, col_packs = rest[0], rest[1 : 1 + rows_late], rest[1 + rows_late :][:shifts]
    even_packs, odd_packs = rest[1 + rows_late + shifts :][:2]
    out, high_l, low_l, high_r, low_r, late_grams, col_params, row_params, last_squares = rest[3 + rows_late + shifts :]
    row, col = meta[0], meta[1]

    high_l[...], low_l[...] = split(last[...])
    last_squares[...] = jnp.sum(last[...] * last[...], axis=1, keepdims=True)
    for shift in range(shifts):
        for block in range(CB):
            lanes = slice(block * BLK, (block + 1) * BLK)
            col_params[shift, block] = col_packs[shift][RHO : RHO + 8, lanes].T
    for bits in range(col_count):
        row_params[bits] = (even_packs, odd_packs)[bits % 2][bits // 2, RHO : RHO + 8, :]
    for line in range(rows_late):
        high_r[line], low_r[line] = split(late[line][...])

    def early_last(line):
        _, start_j, _ = pick_of(sizes, meta, listing, meta[3 + line], shifts_early)
        span_j = pl.ds(start_j, BLK)
        late_grams[shifts_early, meta[3 + line]] = gram_of(
            high_l[span_j, :], low_l[span_j, :], high_last[line], low_last[line]
        )

    each(rows_early, early_last)

    def late_row(line):
        bits = meta[3 + rows_early + line]
        for shift in range(shifts):
            start_i, start_j, _ = pick_of(sizes, meta, listing, bits, shift)
            span_i, span_j = pl.ds(start_i, BLK), pl.ds(start_j, BLK)
            if shift == shifts_early:
                high_j, low_j = high_l[span_j, :], low_l[span_j, :]
            else:
                high_j, low_j = high_c[shift, span_j, :], low_c[shift, span_j, :]
            late_grams[shift, bits] = gram_of(high_j, low_j, high_r[line, span_i, :], low_r[line, span_i, :])

    each(rows_late, late_row)

    positions_j = lax.broadcasted_iota(I32, (BLK, BLK), 0)
    positions_i = lax.broadcasted_iota(I32, (BLK, BLK), 1)
    wanted_seed = lax.broadcasted_iota(I32, (1, SPAN), 1) == col * row_count + row

    def finish(bits, shift, gram):
        start_i, start_j, place = pick_of(sizes, meta, listing, bits, shift)
        params_i = row_params[bits, :, pl.ds(start_i, BLK)]
        rho_i, sigma_i, square_i = params_i[0:1], params_i[1:2], params_i[2:3]
        params_j = col_params[shift, lax.div(start_j, BLK)]
        rho_j, sigma_j = params_j[:, 0:1], params_j[:, 1:2]
        span_j = pl.ds(start_j, BLK)
        square_j = squares[shift, span_j, :] if shift < shifts_early else last_squares[span_j, :]
        distance = jnp.sqrt(jnp.maximum(square_j + square_i - 2.0 * gram, 1.0))
        plane_seeds = row_params[bits, SEEDS - RHO + shift : SEEDS - RHO + shift + 1, :]
        seed_back = jnp.sum(jnp.where(wanted_seed, plane_seeds, 0.0), axis=1, keepdims=True).astype(I32)
        ahead = hash_bits(seeds[place], positions_i, positions_j) * jnp.exp(
            jnp.maximum(distance - rho_i, 0.0) * (-1.0 / sigma_i)
        )
        behind = hash_bits(seed_back, positions_j, positions_i) * jnp.exp(
            jnp.maximum(distance - rho_j, 0.0) * (-1.0 / sigma_j)
        )
        weights = (ahead + behind - ahead * behind).astype(BF16)
        if shift == 0:
            weights = (weights.astype(F32) * jnp.where(bits == 0, 0.5, 1.0)).astype(BF16)
        out[shift * col_count + bits] = weights

    def early_rows(line):
        bits = meta[3 + line]
        for shift in range(shifts):
            finish(bits, shift, grams[line, shift] if shift < shifts_early else late_grams[shift, bits])

    def late_rows(line):
        bits = meta[3 + rows_early + line]
        for shift in range(shifts):
            finish(bits, shift, late_grams[shift, bits])

    each(rows_early, early_rows)
    each(rows_late, late_rows)


def pair_weights(sizes, meta, listing, seeds, early, last, late, packs):
    _, col_count = sizes
    shifts, depth = len(packs) - 2, late[0].shape[-1]
    rows_late = len(late)
    smem = pl.BlockSpec(memory_space=pltpu.SMEM)
    vmem = pl.BlockSpec(memory_space=pltpu.VMEM)
    tiles = shifts * col_count
    return pl.pallas_call(
        functools.partial(weights_kernel, sizes, (shifts - 1, col_count - rows_late)),
        in_specs=[smem] * 3 + [vmem] * (6 + 1 + rows_late + len(packs)),
        out_specs=vmem,
        out_shape=jax.ShapeDtypeStruct((tiles, BLK, BLK), BF16),
        scratch_shapes=[
            pltpu.VMEM((SPAN, depth), BF16),
            pltpu.VMEM((SPAN, depth), BF16),
            pltpu.VMEM((rows_late, SPAN, depth), BF16),
            pltpu.VMEM((rows_late, SPAN, depth), BF16),
            pltpu.VMEM((shifts, col_count, BLK, BLK), F32),
            pltpu.VMEM((shifts, CB, BLK, 8), F32),
            pltpu.VMEM((col_count, 8, SPAN), F32),
            pltpu.VMEM((SPAN, 1), F32),
        ],
        compiler_params=pltpu.CompilerParams(vmem_limit_bytes=VMEM_LIMIT),
        cost_estimate=pl.CostEstimate(
            flops=tiles * 3 * BLK * BLK * depth,
            bytes_accessed=(1 + rows_late) * SPAN * depth * 4,
            transcendentals=tiles * 3 * BLK * BLK,
        ),
        name="weights",
    )(meta, listing, seeds, *early, last, *late, *packs)


def force_kernel(row_count, col_count, by_bits, meta, listing, neg_rows, neg_cols, weights, *rest):
    shifts = row_count // 2 + 1
    row_arrays, rest = (rest[:2], rest[2:]) if by_bits else (rest[:1], rest[1:])
    col_y = rest[:row_count]
    row_force, col_force = rest[row_count], rest[row_count + 1 : 2 * row_count + 1]
    left_gram, right_gram, left_pull, right_pull, left_acc, right_acc, held_v, held_h = rest[2 * row_count + 1 :]
    row, col, live = meta[0], meta[1], meta[2]
    iota = lax.broadcasted_iota(I32, (D_EMB, BLK), 0)
    ones = jnp.ones((16, BLK), BF16)
    blank = jnp.zeros((D_EMB, BLK), BF16)

    def norm_rows(value, first):
        norm = jnp.sum(value * value, axis=0, keepdims=True)
        high, rest_ = split(norm)
        left_over = norm - high.astype(F32) - rest_.astype(F32)
        high, middle = high.astype(F32), rest_.astype(F32)
        return jnp.where(
            iota == first,
            high,
            jnp.where(iota == first + 1, middle, jnp.where(iota == first + 2, left_over, 0.0)),
        )

    def pulls(high, low):
        top = jnp.concatenate([high, ones, low], axis=0)
        bottom = jnp.concatenate([high, ones, blank], axis=0)
        return jnp.concatenate([top, bottom], axis=1)

    def left_block(index, value):
        high, low = split(value)
        extra = norm_rows(value, 0) + jnp.where((iota >= 3) & (iota < 7), 1.0, 0.0)
        left_gram[index] = jnp.concatenate([high, low, high, extra.astype(BF16)], axis=0)
        left_pull[index] = pulls(high, low)
        left_acc[index] = jnp.zeros((PULL, BLK), F32)

    def right_block(index, value):
        high, low = split(value)
        extra = norm_rows(value, 3) + jnp.where((iota < 3) | (iota == 6), 1.0, 0.0)
        twice_high, twice_low = -2.0 * high.astype(F32), -2.0 * low.astype(F32)
        stack = jnp.concatenate([twice_high, twice_high, twice_low, extra], axis=0)
        right_gram[index] = stack.T.astype(BF16)
        right_pull[index] = pulls(high, low)
        right_acc[index] = jnp.zeros((PULL, BLK), F32)

    def row_y(pair, side, block):
        lanes = slice(block * BLK, (block + 1) * BLK)
        line = pair * 2 + side
        if by_bits:
            return row_arrays[side][pair, :D_EMB, lanes], lax.bitwise_xor(line, col)
        return row_arrays[0][line, :D_EMB, lanes], line

    @pl.loop(0, col_count // 2)
    def _(pair):
        for side in range(2):
            for block in range(CB):
                value, group = row_y(pair, side, block)
                left_block(group * CB + block, value)

    for shift in range(row_count):
        for block in range(CB):
            right_block(shift * CB + block, col_y[shift][:D_EMB, block * BLK : (block + 1) * BLK])

    def kernel_of(left, right):
        return 1.0 / nn_dot(right_gram[right], left_gram[left])

    def apply_all(tiles_):
        for lane, (left, right, coefficient) in enumerate(tiles_):
            high, low = split(coefficient())
            held_v[lane, :BLK], held_v[lane, BLK:] = high, low
            held_h[lane, :, :BLK], held_h[lane, :, BLK:] = high, low
        for lane, (left, right, _) in enumerate(tiles_):
            left_acc[left] += nn_dot(right_pull[right], held_v[lane])
        for lane, (left, right, _) in enumerate(tiles_):
            right_acc[right] += nt_dot(left_pull[left], held_h[lane])

    def near_active(group):
        offset = lax.rem(group - col + col_count, col_count)
        return (2 * offset < col_count) | ((2 * offset == col_count) & (2 * col < col_count))

    near = col_count // 2 + 1
    tiles = near + col_count * (shifts - 1)
    last = jnp.where(takes_shift(shifts - 1, row, row_count), tiles, tiles - col_count)

    @pl.loop(0, lax.div(last + UNROLL - 1, UNROLL))
    def _(step):
        batch = []
        for lane in range(UNROLL):
            index = step * UNROLL + lane
            far = jnp.maximum(index - near, 0)
            shift = jnp.where(index < near, 0, 1 + lax.div(far, col_count))
            group = jnp.where(index < near, lax.rem(col + index, col_count), lax.rem(far, col_count))
            inside = index < last
            shift = jnp.where(inside, shift, 0)
            inside &= (shift > 0) | near_active(group)
            slot = shift * col_count + lax.bitwise_xor(group, col)
            entry = (group * row_count + lax.rem(row + shift, row_count)) * 2
            left = group * CB + listing[entry]
            right = shift * CB + listing[entry + 1]

            def pull(left=left, right=right, slot=slot, inside=inside):
                return weights[slot].astype(F32) * (kernel_of(left, right) * jnp.where(inside, 1.0, 0.0))

            batch.append((left, right, pull))
        apply_all(batch)

    @pl.loop(0, lax.div(live + UNROLL - 1, UNROLL))
    def _(step):
        batch = []
        for lane in range(UNROLL):
            index = step * UNROLL + lane
            strength = jnp.where(index < live, -REPULSION, 0.0)
            place = jnp.minimum(index, live - 1)
            left = neg_rows[place]
            other = neg_cols[place]
            shift = lax.rem(lax.div(other, CB) - row + row_count, row_count)
            right = shift * CB + lax.rem(other, CB)
            def push(left=left, right=right, strength=strength):
                kernel = kernel_of(left, right)
                return strength * kernel * kernel
            batch.append((left, right, push))
        apply_all(batch)

    def force_of(acc, value):
        return acc[:D_EMB] + acc[D_EMB + 16 :] - value * acc[D_EMB : D_EMB + 1]

    @pl.loop(0, col_count // 2)
    def _(pair):
        for side in range(2):
            for block in range(CB):
                value, group = row_y(pair, side, block)
                lanes = slice(block * BLK, (block + 1) * BLK)
                row_force[group, :, lanes] = force_of(left_acc[group * CB + block], value)

    for shift in range(row_count):
        for block in range(CB):
            lanes = slice(block * BLK, (block + 1) * BLK)
            col_force[shift][:, lanes] = force_of(right_acc[shift * CB + block], col_y[shift][:D_EMB, lanes])


def pair_forces(sizes, meta, listing, neg_rows, neg_cols, weights, row_y, col_y):
    row_count, col_count = sizes
    smem = pl.BlockSpec(memory_space=pltpu.SMEM)
    vmem = pl.BlockSpec(memory_space=pltpu.VMEM)
    lefts, rights = col_count * CB, row_count * CB
    tiles = col_count * 2 + 48
    outs = pl.pallas_call(
        functools.partial(force_kernel, row_count, col_count, len(row_y) > 1),
        in_specs=[smem] * 4 + [vmem] * (1 + len(row_y) + row_count),
        out_specs=[vmem] * (1 + row_count),
        out_shape=[jax.ShapeDtypeStruct((col_count, D_EMB, SPAN), F32)]
        + [jax.ShapeDtypeStruct((D_EMB, SPAN), F32)] * row_count,
        scratch_shapes=[
            pltpu.VMEM((lefts, STACK, BLK), BF16),
            pltpu.VMEM((rights, BLK, STACK), BF16),
            pltpu.VMEM((lefts, PULL, 2 * BLK), BF16),
            pltpu.VMEM((rights, PULL, 2 * BLK), BF16),
            pltpu.VMEM((lefts, PULL, BLK), F32),
            pltpu.VMEM((rights, PULL, BLK), F32),
            pltpu.VMEM((UNROLL, 2 * BLK, BLK), BF16),
            pltpu.VMEM((UNROLL, BLK, 2 * BLK), BF16),
        ],
        compiler_params=pltpu.CompilerParams(vmem_limit_bytes=VMEM_LIMIT),
        cost_estimate=pl.CostEstimate(
            flops=tiles * 2 * BLK * BLK * (STACK + 4 * PULL),
            bytes_accessed=4 * D_EMB * SPAN * 2 * (col_count + row_count),
            transcendentals=tiles * BLK * BLK,
        ),
        name="forces",
    )(meta, listing, neg_rows, neg_cols, weights, *row_y, *col_y)
    return outs[0], outs[1:]


def shards(inputs, rho, sigma, embed, knn_blocks, knn_seeds, neg_rows, neg_cols, neg_count):
    row_count = lax.axis_size("row")
    col_count = lax.axis_size("col")
    shifts = row_count // 2 + 1
    row, col = lax.axis_index("row"), lax.axis_index("col")
    listing = knn_blocks.reshape(-1)
    seeds = knn_seeds.reshape(-1)
    row_list, col_list = neg_rows.reshape(-1), neg_cols.reshape(-1)
    meta = jnp.stack([row, col, neg_count[0, 0]]).astype(I32)

    def from_shift(value, shift):
        pairs = [((r + shift) % row_count, r) for r in range(row_count)]
        return lax.ppermute(value, "row", pairs)

    def from_half(value):
        half = row_count // 2
        pairs = [(r + half, r) if r % 2 == 0 else (r, r + half) for r in range(half)]
        return lax.ppermute(value, "row", pairs)

    def to_shift(value, shift):
        pairs = [(r, (r + shift) % row_count) for r in range(row_count)]
        return lax.ppermute(value, "row", pairs)

    def from_bits(value, bits):
        pairs = [(c ^ bits, c) for c in range(col_count)]
        return lax.ppermute(value, "col", pairs)

    sizes = row_count, col_count
    single = [1 << place for place in range(1, (col_count - 1).bit_length())]
    early_bits = [0, 1] + [bits + core for bits in single for core in range(2)]
    late_bits = [bits for bits in range(col_count) if bits not in early_bits]
    meta = jnp.concatenate([meta, jnp.array(early_bits + late_bits, I32)])

    def after(value, *others):
        return lax.optimization_barrier((value, *others))[0]

    row_x = {0: inputs}
    for bits in single:
        row_x[bits] = from_bits(inputs, bits)
    col_x = [inputs] + [from_shift(inputs, shift) for shift in range(1, shifts - 1)]
    near = [row_x[bits] for bits in single] + col_x[1:]
    for bits in late_bits:
        if bits % 2 == 0:
            row_x[bits] = from_bits(inputs, bits)
    seed_row = jnp.pad(seeds.astype(F32)[None], ((0, 0), (0, SPAN - seeds.shape[0])))
    params = jnp.stack([rho, sigma])
    blank = jnp.zeros((PACK - SEEDS - 1, SPAN), F32)
    pack = jnp.concatenate([embed, params, jnp.zeros((1, SPAN), F32), seed_row, blank], axis=0)
    col_packs = [pack] + [from_shift(pack, shift) for shift in range(1, shifts)]
    row_x[1] = from_bits(after(inputs, *col_packs[1:]), 1)
    for bits in single:
        row_x[bits + 1] = from_bits(after(row_x[bits], *near), 1)
    col_x.append(from_half(after(inputs, row_x[1])))

    squares = jnp.sum(inputs * inputs, axis=1)[None]
    far_seeds = [far[SEEDS : SEEDS + 1] for far in col_packs[1:]]
    own_pack = jnp.concatenate([embed, params, squares, seed_row, *far_seeds, blank[shifts - 1 :]], axis=0)
    own_pack = after(own_pack, *[row_x[bits + 1] for bits in single])
    early = early_grams(sizes, meta, listing, col_x[:-1], [row_x[bits] for bits in early_bits[1:]])
    even_packs = jnp.stack([own_pack] + [from_bits(own_pack, bits) for bits in range(2, col_count, 2)])
    even_packs = after(even_packs, early[0])
    odd_packs = from_bits(even_packs, 1)
    for bits in late_bits:
        if bits % 2 == 0:
            row_x[bits + 1] = from_bits(after(row_x[bits], even_packs), 1)
    held = after(embed, *[row_x[bits] for bits in late_bits if bits % 2 == 0])
    col_y = col_packs + [from_shift(held, shift) for shift in range(shifts, row_count)]

    weights = pair_weights(
        sizes,
        meta,
        listing,
        seeds,
        early,
        col_x[-1],
        [row_x[bits] for bits in late_bits],
        col_packs + [even_packs, odd_packs],
    )

    row_y = (even_packs, odd_packs)
    for step in range(STEPS):
        if step:
            row_y = (lax.all_gather(embed, "col", axis=0, tiled=False),)
            col_y = [embed] + [from_shift(embed, shift) for shift in range(1, row_count)]
        row_force, col_force = pair_forces(sizes, meta, listing, row_list, col_list, weights, row_y, col_y)
        row_parts = lax.all_to_all(row_force, "col", split_axis=0, concat_axis=0, tiled=True)
        force = jnp.sum(row_parts, axis=0) + col_force[0]
        for shift in range(1, row_count):
            force = force + to_shift(col_force[shift], shift)
        embed = embed + STEP_SIZE * force
    return (embed, force * FORCE_SCALE)


def solution(mesh):
    in_specs = (
        P(("row", "col"), None),
        P(("row", "col")),
        P(("row", "col")),
        P(None, ("row", "col")),
        P("row", "col", None, None, None),
        P("row", "col", None, None),
        P("row", "col", None),
        P("row", "col", None),
        P("row", "col"),
    )
    out_specs = (P(None, ("row", "col")), P(None, ("row", "col")))
    return jax.shard_map(shards, mesh=mesh, in_specs=in_specs, out_specs=out_specs, check_vma=False)
```

```python
import functools

import jax
import jax.numpy as jnp
from jax import lax
from jax.experimental import pallas as pl
from jax.experimental.pallas import tpu as pltpu
from jax.sharding import PartitionSpec as P

D_EMB = 64
BLK = 128
CB = 2
SPAN = CB * BLK
STEPS = 2

STEP_SIZE = 0.0005
REPULSION = 2.0
FORCE_SCALE = 0.015625

RHO, SIGMA, SQUARES, SEEDS = D_EMB, D_EMB + 1, D_EMB + 2, D_EMB + 3
PACK = 72
STACK = 4 * D_EMB
PULL = 2 * D_EMB + 16
UNROLL = 12
F32, BF16, I32 = jnp.float32, jnp.bfloat16, jnp.int32


def split(value):
    high = value.astype(BF16)
    return high, (value - high.astype(F32)).astype(BF16)


def nt_dot(left, right):
    return lax.dot_general(left, right, (((1,), (1,)), ((), ())), preferred_element_type=F32)


def nn_dot(left, right):
    return lax.dot_general(left, right, (((1,), (0,)), ((), ())), preferred_element_type=F32)


def hash_bits(salt_value, first, second):
    mixed = first * 1103515245 + salt_value
    mixed = (mixed ^ second * 747796405) * 277803737
    return (mixed >> 17 & 1).astype(F32)


def takes_shift(shift, row, row_count):
    if 2 * shift != row_count:
        return True
    half = row_count // 2
    return jnp.where(row < half, row % 2 == 0, (row - half) % 2 == 1)


def each(count, body):
    if count <= 8:
        for index in range(count):
            body(index)
    else:
        pl.loop(0, count)(body)


def pick_of(sizes, meta, listing, bits, shift):
    row_count, _ = sizes
    place = lax.bitwise_xor(meta[1], bits) * row_count + lax.rem(meta[0] + shift, row_count)
    start_i = pl.multiple_of(listing[2 * place] * BLK, BLK)
    start_j = pl.multiple_of(listing[2 * place + 1] * BLK, BLK)
    return start_i, start_j, place


def vmem_limit(sizes):
    return (8 + 2 * sizes[1]) * 2**20


def gram_of(high_j, low_j, high_i, low_i):
    return nt_dot(high_j, low_i) + nt_dot(low_j, high_i) + nt_dot(high_j, high_i)


def grams_kernel(sizes, counts, meta, listing, *rest):
    shifts_early, rows_early = counts
    row_count, _ = sizes
    columns, rows = rest[:shifts_early], rest[shifts_early : shifts_early + rows_early - 1]
    grams, high_c, low_c, high_last, low_last, high_r, low_r = rest[shifts_early + rows_early - 1 :]
    for shift in range(shifts_early):
        high_c[shift], low_c[shift] = split(columns[shift][...])
    high_r[0], low_r[0] = high_c[0], low_c[0]
    for line in range(1, rows_early):
        high_r[line], low_r[line] = split(rows[line - 1][...])

    def row_span(line):
        bits = meta[3 + line]
        for shift in range(shifts_early):
            start_i, start_j, _ = pick_of(sizes, meta, listing, bits, shift)
            span_i, span_j = pl.ds(start_i, BLK), pl.ds(start_j, BLK)
            grams[line, shift] = gram_of(
                high_c[shift, span_j, :], low_c[shift, span_j, :], high_r[line, span_i, :], low_r[line, span_i, :]
            )
        start_i, _, _ = pick_of(sizes, meta, listing, bits, shifts_early)
        high_last[line] = high_r[line, pl.ds(start_i, BLK), :]
        low_last[line] = low_r[line, pl.ds(start_i, BLK), :]

    each(rows_early, row_span)


def early_grams(sizes, meta, listing, columns, rows):
    shifts_early, rows_early, depth = len(columns), len(rows) + 1, rows[0].shape[-1]
    smem = pl.BlockSpec(memory_space=pltpu.SMEM)
    vmem = pl.BlockSpec(memory_space=pltpu.VMEM)
    tiles = shifts_early * rows_early
    return pl.pallas_call(
        functools.partial(grams_kernel, sizes, (shifts_early, rows_early)),
        in_specs=[smem] * 2 + [vmem] * (len(columns) + len(rows)),
        out_specs=[vmem] * 5,
        out_shape=[
            jax.ShapeDtypeStruct((rows_early, shifts_early, BLK, BLK), F32),
            jax.ShapeDtypeStruct((shifts_early, SPAN, depth), BF16),
            jax.ShapeDtypeStruct((shifts_early, SPAN, depth), BF16),
            jax.ShapeDtypeStruct((rows_early, BLK, depth), BF16),
            jax.ShapeDtypeStruct((rows_early, BLK, depth), BF16),
        ],
        scratch_shapes=[pltpu.VMEM((rows_early, SPAN, depth), BF16)] * 2,
        compiler_params=pltpu.CompilerParams(vmem_limit_bytes=vmem_limit(sizes)),
        cost_estimate=pl.CostEstimate(
            flops=tiles * 6 * BLK * BLK * depth,
            bytes_accessed=(shifts_early + rows_early) * SPAN * depth * 4,
            transcendentals=0,
        ),
        name="grams",
    )(meta, listing, *columns, *rows)


def weights_kernel(sizes, counts, meta, listing, seeds, grams, high_c, low_c, high_last, low_last, *rest):
    row_count, col_count = sizes
    shifts_early, rows_early = counts
    shifts, rows_late = shifts_early + 1, col_count - rows_early
    last, late, col_packs = rest[0], rest[1 : 1 + rows_late], rest[1 + rows_late :][:shifts]
    even_packs, odd_packs = rest[1 + rows_late + shifts :][:2]
    out, high_l, low_l, high_r, low_r, late_grams, col_params, row_params = rest[3 + rows_late + shifts :]
    row, col = meta[0], meta[1]

    high_l[...], low_l[...] = split(last[...])
    for shift in range(shifts):
        for block in range(CB):
            lanes = slice(block * BLK, (block + 1) * BLK)
            col_params[shift, block] = col_packs[shift][RHO : RHO + 8, lanes].T
    for bits in range(col_count):
        row_params[bits] = (even_packs, odd_packs)[bits % 2][bits // 2, RHO : RHO + 8, :]
    for line in range(rows_late):
        high_r[line], low_r[line] = split(late[line][...])

    def early_last(line):
        _, start_j, _ = pick_of(sizes, meta, listing, meta[3 + line], shifts_early)
        span_j = pl.ds(start_j, BLK)
        late_grams[shifts_early, meta[3 + line]] = gram_of(
            high_l[span_j, :], low_l[span_j, :], high_last[line], low_last[line]
        )

    each(rows_early, early_last)

    def late_row(line):
        bits = meta[3 + rows_early + line]
        for shift in range(shifts):
            start_i, start_j, _ = pick_of(sizes, meta, listing, bits, shift)
            span_i, span_j = pl.ds(start_i, BLK), pl.ds(start_j, BLK)
            if shift == shifts_early:
                high_j, low_j = high_l[span_j, :], low_l[span_j, :]
            else:
                high_j, low_j = high_c[shift, span_j, :], low_c[shift, span_j, :]
            late_grams[shift, bits] = gram_of(high_j, low_j, high_r[line, span_i, :], low_r[line, span_i, :])

    each(rows_late, late_row)

    positions_j = lax.broadcasted_iota(I32, (BLK, BLK), 0)
    positions_i = lax.broadcasted_iota(I32, (BLK, BLK), 1)
    wanted_seed = lax.broadcasted_iota(I32, (1, SPAN), 1) == col * row_count + row

    def finish(bits, shift, gram):
        start_i, start_j, place = pick_of(sizes, meta, listing, bits, shift)
        params_i = row_params[bits, :, pl.ds(start_i, BLK)]
        rho_i, sigma_i, square_i = params_i[0:1], params_i[1:2], params_i[2:3]
        params_j = col_params[shift, lax.div(start_j, BLK)]
        rho_j, sigma_j, square_j = params_j[:, 0:1], params_j[:, 1:2], params_j[:, 2:3]
        distance = jnp.sqrt(jnp.maximum(square_j + square_i - 2.0 * gram, 1.0))
        plane_seeds = row_params[bits, SEEDS - RHO + shift : SEEDS - RHO + shift + 1, :]
        seed_back = jnp.sum(jnp.where(wanted_seed, plane_seeds, 0.0), axis=1, keepdims=True).astype(I32)
        ahead = hash_bits(seeds[place], positions_i, positions_j) * jnp.exp(
            jnp.maximum(distance - rho_i, 0.0) * (-1.0 / sigma_i)
        )
        behind = hash_bits(seed_back, positions_j, positions_i) * jnp.exp(
            jnp.maximum(distance - rho_j, 0.0) * (-1.0 / sigma_j)
        )
        weights = (ahead + behind - ahead * behind).astype(BF16)
        if shift == 0:
            weights = (weights.astype(F32) * jnp.where(bits == 0, 0.5, 1.0)).astype(BF16)
        out[shift * col_count + bits] = weights

    def early_rows(line):
        bits = meta[3 + line]
        for shift in range(shifts):
            finish(bits, shift, grams[line, shift] if shift < shifts_early else late_grams[shift, bits])

    def late_rows(line):
        bits = meta[3 + rows_early + line]
        for shift in range(shifts):
            finish(bits, shift, late_grams[shift, bits])

    each(rows_early, early_rows)
    each(rows_late, late_rows)


def pair_weights(sizes, meta, listing, seeds, early, last, late, packs):
    _, col_count = sizes
    shifts, depth = len(packs) - 2, late[0].shape[-1]
    rows_late = len(late)
    smem = pl.BlockSpec(memory_space=pltpu.SMEM)
    vmem = pl.BlockSpec(memory_space=pltpu.VMEM)
    tiles = shifts * col_count
    return pl.pallas_call(
        functools.partial(weights_kernel, sizes, (shifts - 1, col_count - rows_late)),
        in_specs=[smem] * 3 + [vmem] * (5 + 1 + rows_late + len(packs)),
        out_specs=vmem,
        out_shape=jax.ShapeDtypeStruct((tiles, BLK, BLK), BF16),
        scratch_shapes=[
            pltpu.VMEM((SPAN, depth), BF16),
            pltpu.VMEM((SPAN, depth), BF16),
            pltpu.VMEM((rows_late, SPAN, depth), BF16),
            pltpu.VMEM((rows_late, SPAN, depth), BF16),
            pltpu.VMEM((shifts, col_count, BLK, BLK), F32),
            pltpu.VMEM((shifts, CB, BLK, 8), F32),
            pltpu.VMEM((col_count, 8, SPAN), F32),
        ],
        compiler_params=pltpu.CompilerParams(vmem_limit_bytes=vmem_limit(sizes)),
        cost_estimate=pl.CostEstimate(
            flops=tiles * 3 * BLK * BLK * depth,
            bytes_accessed=(1 + rows_late) * SPAN * depth * 4,
            transcendentals=tiles * 3 * BLK * BLK,
        ),
        name="weights",
    )(meta, listing, seeds, *early, last, *late, *packs)


def force_kernel(row_count, col_count, by_bits, meta, listing, neg_rows, neg_cols, weights, *rest):
    shifts = row_count // 2 + 1
    row_arrays, rest = (rest[:2], rest[2:]) if by_bits else (rest[:1], rest[1:])
    col_y = rest[:row_count]
    row_force, col_force = rest[row_count], rest[row_count + 1 : 2 * row_count + 1]
    left_gram, right_gram, left_pull, right_pull, left_acc, right_acc, held_v, held_h = rest[2 * row_count + 1 :]
    row, col, live = meta[0], meta[1], meta[2]
    iota = lax.broadcasted_iota(I32, (D_EMB, BLK), 0)
    ones = jnp.ones((16, BLK), BF16)
    blank = jnp.zeros((D_EMB, BLK), BF16)

    def norm_rows(value, first):
        norm = jnp.sum(value * value, axis=0, keepdims=True)
        high, rest_ = split(norm)
        left_over = norm - high.astype(F32) - rest_.astype(F32)
        high, middle = high.astype(F32), rest_.astype(F32)
        return jnp.where(
            iota == first,
            high,
            jnp.where(iota == first + 1, middle, jnp.where(iota == first + 2, left_over, 0.0)),
        )

    def pulls(high, low):
        top = jnp.concatenate([high, ones, low], axis=0)
        bottom = jnp.concatenate([high, ones, blank], axis=0)
        return jnp.concatenate([top, bottom], axis=1)

    def left_block(index, value):
        high, low = split(value)
        extra = norm_rows(value, 0) + jnp.where((iota >= 3) & (iota < 7), 1.0, 0.0)
        left_gram[index] = jnp.concatenate([high, low, high, extra.astype(BF16)], axis=0)
        left_pull[index] = pulls(high, low)
        left_acc[index] = jnp.zeros((PULL, BLK), F32)

    def right_block(index, value):
        high, low = split(value)
        extra = norm_rows(value, 3) + jnp.where((iota < 3) | (iota == 6), 1.0, 0.0)
        twice_high, twice_low = -2.0 * high.astype(F32), -2.0 * low.astype(F32)
        stack = jnp.concatenate([twice_high, twice_high, twice_low, extra], axis=0)
        right_gram[index] = stack.T.astype(BF16)
        right_pull[index] = pulls(high, low)
        right_acc[index] = jnp.zeros((PULL, BLK), F32)

    def row_y(pair, side, block):
        lanes = slice(block * BLK, (block + 1) * BLK)
        line = pair * 2 + side
        if by_bits:
            return row_arrays[side][pair, :D_EMB, lanes], lax.bitwise_xor(line, col)
        return row_arrays[0][line, :D_EMB, lanes], line

    @pl.loop(0, col_count // 2)
    def _(pair):
        for side in range(2):
            for block in range(CB):
                value, group = row_y(pair, side, block)
                left_block(group * CB + block, value)

    for shift in range(row_count):
        for block in range(CB):
            right_block(shift * CB + block, col_y[shift][:D_EMB, block * BLK : (block + 1) * BLK])

    def kernel_of(left, right):
        return 1.0 / nn_dot(right_gram[right], left_gram[left])

    def apply_all(tiles_):
        for lane, (left, right, coefficient) in enumerate(tiles_):
            high, low = split(coefficient())
            held_v[lane, :BLK], held_v[lane, BLK:] = high, low
            held_h[lane, :, :BLK], held_h[lane, :, BLK:] = high, low
        for lane, (left, right, _) in enumerate(tiles_):
            left_acc[left] += nn_dot(right_pull[right], held_v[lane])
        for lane, (left, right, _) in enumerate(tiles_):
            right_acc[right] += nt_dot(left_pull[left], held_h[lane])

    def near_active(group):
        offset = lax.rem(group - col + col_count, col_count)
        return (2 * offset < col_count) | ((2 * offset == col_count) & (2 * col < col_count))

    near = col_count // 2 + 1
    tiles = near + col_count * (shifts - 1)
    last = jnp.where(takes_shift(shifts - 1, row, row_count), tiles, tiles - col_count)

    @pl.loop(0, lax.div(last + UNROLL - 1, UNROLL))
    def _(step):
        batch = []
        for lane in range(UNROLL):
            index = step * UNROLL + lane
            far = jnp.maximum(index - near, 0)
            shift = jnp.where(index < near, 0, 1 + lax.div(far, col_count))
            group = jnp.where(index < near, lax.rem(col + index, col_count), lax.rem(far, col_count))
            inside = index < last
            shift = jnp.where(inside, shift, 0)
            inside &= (shift > 0) | near_active(group)
            slot = shift * col_count + lax.bitwise_xor(group, col)
            entry = (group * row_count + lax.rem(row + shift, row_count)) * 2
            left = group * CB + listing[entry]
            right = shift * CB + listing[entry + 1]

            def pull(left=left, right=right, slot=slot, inside=inside):
                return weights[slot].astype(F32) * (kernel_of(left, right) * jnp.where(inside, 1.0, 0.0))

            batch.append((left, right, pull))
        apply_all(batch)

    @pl.loop(0, lax.div(live + UNROLL - 1, UNROLL))
    def _(step):
        batch = []
        for lane in range(UNROLL):
            index = step * UNROLL + lane
            strength = jnp.where(index < live, -REPULSION, 0.0)
            place = jnp.minimum(index, live - 1)
            left = neg_rows[place]
            other = neg_cols[place]
            shift = lax.rem(lax.div(other, CB) - row + row_count, row_count)
            right = shift * CB + lax.rem(other, CB)
            def push(left=left, right=right, strength=strength):
                kernel = kernel_of(left, right)
                return strength * kernel * kernel
            batch.append((left, right, push))
        apply_all(batch)

    def force_of(acc, value):
        return acc[:D_EMB] + acc[D_EMB + 16 :] - value * acc[D_EMB : D_EMB + 1]

    @pl.loop(0, col_count // 2)
    def _(pair):
        for side in range(2):
            for block in range(CB):
                value, group = row_y(pair, side, block)
                lanes = slice(block * BLK, (block + 1) * BLK)
                row_force[group, :, lanes] = force_of(left_acc[group * CB + block], value)

    for shift in range(row_count):
        for block in range(CB):
            lanes = slice(block * BLK, (block + 1) * BLK)
            col_force[shift][:, lanes] = force_of(right_acc[shift * CB + block], col_y[shift][:D_EMB, lanes])


def pair_forces(sizes, meta, listing, neg_rows, neg_cols, weights, row_y, col_y):
    row_count, col_count = sizes
    smem = pl.BlockSpec(memory_space=pltpu.SMEM)
    vmem = pl.BlockSpec(memory_space=pltpu.VMEM)
    lefts, rights = col_count * CB, row_count * CB
    tiles = col_count * 2 + 48
    outs = pl.pallas_call(
        functools.partial(force_kernel, row_count, col_count, len(row_y) > 1),
        in_specs=[smem] * 4 + [vmem] * (1 + len(row_y) + row_count),
        out_specs=[vmem] * (1 + row_count),
        out_shape=[jax.ShapeDtypeStruct((col_count, D_EMB, SPAN), F32)]
        + [jax.ShapeDtypeStruct((D_EMB, SPAN), F32)] * row_count,
        scratch_shapes=[
            pltpu.VMEM((lefts, STACK, BLK), BF16),
            pltpu.VMEM((rights, BLK, STACK), BF16),
            pltpu.VMEM((lefts, PULL, 2 * BLK), BF16),
            pltpu.VMEM((rights, PULL, 2 * BLK), BF16),
            pltpu.VMEM((lefts, PULL, BLK), F32),
            pltpu.VMEM((rights, PULL, BLK), F32),
            pltpu.VMEM((UNROLL, 2 * BLK, BLK), BF16),
            pltpu.VMEM((UNROLL, BLK, 2 * BLK), BF16),
        ],
        compiler_params=pltpu.CompilerParams(vmem_limit_bytes=vmem_limit(sizes)),
        cost_estimate=pl.CostEstimate(
            flops=tiles * 2 * BLK * BLK * (STACK + 4 * PULL),
            bytes_accessed=4 * D_EMB * SPAN * 2 * (col_count + row_count),
            transcendentals=tiles * BLK * BLK,
        ),
        name="forces",
    )(meta, listing, neg_rows, neg_cols, weights, *row_y, *col_y)
    return outs[0], outs[1:]


def shards(inputs, rho, sigma, embed, knn_blocks, knn_seeds, neg_rows, neg_cols, neg_count):
    row_count = lax.axis_size("row")
    col_count = lax.axis_size("col")
    shifts = row_count // 2 + 1
    row, col = lax.axis_index("row"), lax.axis_index("col")
    listing = knn_blocks.reshape(-1)
    seeds = knn_seeds.reshape(-1)
    row_list, col_list = neg_rows.reshape(-1), neg_cols.reshape(-1)
    meta = jnp.stack([row, col, neg_count[0, 0]]).astype(I32)

    def from_shift(value, shift):
        pairs = [((r + shift) % row_count, r) for r in range(row_count)]
        return lax.ppermute(value, "row", pairs)

    def from_half(value):
        half = row_count // 2
        pairs = [(r + half, r) if r % 2 == 0 else (r, r + half) for r in range(half)]
        return lax.ppermute(value, "row", pairs)

    def to_shift(value, shift):
        pairs = [(r, (r + shift) % row_count) for r in range(row_count)]
        return lax.ppermute(value, "row", pairs)

    def from_bits(value, bits):
        pairs = [(c ^ bits, c) for c in range(col_count)]
        return lax.ppermute(value, "col", pairs)

    sizes = row_count, col_count
    single = [1 << place for place in range(1, (col_count - 1).bit_length())]
    early_bits = [0, 1] + [bits + core for bits in single for core in range(2)]
    late_bits = [bits for bits in range(col_count) if bits not in early_bits]
    meta = jnp.concatenate([meta, jnp.array(early_bits + late_bits, I32)])

    def after(value, *others):
        return lax.optimization_barrier((value, *others))[0]

    row_x = {0: inputs}
    for bits in single:
        row_x[bits] = from_bits(inputs, bits)
    col_x = [inputs] + [from_shift(inputs, shift) for shift in range(1, shifts - 1)]
    near = [row_x[bits] for bits in single] + col_x[1:]
    for bits in late_bits:
        if bits % 2 == 0:
            row_x[bits] = from_bits(inputs, bits)
    seed_row = jnp.pad(seeds.astype(F32)[None], ((0, 0), (0, SPAN - seeds.shape[0])))
    params = jnp.stack([rho, sigma, jnp.sum(inputs * inputs, axis=1)])
    blank = jnp.zeros((PACK - SEEDS - 1, SPAN), F32)
    pack = jnp.concatenate([embed, params, seed_row, blank], axis=0)
    col_packs = [pack] + [from_shift(pack, shift) for shift in range(1, shifts)]
    held, meta, listing, seeds = lax.optimization_barrier((inputs, meta, listing, seeds, *col_packs[1:]))[:4]
    row_x[1] = from_bits(held, 1)
    for bits in single:
        row_x[bits + 1] = from_bits(after(row_x[bits], *near), 1)
    col_x.append(from_half(after(inputs, row_x[1])))

    own_pack = pack
    for shift in range(1, shifts):
        place = SEEDS + shift
        far_seed = col_packs[shift][SEEDS : SEEDS + 1]
        own_pack = own_pack + jnp.pad(far_seed, ((place, PACK - place - 1), (0, 0)))
    own_pack = after(own_pack, *[row_x[bits + 1] for bits in single])
    early = early_grams(sizes, meta, listing, col_x[:-1], [row_x[bits] for bits in early_bits[1:]])
    even_packs = jnp.stack([own_pack] + [from_bits(own_pack, bits) for bits in range(2, col_count, 2)])
    even_packs = after(even_packs, early[0])
    odd_packs = from_bits(even_packs, 1)
    for bits in late_bits:
        if bits % 2 == 0:
            row_x[bits + 1] = from_bits(after(row_x[bits], even_packs), 1)
    held = after(embed, *[row_x[bits] for bits in late_bits if bits % 2 == 0])
    col_y = col_packs + [from_shift(held, shift) for shift in range(shifts, row_count)]

    weights = pair_weights(
        sizes,
        meta,
        listing,
        seeds,
        early,
        col_x[-1],
        [row_x[bits] for bits in late_bits],
        col_packs + [even_packs, odd_packs],
    )

    row_y = (even_packs, odd_packs)
    for step in range(STEPS):
        if step:
            col_y = [embed] + [from_shift(embed, shift) for shift in range(1, row_count)]
            even = jnp.stack([embed] + [from_bits(embed, bits) for bits in range(2, col_count, 2)])
            row_y = (even, from_bits(even, 1))
        row_force, col_force = pair_forces(sizes, meta, listing, row_list, col_list, weights, row_y, col_y)
        row_parts = lax.all_to_all(row_force, "col", split_axis=0, concat_axis=0, tiled=True)
        force = jnp.sum(row_parts, axis=0) + col_force[0]
        for shift in range(1, row_count):
            force = force + to_shift(col_force[shift], shift)
        embed = embed + STEP_SIZE * force
    return (embed, force * FORCE_SCALE)


def solution(mesh):
    in_specs = (
        P(("row", "col"), None),
        P(("row", "col")),
        P(("row", "col")),
        P(None, ("row", "col")),
        P("row", "col", None, None, None),
        P("row", "col", None, None),
        P("row", "col", None),
        P("row", "col", None),
        P("row", "col"),
    )
    out_specs = (P(None, ("row", "col")), P(None, ("row", "col")))
    return jax.shard_map(shards, mesh=mesh, in_specs=in_specs, out_specs=out_specs, check_vma=False)
```

```python
import functools

import jax
import jax.numpy as jnp
from jax import lax
from jax.experimental import pallas as pl
from jax.experimental.pallas import tpu as pltpu
from jax.sharding import PartitionSpec as P

D_EMB = 64
BLK = 128
CB = 2
SPAN = CB * BLK
STEPS = 2

STEP_SIZE = 0.0005
REPULSION = 2.0
FORCE_SCALE = 0.015625

RHO, SIGMA, SQUARES, SEEDS = D_EMB, D_EMB + 1, D_EMB + 2, D_EMB + 3
PACK = 72
STACK = 4 * D_EMB
PULL = 2 * D_EMB + 16
UNROLL = 12
F32, BF16, I32 = jnp.float32, jnp.bfloat16, jnp.int32


def split(value):
    high = value.astype(BF16)
    return high, (value - high.astype(F32)).astype(BF16)


def nt_dot(left, right):
    return lax.dot_general(left, right, (((1,), (1,)), ((), ())), preferred_element_type=F32)


def nn_dot(left, right):
    return lax.dot_general(left, right, (((1,), (0,)), ((), ())), preferred_element_type=F32)


def hash_bits(salt_value, first, second):
    mixed = first * 1103515245 + salt_value
    mixed = (mixed ^ second * 747796405) * 277803737
    return (mixed >> 17 & 1).astype(F32)


def takes_shift(shift, row, row_count):
    if 2 * shift != row_count:
        return True
    half = row_count // 2
    return jnp.where(row < half, row % 2 == 0, (row - half) % 2 == 1)


def each(count, body):
    if count <= 8:
        for index in range(count):
            body(index)
    else:
        pl.loop(0, count)(body)


def pick_of(sizes, meta, listing, bits, shift):
    row_count, _ = sizes
    place = lax.bitwise_xor(meta[1], bits) * row_count + lax.rem(meta[0] + shift, row_count)
    start_i = pl.multiple_of(listing[2 * place] * BLK, BLK)
    start_j = pl.multiple_of(listing[2 * place + 1] * BLK, BLK)
    return start_i, start_j, place


def vmem_limit(sizes):
    return (8 + 2 * sizes[1]) * 2**20


def gram_of(high_j, low_j, high_i, low_i):
    return nt_dot(high_j, low_i) + nt_dot(low_j, high_i) + nt_dot(high_j, high_i)


def grams_kernel(sizes, counts, meta, listing, *rest):
    shifts_early, rows_early = counts
    row_count, _ = sizes
    columns, rows = rest[:shifts_early], rest[shifts_early : shifts_early + rows_early - 1]
    grams, high_c, low_c, high_last, low_last, high_r, low_r = rest[shifts_early + rows_early - 1 :]
    for shift in range(shifts_early):
        high_c[shift], low_c[shift] = split(columns[shift][...])
    high_r[0], low_r[0] = high_c[0], low_c[0]
    for line in range(1, rows_early):
        high_r[line], low_r[line] = split(rows[line - 1][...])

    def row_span(line):
        bits = meta[3 + line]
        for shift in range(shifts_early):
            start_i, start_j, _ = pick_of(sizes, meta, listing, bits, shift)
            span_i, span_j = pl.ds(start_i, BLK), pl.ds(start_j, BLK)
            grams[line, shift] = gram_of(
                high_c[shift, span_j, :], low_c[shift, span_j, :], high_r[line, span_i, :], low_r[line, span_i, :]
            )
        start_i, _, _ = pick_of(sizes, meta, listing, bits, shifts_early)
        high_last[line] = high_r[line, pl.ds(start_i, BLK), :]
        low_last[line] = low_r[line, pl.ds(start_i, BLK), :]

    each(rows_early, row_span)


def early_grams(sizes, meta, listing, columns, rows):
    shifts_early, rows_early, depth = len(columns), len(rows) + 1, rows[0].shape[-1]
    smem = pl.BlockSpec(memory_space=pltpu.SMEM)
    vmem = pl.BlockSpec(memory_space=pltpu.VMEM)
    tiles = shifts_early * rows_early
    return pl.pallas_call(
        functools.partial(grams_kernel, sizes, (shifts_early, rows_early)),
        in_specs=[smem] * 2 + [vmem] * (len(columns) + len(rows)),
        out_specs=[vmem] * 5,
        out_shape=[
            jax.ShapeDtypeStruct((rows_early, shifts_early, BLK, BLK), F32),
            jax.ShapeDtypeStruct((shifts_early, SPAN, depth), BF16),
            jax.ShapeDtypeStruct((shifts_early, SPAN, depth), BF16),
            jax.ShapeDtypeStruct((rows_early, BLK, depth), BF16),
            jax.ShapeDtypeStruct((rows_early, BLK, depth), BF16),
        ],
        scratch_shapes=[pltpu.VMEM((rows_early, SPAN, depth), BF16)] * 2,
        compiler_params=pltpu.CompilerParams(vmem_limit_bytes=vmem_limit(sizes)),
        cost_estimate=pl.CostEstimate(
            flops=tiles * 6 * BLK * BLK * depth,
            bytes_accessed=(shifts_early + rows_early) * SPAN * depth * 4,
            transcendentals=0,
        ),
        name="grams",
    )(meta, listing, *columns, *rows)


def weights_kernel(sizes, counts, meta, listing, seeds, grams, high_c, low_c, high_last, low_last, *rest):
    row_count, col_count = sizes
    shifts_early, rows_early = counts
    shifts, rows_late = shifts_early + 1, col_count - rows_early
    spans = CB * (1 + rows_late)
    last, late, col_packs = rest[:CB], rest[CB:spans], rest[spans : spans + shifts]
    even_packs, odd_packs = rest[spans + shifts :][:2]
    out, high_l, low_l, high_r, low_r, late_grams, col_params, row_params = rest[spans + shifts + 2 :]
    row, col = meta[0], meta[1]

    for block in range(CB):
        high_l[block * BLK : (block + 1) * BLK], low_l[block * BLK : (block + 1) * BLK] = split(last[block][...])
    for shift in range(shifts):
        for block in range(CB):
            lanes = slice(block * BLK, (block + 1) * BLK)
            col_params[shift, block] = col_packs[shift][RHO : RHO + 8, lanes].T
    for bits in range(col_count):
        row_params[bits] = (even_packs, odd_packs)[bits % 2][bits // 2, RHO : RHO + 8, :]
    for line in range(rows_late):
        for block in range(CB):
            part = slice(block * BLK, (block + 1) * BLK)
            high_r[line, part], low_r[line, part] = split(late[CB * line + block][...])

    def early_last(line):
        _, start_j, _ = pick_of(sizes, meta, listing, meta[3 + line], shifts_early)
        span_j = pl.ds(start_j, BLK)
        late_grams[shifts_early, meta[3 + line]] = gram_of(
            high_l[span_j, :], low_l[span_j, :], high_last[line], low_last[line]
        )

    each(rows_early, early_last)

    def late_row(line):
        bits = meta[3 + rows_early + line]
        for shift in range(shifts):
            start_i, start_j, _ = pick_of(sizes, meta, listing, bits, shift)
            span_i, span_j = pl.ds(start_i, BLK), pl.ds(start_j, BLK)
            if shift == shifts_early:
                high_j, low_j = high_l[span_j, :], low_l[span_j, :]
            else:
                high_j, low_j = high_c[shift, span_j, :], low_c[shift, span_j, :]
            late_grams[shift, bits] = gram_of(high_j, low_j, high_r[line, span_i, :], low_r[line, span_i, :])

    each(rows_late, late_row)

    positions_j = lax.broadcasted_iota(I32, (BLK, BLK), 0)
    positions_i = lax.broadcasted_iota(I32, (BLK, BLK), 1)
    wanted_seed = lax.broadcasted_iota(I32, (1, SPAN), 1) == col * row_count + row

    def finish(bits, shift, gram):
        start_i, start_j, place = pick_of(sizes, meta, listing, bits, shift)
        params_i = row_params[bits, :, pl.ds(start_i, BLK)]
        rho_i, sigma_i, square_i = params_i[0:1], params_i[1:2], params_i[2:3]
        params_j = col_params[shift, lax.div(start_j, BLK)]
        rho_j, sigma_j, square_j = params_j[:, 0:1], params_j[:, 1:2], params_j[:, 2:3]
        distance = jnp.sqrt(jnp.maximum(square_j + square_i - 2.0 * gram, 1.0))
        plane_seeds = row_params[bits, SEEDS - RHO + shift : SEEDS - RHO + shift + 1, :]
        seed_back = jnp.sum(jnp.where(wanted_seed, plane_seeds, 0.0), axis=1, keepdims=True).astype(I32)
        ahead = hash_bits(seeds[place], positions_i, positions_j) * jnp.exp(
            jnp.maximum(distance - rho_i, 0.0) * (-1.0 / sigma_i)
        )
        behind = hash_bits(seed_back, positions_j, positions_i) * jnp.exp(
            jnp.maximum(distance - rho_j, 0.0) * (-1.0 / sigma_j)
        )
        weights = (ahead + behind - ahead * behind).astype(BF16)
        if shift == 0:
            weights = (weights.astype(F32) * jnp.where(bits == 0, 0.5, 1.0)).astype(BF16)
        out[shift * col_count + bits] = weights

    def early_rows(line):
        bits = meta[3 + line]
        for shift in range(shifts):
            finish(bits, shift, grams[line, shift] if shift < shifts_early else late_grams[shift, bits])

    def late_rows(line):
        bits = meta[3 + rows_early + line]
        for shift in range(shifts):
            finish(bits, shift, late_grams[shift, bits])

    each(rows_early, early_rows)
    each(rows_late, late_rows)


def pair_weights(sizes, meta, listing, seeds, early, last, late, packs):
    _, col_count = sizes
    shifts, depth = len(packs) - 2, late[0].shape[-1]
    rows_late = len(late) // CB
    smem = pl.BlockSpec(memory_space=pltpu.SMEM)
    vmem = pl.BlockSpec(memory_space=pltpu.VMEM)
    tiles = shifts * col_count
    return pl.pallas_call(
        functools.partial(weights_kernel, sizes, (shifts - 1, col_count - rows_late)),
        in_specs=[smem] * 3 + [vmem] * (5 + CB * (1 + rows_late) + len(packs)),
        out_specs=vmem,
        out_shape=jax.ShapeDtypeStruct((tiles, BLK, BLK), BF16),
        scratch_shapes=[
            pltpu.VMEM((SPAN, depth), BF16),
            pltpu.VMEM((SPAN, depth), BF16),
            pltpu.VMEM((rows_late, SPAN, depth), BF16),
            pltpu.VMEM((rows_late, SPAN, depth), BF16),
            pltpu.VMEM((shifts, col_count, BLK, BLK), F32),
            pltpu.VMEM((shifts, CB, BLK, 8), F32),
            pltpu.VMEM((col_count, 8, SPAN), F32),
        ],
        compiler_params=pltpu.CompilerParams(vmem_limit_bytes=vmem_limit(sizes)),
        cost_estimate=pl.CostEstimate(
            flops=tiles * 3 * BLK * BLK * depth,
            bytes_accessed=(1 + rows_late) * SPAN * depth * 4,
            transcendentals=tiles * 3 * BLK * BLK,
        ),
        name="weights",
    )(meta, listing, seeds, *early, *last, *late, *packs)


def force_kernel(row_count, col_count, by_bits, meta, listing, neg_rows, neg_cols, weights, *rest):
    shifts = row_count // 2 + 1
    row_arrays, rest = (rest[:2], rest[2:]) if by_bits else (rest[:1], rest[1:])
    col_y = rest[:row_count]
    row_force, col_force = rest[row_count], rest[row_count + 1 : 2 * row_count + 1]
    left_gram, right_gram, left_pull, right_pull, left_acc, right_acc, held_v, held_h = rest[2 * row_count + 1 :]
    row, col, live = meta[0], meta[1], meta[2]
    iota = lax.broadcasted_iota(I32, (D_EMB, BLK), 0)
    ones = jnp.ones((16, BLK), BF16)
    blank = jnp.zeros((D_EMB, BLK), BF16)

    def norm_rows(value, first):
        norm = jnp.sum(value * value, axis=0, keepdims=True)
        high, rest_ = split(norm)
        left_over = norm - high.astype(F32) - rest_.astype(F32)
        high, middle = high.astype(F32), rest_.astype(F32)
        return jnp.where(
            iota == first,
            high,
            jnp.where(iota == first + 1, middle, jnp.where(iota == first + 2, left_over, 0.0)),
        )

    def pulls(high, low):
        top = jnp.concatenate([high, ones, low], axis=0)
        bottom = jnp.concatenate([high, ones, blank], axis=0)
        return jnp.concatenate([top, bottom], axis=1)

    def left_block(index, value):
        high, low = split(value)
        extra = norm_rows(value, 0) + jnp.where((iota >= 3) & (iota < 7), 1.0, 0.0)
        left_gram[index] = jnp.concatenate([high, low, high, extra.astype(BF16)], axis=0)
        left_pull[index] = pulls(high, low)
        left_acc[index] = jnp.zeros((PULL, BLK), F32)

    def right_block(index, value):
        high, low = split(value)
        extra = norm_rows(value, 3) + jnp.where((iota < 3) | (iota == 6), 1.0, 0.0)
        twice_high, twice_low = -2.0 * high.astype(F32), -2.0 * low.astype(F32)
        stack = jnp.concatenate([twice_high, twice_high, twice_low, extra], axis=0)
        right_gram[index] = stack.T.astype(BF16)
        right_pull[index] = pulls(high, low)
        right_acc[index] = jnp.zeros((PULL, BLK), F32)

    def row_y(pair, side, block):
        lanes = slice(block * BLK, (block + 1) * BLK)
        line = pair * 2 + side
        if by_bits:
            return row_arrays[side][pair, :D_EMB, lanes], lax.bitwise_xor(line, col)
        return row_arrays[0][line, :D_EMB, lanes], line

    @pl.loop(0, col_count // 2)
    def _(pair):
        for side in range(2):
            for block in range(CB):
                value, group = row_y(pair, side, block)
                left_block(group * CB + block, value)

    for shift in range(row_count):
        for block in range(CB):
            right_block(shift * CB + block, col_y[shift][:D_EMB, block * BLK : (block + 1) * BLK])

    def kernel_of(left, right):
        return 1.0 / nn_dot(right_gram[right], left_gram[left])

    def apply_all(tiles_):
        for lane, (left, right, coefficient) in enumerate(tiles_):
            high, low = split(coefficient())
            held_v[lane, :BLK], held_v[lane, BLK:] = high, low
            held_h[lane, :, :BLK], held_h[lane, :, BLK:] = high, low
        for lane, (left, right, _) in enumerate(tiles_):
            left_acc[left] += nn_dot(right_pull[right], held_v[lane])
        for lane, (left, right, _) in enumerate(tiles_):
            right_acc[right] += nt_dot(left_pull[left], held_h[lane])

    def near_active(group):
        offset = lax.rem(group - col + col_count, col_count)
        return (2 * offset < col_count) | ((2 * offset == col_count) & (2 * col < col_count))

    near = col_count // 2 + 1
    tiles = near + col_count * (shifts - 1)
    last = jnp.where(takes_shift(shifts - 1, row, row_count), tiles, tiles - col_count)

    @pl.loop(0, lax.div(last + UNROLL - 1, UNROLL))
    def _(step):
        batch = []
        for lane in range(UNROLL):
            index = step * UNROLL + lane
            far = jnp.maximum(index - near, 0)
            shift = jnp.where(index < near, 0, 1 + lax.div(far, col_count))
            group = jnp.where(index < near, lax.rem(col + index, col_count), lax.rem(far, col_count))
            inside = index < last
            shift = jnp.where(inside, shift, 0)
            inside &= (shift > 0) | near_active(group)
            slot = shift * col_count + lax.bitwise_xor(group, col)
            entry = (group * row_count + lax.rem(row + shift, row_count)) * 2
            left = group * CB + listing[entry]
            right = shift * CB + listing[entry + 1]

            def pull(left=left, right=right, slot=slot, inside=inside):
                return weights[slot].astype(F32) * (kernel_of(left, right) * jnp.where(inside, 1.0, 0.0))

            batch.append((left, right, pull))
        apply_all(batch)

    @pl.loop(0, lax.div(live + UNROLL - 1, UNROLL))
    def _(step):
        batch = []
        for lane in range(UNROLL):
            index = step * UNROLL + lane
            strength = jnp.where(index < live, -REPULSION, 0.0)
            place = jnp.minimum(index, live - 1)
            left = neg_rows[place]
            other = neg_cols[place]
            shift = lax.rem(lax.div(other, CB) - row + row_count, row_count)
            right = shift * CB + lax.rem(other, CB)
            def push(left=left, right=right, strength=strength):
                kernel = kernel_of(left, right)
                return strength * kernel * kernel
            batch.append((left, right, push))
        apply_all(batch)

    def force_of(acc, value):
        return acc[:D_EMB] + acc[D_EMB + 16 :] - value * acc[D_EMB : D_EMB + 1]

    @pl.loop(0, col_count // 2)
    def _(pair):
        for side in range(2):
            for block in range(CB):
                value, group = row_y(pair, side, block)
                lanes = slice(block * BLK, (block + 1) * BLK)
                row_force[group, :, lanes] = force_of(left_acc[group * CB + block], value)

    for shift in range(row_count):
        for block in range(CB):
            lanes = slice(block * BLK, (block + 1) * BLK)
            col_force[shift][:, lanes] = force_of(right_acc[shift * CB + block], col_y[shift][:D_EMB, lanes])


def pair_forces(sizes, meta, listing, neg_rows, neg_cols, weights, row_y, col_y):
    row_count, col_count = sizes
    smem = pl.BlockSpec(memory_space=pltpu.SMEM)
    vmem = pl.BlockSpec(memory_space=pltpu.VMEM)
    lefts, rights = col_count * CB, row_count * CB
    tiles = col_count * 2 + 48
    outs = pl.pallas_call(
        functools.partial(force_kernel, row_count, col_count, len(row_y) > 1),
        in_specs=[smem] * 4 + [vmem] * (1 + len(row_y) + row_count),
        out_specs=[vmem] * (1 + row_count),
        out_shape=[jax.ShapeDtypeStruct((col_count, D_EMB, SPAN), F32)]
        + [jax.ShapeDtypeStruct((D_EMB, SPAN), F32)] * row_count,
        scratch_shapes=[
            pltpu.VMEM((lefts, STACK, BLK), BF16),
            pltpu.VMEM((rights, BLK, STACK), BF16),
            pltpu.VMEM((lefts, PULL, 2 * BLK), BF16),
            pltpu.VMEM((rights, PULL, 2 * BLK), BF16),
            pltpu.VMEM((lefts, PULL, BLK), F32),
            pltpu.VMEM((rights, PULL, BLK), F32),
            pltpu.VMEM((UNROLL, 2 * BLK, BLK), BF16),
            pltpu.VMEM((UNROLL, BLK, 2 * BLK), BF16),
        ],
        compiler_params=pltpu.CompilerParams(vmem_limit_bytes=vmem_limit(sizes)),
        cost_estimate=pl.CostEstimate(
            flops=tiles * 2 * BLK * BLK * (STACK + 4 * PULL),
            bytes_accessed=4 * D_EMB * SPAN * 2 * (col_count + row_count),
            transcendentals=tiles * BLK * BLK,
        ),
        name="forces",
    )(meta, listing, neg_rows, neg_cols, weights, *row_y, *col_y)
    return outs[0], outs[1:]


def shards(inputs, rho, sigma, embed, knn_blocks, knn_seeds, neg_rows, neg_cols, neg_count):
    row_count = lax.axis_size("row")
    col_count = lax.axis_size("col")
    shifts = row_count // 2 + 1
    row, col = lax.axis_index("row"), lax.axis_index("col")
    listing = knn_blocks.reshape(-1)
    seeds = knn_seeds.reshape(-1)
    row_list, col_list = neg_rows.reshape(-1), neg_cols.reshape(-1)
    meta = jnp.stack([row, col, neg_count[0, 0]]).astype(I32)

    def from_shift(value, shift):
        pairs = [((r + shift) % row_count, r) for r in range(row_count)]
        return lax.ppermute(value, "row", pairs)

    def from_half(value):
        half = row_count // 2
        pairs = [(r + half, r) if r % 2 == 0 else (r, r + half) for r in range(half)]
        return lax.ppermute(value, "row", pairs)

    def to_shift(value, shift):
        pairs = [(r, (r + shift) % row_count) for r in range(row_count)]
        return lax.ppermute(value, "row", pairs)

    def from_bits(value, bits):
        pairs = [(c ^ bits, c) for c in range(col_count)]
        return lax.ppermute(value, "col", pairs)

    sizes = row_count, col_count
    single = [1 << place for place in range(1, (col_count - 1).bit_length())]
    early_bits = [0, 1] + [bits + core for bits in single for core in range(2)]
    late_bits = [bits for bits in range(col_count) if bits not in early_bits]
    meta = jnp.concatenate([meta, jnp.array(early_bits + late_bits, I32)])

    def after(value, *others):
        return lax.optimization_barrier((value, *others))[0]

    row_x = {0: inputs}
    for bits in single:
        row_x[bits] = from_bits(inputs, bits)
    col_x = [inputs] + [from_shift(inputs, shift) for shift in range(1, shifts - 1)]
    blocks = [inputs[block * BLK : (block + 1) * BLK] for block in range(CB)]
    first = {bits: from_bits(blocks[0], bits) for bits in late_bits if bits % 2 == 0}
    seed_row = jnp.pad(seeds.astype(F32)[None], ((0, 0), (0, SPAN - seeds.shape[0])))
    params = jnp.stack([rho, sigma, jnp.sum(inputs * inputs, axis=1)])
    blank = jnp.zeros((PACK - SEEDS - 1, SPAN), F32)
    pack = jnp.concatenate([embed, params, seed_row, blank], axis=0)
    col_packs = [pack] + [from_shift(pack, shift) for shift in range(1, shifts)]
    held, meta, listing, seeds = lax.optimization_barrier((inputs, meta, listing, seeds, *col_packs[1:]))[:4]
    row_x[1] = from_bits(held, 1)
    last = [from_half(after(blocks[0], *col_packs[1:]))]
    near = [row_x[bits] for bits in single] + col_x[1:] + list(first.values()) + last
    for bits in single:
        row_x[bits + 1] = from_bits(after(row_x[bits], *near), 1)
    last.append(from_half(after(blocks[1], *near)))
    late_x = {bits: [first[bits], from_bits(after(blocks[1], *near), bits)] for bits in first}
    late_x |= {bits + 1: [from_bits(after(first[bits], *near), 1)] for bits in first}

    own_pack = pack
    for shift in range(1, shifts):
        place = SEEDS + shift
        far_seed = col_packs[shift][SEEDS : SEEDS + 1]
        own_pack = own_pack + jnp.pad(far_seed, ((place, PACK - place - 1), (0, 0)))
    own_pack = after(own_pack, *[row_x[bits + 1] for bits in single])
    early = early_grams(sizes, meta, listing, col_x, [row_x[bits] for bits in early_bits[1:]])
    even_packs = jnp.stack([own_pack] + [from_bits(own_pack, bits) for bits in range(2, col_count, 2)])
    even_packs = after(even_packs, early[0])
    odd_packs = from_bits(even_packs, 1)
    for bits in late_bits:
        if bits % 2 == 0:
            late_x[bits + 1].append(from_bits(after(late_x[bits][1], even_packs), 1))
    held = after(embed, *[late_x[bits][1] for bits in first])
    col_y = col_packs + [from_shift(held, shift) for shift in range(shifts, row_count)]

    weights = pair_weights(
        sizes,
        meta,
        listing,
        seeds,
        early,
        last,
        [part for bits in late_bits for part in late_x[bits]],
        col_packs + [even_packs, odd_packs],
    )

    row_y = (even_packs, odd_packs)
    for step in range(STEPS):
        if step:
            row_y = (lax.all_gather(embed, "col", axis=0, tiled=False),)
            col_y = [embed] + [from_shift(embed, shift) for shift in range(1, row_count)]
        row_force, col_force = pair_forces(sizes, meta, listing, row_list, col_list, weights, row_y, col_y)
        row_parts = lax.all_to_all(row_force, "col", split_axis=0, concat_axis=0, tiled=True)
        force = jnp.sum(row_parts, axis=0) + col_force[0]
        for shift in range(1, row_count):
            force = force + to_shift(col_force[shift], shift)
        embed = embed + STEP_SIZE * force
    return (embed, force * FORCE_SCALE)


def solution(mesh):
    in_specs = (
        P(("row", "col"), None),
        P(("row", "col")),
        P(("row", "col")),
        P(None, ("row", "col")),
        P("row", "col", None, None, None),
        P("row", "col", None, None),
        P("row", "col", None),
        P("row", "col", None),
        P("row", "col"),
    )
    out_specs = (P(None, ("row", "col")), P(None, ("row", "col")))
    return jax.shard_map(shards, mesh=mesh, in_specs=in_specs, out_specs=out_specs, check_vma=False)
```

```python
import functools

import jax
import jax.numpy as jnp
from jax import lax
from jax.experimental import pallas as pl
from jax.experimental.pallas import tpu as pltpu
from jax.sharding import PartitionSpec as P

D_EMB = 64
BLK = 128
CB = 2
SPAN = CB * BLK
STEPS = 2

STEP_SIZE = 0.0005
REPULSION = 2.0
FORCE_SCALE = 0.015625

RHO, SIGMA, SQUARES, SEEDS = D_EMB, D_EMB + 1, D_EMB + 2, D_EMB + 3
PACK = 72
STACK = 4 * D_EMB
PULL = 2 * D_EMB + 16
UNROLL = 12
F32, BF16, I32 = jnp.float32, jnp.bfloat16, jnp.int32


def split(value):
    high = value.astype(BF16)
    return high, (value - high.astype(F32)).astype(BF16)


def nt_dot(left, right):
    return lax.dot_general(left, right, (((1,), (1,)), ((), ())), preferred_element_type=F32)


def nn_dot(left, right):
    return lax.dot_general(left, right, (((1,), (0,)), ((), ())), preferred_element_type=F32)


def hash_bits(salt_value, first, second):
    mixed = first * 1103515245 + salt_value
    mixed = (mixed ^ second * 747796405) * 277803737
    return (mixed >> 17 & 1).astype(F32)


def takes_shift(shift, row, row_count):
    if 2 * shift != row_count:
        return True
    half = row_count // 2
    return jnp.where(row < half, row % 2 == 0, (row - half) % 2 == 1)


def each(count, body):
    if count <= 8:
        for index in range(count):
            body(index)
    else:
        pl.loop(0, count)(body)


def pick_of(sizes, meta, listing, bits, shift):
    row_count, _ = sizes
    place = lax.bitwise_xor(meta[1], bits) * row_count + lax.rem(meta[0] + shift, row_count)
    start_i = pl.multiple_of(listing[2 * place] * BLK, BLK)
    start_j = pl.multiple_of(listing[2 * place + 1] * BLK, BLK)
    return start_i, start_j, place


def vmem_limit(sizes):
    return (8 + 2 * sizes[1]) * 2**20


def gram_of(high_j, low_j, high_i, low_i):
    return nt_dot(high_j, low_i) + nt_dot(low_j, high_i) + nt_dot(high_j, high_i)


def grams_kernel(sizes, counts, meta, listing, *rest):
    shifts_early, rows_early = counts
    row_count, _ = sizes
    columns, rows = rest[:shifts_early], rest[shifts_early : shifts_early + rows_early - 1]
    grams, high_c, low_c, high_last, low_last, high_r, low_r = rest[shifts_early + rows_early - 1 :]
    for shift in range(shifts_early):
        high_c[shift], low_c[shift] = split(columns[shift][...])
    high_r[0], low_r[0] = high_c[0], low_c[0]
    for line in range(1, rows_early):
        high_r[line], low_r[line] = split(rows[line - 1][...])

    def row_span(line):
        bits = meta[3 + line]
        for shift in range(shifts_early):
            start_i, start_j, _ = pick_of(sizes, meta, listing, bits, shift)
            span_i, span_j = pl.ds(start_i, BLK), pl.ds(start_j, BLK)
            grams[line, shift] = gram_of(
                high_c[shift, span_j, :], low_c[shift, span_j, :], high_r[line, span_i, :], low_r[line, span_i, :]
            )
        start_i, _, _ = pick_of(sizes, meta, listing, bits, shifts_early)
        high_last[line] = high_r[line, pl.ds(start_i, BLK), :]
        low_last[line] = low_r[line, pl.ds(start_i, BLK), :]

    each(rows_early, row_span)


def early_grams(sizes, meta, listing, columns, rows):
    shifts_early, rows_early, depth = len(columns), len(rows) + 1, rows[0].shape[-1]
    smem = pl.BlockSpec(memory_space=pltpu.SMEM)
    vmem = pl.BlockSpec(memory_space=pltpu.VMEM)
    tiles = shifts_early * rows_early
    return pl.pallas_call(
        functools.partial(grams_kernel, sizes, (shifts_early, rows_early)),
        in_specs=[smem] * 2 + [vmem] * (len(columns) + len(rows)),
        out_specs=[vmem] * 5,
        out_shape=[
            jax.ShapeDtypeStruct((rows_early, shifts_early, BLK, BLK), F32),
            jax.ShapeDtypeStruct((shifts_early, SPAN, depth), BF16),
            jax.ShapeDtypeStruct((shifts_early, SPAN, depth), BF16),
            jax.ShapeDtypeStruct((rows_early, BLK, depth), BF16),
            jax.ShapeDtypeStruct((rows_early, BLK, depth), BF16),
        ],
        scratch_shapes=[pltpu.VMEM((rows_early, SPAN, depth), BF16)] * 2,
        compiler_params=pltpu.CompilerParams(vmem_limit_bytes=vmem_limit(sizes)),
        cost_estimate=pl.CostEstimate(
            flops=tiles * 6 * BLK * BLK * depth,
            bytes_accessed=(shifts_early + rows_early) * SPAN * depth * 4,
            transcendentals=0,
        ),
        name="grams",
    )(meta, listing, *columns, *rows)


def weights_kernel(sizes, counts, meta, listing, seeds, grams, high_c, low_c, high_last, low_last, *rest):
    row_count, col_count = sizes
    shifts_early, rows_early = counts
    shifts, rows_late = shifts_early + 1, col_count - rows_early
    last, late, col_packs = rest[0], rest[1 : 1 + rows_late], rest[1 + rows_late :][:shifts]
    even_packs, odd_packs = rest[1 + rows_late + shifts :][:2]
    out, high_l, low_l, high_r, low_r, late_grams, col_params, row_params = rest[3 + rows_late + shifts :]
    row, col = meta[0], meta[1]

    high_l[...], low_l[...] = split(last[...])
    for shift in range(shifts):
        for block in range(CB):
            lanes = slice(block * BLK, (block + 1) * BLK)
            col_params[shift, block] = col_packs[shift][RHO : RHO + 8, lanes].T
    for bits in range(col_count):
        row_params[bits] = (even_packs, odd_packs)[bits % 2][bits // 2, RHO : RHO + 8, :]
    for line in range(rows_late):
        high_r[line], low_r[line] = split(late[line][...])

    def early_last(line):
        _, start_j, _ = pick_of(sizes, meta, listing, meta[3 + line], shifts_early)
        span_j = pl.ds(start_j, BLK)
        late_grams[shifts_early, meta[3 + line]] = gram_of(
            high_l[span_j, :], low_l[span_j, :], high_last[line], low_last[line]
        )

    each(rows_early, early_last)

    def late_row(line):
        bits = meta[3 + rows_early + line]
        for shift in range(shifts):
            start_i, start_j, _ = pick_of(sizes, meta, listing, bits, shift)
            span_i, span_j = pl.ds(start_i, BLK), pl.ds(start_j, BLK)
            if shift == shifts_early:
                high_j, low_j = high_l[span_j, :], low_l[span_j, :]
            else:
                high_j, low_j = high_c[shift, span_j, :], low_c[shift, span_j, :]
            late_grams[shift, bits] = gram_of(high_j, low_j, high_r[line, span_i, :], low_r[line, span_i, :])

    each(rows_late, late_row)

    positions_j = lax.broadcasted_iota(I32, (BLK, BLK), 0)
    positions_i = lax.broadcasted_iota(I32, (BLK, BLK), 1)
    wanted_seed = lax.broadcasted_iota(I32, (1, SPAN), 1) == col * row_count + row

    def finish(bits, shift, gram):
        start_i, start_j, place = pick_of(sizes, meta, listing, bits, shift)
        params_i = row_params[bits, :, pl.ds(start_i, BLK)]
        rho_i, sigma_i, square_i = params_i[0:1], params_i[1:2], params_i[2:3]
        params_j = col_params[shift, lax.div(start_j, BLK)]
        rho_j, sigma_j, square_j = params_j[:, 0:1], params_j[:, 1:2], params_j[:, 2:3]
        distance = jnp.sqrt(jnp.maximum(square_j + square_i - 2.0 * gram, 1.0))
        plane_seeds = row_params[bits, SEEDS - RHO + shift : SEEDS - RHO + shift + 1, :]
        seed_back = jnp.sum(jnp.where(wanted_seed, plane_seeds, 0.0), axis=1, keepdims=True).astype(I32)
        ahead = hash_bits(seeds[place], positions_i, positions_j) * jnp.exp(
            jnp.maximum(distance - rho_i, 0.0) * (-1.0 / sigma_i)
        )
        behind = hash_bits(seed_back, positions_j, positions_i) * jnp.exp(
            jnp.maximum(distance - rho_j, 0.0) * (-1.0 / sigma_j)
        )
        weights = (ahead + behind - ahead * behind).astype(BF16)
        if shift == 0:
            weights = (weights.astype(F32) * jnp.where(bits == 0, 0.5, 1.0)).astype(BF16)
        out[shift * col_count + bits] = weights

    def early_rows(line):
        bits = meta[3 + line]
        for shift in range(shifts):
            finish(bits, shift, grams[line, shift] if shift < shifts_early else late_grams[shift, bits])

    def late_rows(line):
        bits = meta[3 + rows_early + line]
        for shift in range(shifts):
            finish(bits, shift, late_grams[shift, bits])

    each(rows_early, early_rows)
    each(rows_late, late_rows)


def pair_weights(sizes, meta, listing, seeds, early, last, late, packs):
    _, col_count = sizes
    shifts, depth = len(packs) - 2, late[0].shape[-1]
    rows_late = len(late)
    smem = pl.BlockSpec(memory_space=pltpu.SMEM)
    vmem = pl.BlockSpec(memory_space=pltpu.VMEM)
    tiles = shifts * col_count
    return pl.pallas_call(
        functools.partial(weights_kernel, sizes, (shifts - 1, col_count - rows_late)),
        in_specs=[smem] * 3 + [vmem] * (5 + 1 + rows_late + len(packs)),
        out_specs=vmem,
        out_shape=jax.ShapeDtypeStruct((tiles, BLK, BLK), BF16),
        scratch_shapes=[
            pltpu.VMEM((SPAN, depth), BF16),
            pltpu.VMEM((SPAN, depth), BF16),
            pltpu.VMEM((rows_late, SPAN, depth), BF16),
            pltpu.VMEM((rows_late, SPAN, depth), BF16),
            pltpu.VMEM((shifts, col_count, BLK, BLK), F32),
            pltpu.VMEM((shifts, CB, BLK, 8), F32),
            pltpu.VMEM((col_count, 8, SPAN), F32),
        ],
        compiler_params=pltpu.CompilerParams(vmem_limit_bytes=vmem_limit(sizes)),
        cost_estimate=pl.CostEstimate(
            flops=tiles * 3 * BLK * BLK * depth,
            bytes_accessed=(1 + rows_late) * SPAN * depth * 4,
            transcendentals=tiles * 3 * BLK * BLK,
        ),
        name="weights",
    )(meta, listing, seeds, *early, last, *late, *packs)


def force_kernel(row_count, col_count, by_bits, meta, listing, neg_rows, neg_cols, weights, *rest):
    shifts = row_count // 2 + 1
    row_arrays, rest = (rest[:2], rest[2:]) if by_bits else (rest[:1], rest[1:])
    col_y = rest[:row_count]
    row_force, col_force = rest[row_count], rest[row_count + 1 : 2 * row_count + 1]
    left_gram, right_gram, left_pull, right_pull, left_acc, right_acc, held_v, held_h = rest[2 * row_count + 1 :]
    row, col, live = meta[0], meta[1], meta[2]
    iota = lax.broadcasted_iota(I32, (D_EMB, BLK), 0)
    ones = jnp.ones((16, BLK), BF16)
    blank = jnp.zeros((D_EMB, BLK), BF16)

    def norm_rows(value, first):
        norm = jnp.sum(value * value, axis=0, keepdims=True)
        high, rest_ = split(norm)
        left_over = norm - high.astype(F32) - rest_.astype(F32)
        high, middle = high.astype(F32), rest_.astype(F32)
        return jnp.where(
            iota == first,
            high,
            jnp.where(iota == first + 1, middle, jnp.where(iota == first + 2, left_over, 0.0)),
        )

    def pulls(high, low):
        top = jnp.concatenate([high, ones, low], axis=0)
        bottom = jnp.concatenate([high, ones, blank], axis=0)
        return jnp.concatenate([top, bottom], axis=1)

    def left_block(index, value):
        high, low = split(value)
        extra = norm_rows(value, 0) + jnp.where((iota >= 3) & (iota < 7), 1.0, 0.0)
        left_gram[index] = jnp.concatenate([high, low, high, extra.astype(BF16)], axis=0)
        left_pull[index] = pulls(high, low)
        left_acc[index] = jnp.zeros((PULL, BLK), F32)

    def right_block(index, value):
        high, low = split(value)
        extra = norm_rows(value, 3) + jnp.where((iota < 3) | (iota == 6), 1.0, 0.0)
        twice_high, twice_low = -2.0 * high.astype(F32), -2.0 * low.astype(F32)
        stack = jnp.concatenate([twice_high, twice_high, twice_low, extra], axis=0)
        right_gram[index] = stack.T.astype(BF16)
        right_pull[index] = pulls(high, low)
        right_acc[index] = jnp.zeros((PULL, BLK), F32)

    def row_y(pair, side, block):
        lanes = slice(block * BLK, (block + 1) * BLK)
        line = pair * 2 + side
        if by_bits:
            return row_arrays[side][pair, :D_EMB, lanes], lax.bitwise_xor(line, col)
        return row_arrays[0][line, :D_EMB, lanes], line

    @pl.loop(0, col_count // 2)
    def _(pair):
        for side in range(2):
            for block in range(CB):
                value, group = row_y(pair, side, block)
                left_block(group * CB + block, value)

    for shift in range(row_count):
        for block in range(CB):
            right_block(shift * CB + block, col_y[shift][:D_EMB, block * BLK : (block + 1) * BLK])

    def kernel_of(left, right):
        return 1.0 / nn_dot(right_gram[right], left_gram[left])

    def apply_all(tiles_):
        for lane, (left, right, coefficient) in enumerate(tiles_):
            high, low = split(coefficient())
            held_v[lane, :BLK], held_v[lane, BLK:] = high, low
            held_h[lane, :, :BLK], held_h[lane, :, BLK:] = high, low
        for lane, (left, right, _) in enumerate(tiles_):
            left_acc[left] += nn_dot(right_pull[right], held_v[lane])
        for lane, (left, right, _) in enumerate(tiles_):
            right_acc[right] += nt_dot(left_pull[left], held_h[lane])

    def near_active(group):
        offset = lax.rem(group - col + col_count, col_count)
        return (2 * offset < col_count) | ((2 * offset == col_count) & (2 * col < col_count))

    near = col_count // 2 + 1
    tiles = near + col_count * (shifts - 1)
    last = jnp.where(takes_shift(shifts - 1, row, row_count), tiles, tiles - col_count)

    @pl.loop(0, lax.div(last + UNROLL - 1, UNROLL))
    def _(step):
        batch = []
        for lane in range(UNROLL):
            index = step * UNROLL + lane
            far = jnp.maximum(index - near, 0)
            shift = jnp.where(index < near, 0, 1 + lax.div(far, col_count))
            group = jnp.where(index < near, lax.rem(col + index, col_count), lax.rem(far, col_count))
            inside = index < last
            shift = jnp.where(inside, shift, 0)
            inside &= (shift > 0) | near_active(group)
            slot = shift * col_count + lax.bitwise_xor(group, col)
            entry = (group * row_count + lax.rem(row + shift, row_count)) * 2
            left = group * CB + listing[entry]
            right = shift * CB + listing[entry + 1]

            def pull(left=left, right=right, slot=slot, inside=inside):
                return weights[slot].astype(F32) * (kernel_of(left, right) * jnp.where(inside, 1.0, 0.0))

            batch.append((left, right, pull))
        apply_all(batch)

    @pl.loop(0, lax.div(live + UNROLL - 1, UNROLL))
    def _(step):
        batch = []
        for lane in range(UNROLL):
            index = step * UNROLL + lane
            strength = jnp.where(index < live, -REPULSION, 0.0)
            place = jnp.minimum(index, live - 1)
            left = neg_rows[place]
            other = neg_cols[place]
            shift = lax.rem(lax.div(other, CB) - row + row_count, row_count)
            right = shift * CB + lax.rem(other, CB)
            def push(left=left, right=right, strength=strength):
                kernel = kernel_of(left, right)
                return strength * kernel * kernel
            batch.append((left, right, push))
        apply_all(batch)

    def force_of(acc, value):
        return acc[:D_EMB] + acc[D_EMB + 16 :] - value * acc[D_EMB : D_EMB + 1]

    @pl.loop(0, col_count // 2)
    def _(pair):
        for side in range(2):
            for block in range(CB):
                value, group = row_y(pair, side, block)
                lanes = slice(block * BLK, (block + 1) * BLK)
                row_force[group, :, lanes] = force_of(left_acc[group * CB + block], value)

    for shift in range(row_count):
        for block in range(CB):
            lanes = slice(block * BLK, (block + 1) * BLK)
            col_force[shift][:, lanes] = force_of(right_acc[shift * CB + block], col_y[shift][:D_EMB, lanes])


def pair_forces(sizes, meta, listing, neg_rows, neg_cols, weights, row_y, col_y):
    row_count, col_count = sizes
    smem = pl.BlockSpec(memory_space=pltpu.SMEM)
    vmem = pl.BlockSpec(memory_space=pltpu.VMEM)
    lefts, rights = col_count * CB, row_count * CB
    tiles = col_count * 2 + 48
    outs = pl.pallas_call(
        functools.partial(force_kernel, row_count, col_count, len(row_y) > 1),
        in_specs=[smem] * 4 + [vmem] * (1 + len(row_y) + row_count),
        out_specs=[vmem] * (1 + row_count),
        out_shape=[jax.ShapeDtypeStruct((col_count, D_EMB, SPAN), F32)]
        + [jax.ShapeDtypeStruct((D_EMB, SPAN), F32)] * row_count,
        scratch_shapes=[
            pltpu.VMEM((lefts, STACK, BLK), BF16),
            pltpu.VMEM((rights, BLK, STACK), BF16),
            pltpu.VMEM((lefts, PULL, 2 * BLK), BF16),
            pltpu.VMEM((rights, PULL, 2 * BLK), BF16),
            pltpu.VMEM((lefts, PULL, BLK), F32),
            pltpu.VMEM((rights, PULL, BLK), F32),
            pltpu.VMEM((UNROLL, 2 * BLK, BLK), BF16),
            pltpu.VMEM((UNROLL, BLK, 2 * BLK), BF16),
        ],
        compiler_params=pltpu.CompilerParams(vmem_limit_bytes=vmem_limit(sizes)),
        cost_estimate=pl.CostEstimate(
            flops=tiles * 2 * BLK * BLK * (STACK + 4 * PULL),
            bytes_accessed=4 * D_EMB * SPAN * 2 * (col_count + row_count),
            transcendentals=tiles * BLK * BLK,
        ),
        name="forces",
    )(meta, listing, neg_rows, neg_cols, weights, *row_y, *col_y)
    return outs[0], outs[1:]


def shards(inputs, rho, sigma, embed, knn_blocks, knn_seeds, neg_rows, neg_cols, neg_count):
    row_count = lax.axis_size("row")
    col_count = lax.axis_size("col")
    shifts = row_count // 2 + 1
    row, col = lax.axis_index("row"), lax.axis_index("col")
    listing = knn_blocks.reshape(-1)
    seeds = knn_seeds.reshape(-1)
    row_list, col_list = neg_rows.reshape(-1), neg_cols.reshape(-1)
    meta = jnp.stack([row, col, neg_count[0, 0]]).astype(I32)

    def from_shift(value, shift):
        pairs = [((r + shift) % row_count, r) for r in range(row_count)]
        return lax.ppermute(value, "row", pairs)

    def from_half(value):
        half = row_count // 2
        pairs = [(r + half, r) if r % 2 == 0 else (r, r + half) for r in range(half)]
        return lax.ppermute(value, "row", pairs)

    def to_shift(value, shift):
        pairs = [(r, (r + shift) % row_count) for r in range(row_count)]
        return lax.ppermute(value, "row", pairs)

    def from_bits(value, bits):
        pairs = [(c ^ bits, c) for c in range(col_count)]
        return lax.ppermute(value, "col", pairs)

    sizes = row_count, col_count
    single = [1 << place for place in range(1, (col_count - 1).bit_length())]
    early_bits = [0, 1] + [bits + core for bits in single for core in range(2)]
    late_bits = [bits for bits in range(col_count) if bits not in early_bits]
    meta = jnp.concatenate([meta, jnp.array(early_bits + late_bits, I32)])

    def after(value, *others):
        return lax.optimization_barrier((value, *others))[0]

    row_x = {0: inputs}
    for bits in single:
        row_x[bits] = from_bits(inputs, bits)
    col_x = [inputs] + [from_shift(inputs, shift) for shift in range(1, shifts - 1)]
    near = [row_x[bits] for bits in single] + col_x[1:]
    for bits in late_bits:
        if bits % 2 == 0:
            row_x[bits] = from_bits(inputs, bits)
    seed_row = jnp.pad(seeds.astype(F32)[None], ((0, 0), (0, SPAN - seeds.shape[0])))
    params = jnp.stack([rho, sigma, jnp.sum(inputs * inputs, axis=1)])
    blank = jnp.zeros((PACK - SEEDS - 1, SPAN), F32)
    pack = jnp.concatenate([embed, params, seed_row, blank], axis=0)
    col_packs = [pack] + [from_shift(pack, shift) for shift in range(1, shifts)]
    far_y = [from_shift(embed, shift) for shift in range(shifts, row_count)]
    held, meta, listing, seeds = lax.optimization_barrier((inputs, meta, listing, seeds, *col_packs[1:], *far_y))[:4]
    row_x[1] = from_bits(held, 1)
    for bits in single:
        row_x[bits + 1] = from_bits(after(row_x[bits], *near), 1)
    col_x.append(from_half(after(inputs, *col_packs[1:], *far_y)))

    own_pack = pack
    for shift in range(1, shifts):
        place = SEEDS + shift
        far_seed = col_packs[shift][SEEDS : SEEDS + 1]
        own_pack = own_pack + jnp.pad(far_seed, ((place, PACK - place - 1), (0, 0)))
    own_pack = after(own_pack, *[row_x[bits + 1] for bits in single])
    early = early_grams(sizes, meta, listing, col_x[:-1], [row_x[bits] for bits in early_bits[1:]])
    even_packs = jnp.stack([own_pack] + [from_bits(own_pack, bits) for bits in range(2, col_count, 2)])
    even_packs = after(even_packs, early[0])
    odd_packs = from_bits(even_packs, 1)
    for bits in late_bits:
        if bits % 2 == 0:
            row_x[bits + 1] = from_bits(after(row_x[bits], even_packs), 1)
    col_y = col_packs + far_y

    weights = pair_weights(
        sizes,
        meta,
        listing,
        seeds,
        early,
        col_x[-1],
        [row_x[bits] for bits in late_bits],
        col_packs + [even_packs, odd_packs],
    )

    row_y = (even_packs, odd_packs)
    for step in range(STEPS):
        if step:
            row_y = (lax.all_gather(embed, "col", axis=0, tiled=False),)
            col_y = [embed] + [from_shift(embed, shift) for shift in range(1, row_count)]
        row_force, col_force = pair_forces(sizes, meta, listing, row_list, col_list, weights, row_y, col_y)
        row_parts = lax.all_to_all(row_force, "col", split_axis=0, concat_axis=0, tiled=True)
        force = jnp.sum(row_parts, axis=0) + col_force[0]
        for shift in range(1, row_count):
            force = force + to_shift(col_force[shift], shift)
        embed = embed + STEP_SIZE * force
    return (embed, force * FORCE_SCALE)


def solution(mesh):
    in_specs = (
        P(("row", "col"), None),
        P(("row", "col")),
        P(("row", "col")),
        P(None, ("row", "col")),
        P("row", "col", None, None, None),
        P("row", "col", None, None),
        P("row", "col", None),
        P("row", "col", None),
        P("row", "col"),
    )
    out_specs = (P(None, ("row", "col")), P(None, ("row", "col")))
    return jax.shard_map(shards, mesh=mesh, in_specs=in_specs, out_specs=out_specs, check_vma=False)
```

```python
import functools

import jax
import jax.numpy as jnp
from jax import lax
from jax.experimental import pallas as pl
from jax.experimental.pallas import tpu as pltpu
from jax.sharding import PartitionSpec as P

D_EMB = 64
BLK = 128
CB = 2
SPAN = CB * BLK
STEPS = 2

STEP_SIZE = 0.0005
REPULSION = 2.0
FORCE_SCALE = 0.015625

RHO, SIGMA, SQUARES, SEEDS = D_EMB, D_EMB + 1, D_EMB + 2, D_EMB + 3
PACK = 72
STACK = 4 * D_EMB
PULL = 2 * D_EMB + 16
UNROLL = 12
F32, BF16, I32 = jnp.float32, jnp.bfloat16, jnp.int32


def split(value):
    high = value.astype(BF16)
    return high, (value - high.astype(F32)).astype(BF16)


def nt_dot(left, right):
    return lax.dot_general(left, right, (((1,), (1,)), ((), ())), preferred_element_type=F32)


def nn_dot(left, right):
    return lax.dot_general(left, right, (((1,), (0,)), ((), ())), preferred_element_type=F32)


def hash_bits(salt_value, first, second):
    mixed = first * 1103515245 + salt_value
    mixed = (mixed ^ second * 747796405) * 277803737
    return (mixed >> 17 & 1).astype(F32)


def takes_shift(shift, row, row_count):
    if 2 * shift != row_count:
        return True
    half = row_count // 2
    return jnp.where(row < half, row % 2 == 0, (row - half) % 2 == 1)


def each(count, body):
    if count <= 8:
        for index in range(count):
            body(index)
    else:
        pl.loop(0, count)(body)


def pick_of(sizes, meta, listing, bits, shift):
    row_count, _ = sizes
    place = lax.bitwise_xor(meta[1], bits) * row_count + lax.rem(meta[0] + shift, row_count)
    start_i = pl.multiple_of(listing[2 * place] * BLK, BLK)
    start_j = pl.multiple_of(listing[2 * place + 1] * BLK, BLK)
    return start_i, start_j, place


def vmem_limit(sizes):
    return (8 + 2 * sizes[1]) * 2**20


def gram_of(high_j, low_j, high_i, low_i):
    return nt_dot(high_j, low_i) + nt_dot(low_j, high_i) + nt_dot(high_j, high_i)


def grams_kernel(sizes, counts, meta, listing, *rest):
    shifts_early, rows_early = counts
    row_count, _ = sizes
    columns, rows = rest[:shifts_early], rest[shifts_early : shifts_early + rows_early - 1]
    grams, high_c, low_c, high_last, low_last, high_r, low_r = rest[shifts_early + rows_early - 1 :]
    for shift in range(shifts_early):
        high_c[shift], low_c[shift] = split(columns[shift][...])
    high_r[0], low_r[0] = high_c[0], low_c[0]
    for line in range(1, rows_early):
        high_r[line], low_r[line] = split(rows[line - 1][...])

    def row_span(line):
        bits = meta[3 + line]
        for shift in range(shifts_early):
            start_i, start_j, _ = pick_of(sizes, meta, listing, bits, shift)
            span_i, span_j = pl.ds(start_i, BLK), pl.ds(start_j, BLK)
            grams[line, shift] = gram_of(
                high_c[shift, span_j, :], low_c[shift, span_j, :], high_r[line, span_i, :], low_r[line, span_i, :]
            )
        start_i, _, _ = pick_of(sizes, meta, listing, bits, shifts_early)
        high_last[line] = high_r[line, pl.ds(start_i, BLK), :]
        low_last[line] = low_r[line, pl.ds(start_i, BLK), :]

    each(rows_early, row_span)


def early_grams(sizes, meta, listing, columns, rows):
    shifts_early, rows_early, depth = len(columns), len(rows) + 1, rows[0].shape[-1]
    smem = pl.BlockSpec(memory_space=pltpu.SMEM)
    vmem = pl.BlockSpec(memory_space=pltpu.VMEM)
    tiles = shifts_early * rows_early
    return pl.pallas_call(
        functools.partial(grams_kernel, sizes, (shifts_early, rows_early)),
        in_specs=[smem] * 2 + [vmem] * (len(columns) + len(rows)),
        out_specs=[vmem] * 5,
        out_shape=[
            jax.ShapeDtypeStruct((rows_early, shifts_early, BLK, BLK), F32),
            jax.ShapeDtypeStruct((shifts_early, SPAN, depth), BF16),
            jax.ShapeDtypeStruct((shifts_early, SPAN, depth), BF16),
            jax.ShapeDtypeStruct((rows_early, BLK, depth), BF16),
            jax.ShapeDtypeStruct((rows_early, BLK, depth), BF16),
        ],
        scratch_shapes=[pltpu.VMEM((rows_early, SPAN, depth), BF16)] * 2,
        compiler_params=pltpu.CompilerParams(vmem_limit_bytes=vmem_limit(sizes)),
        cost_estimate=pl.CostEstimate(
            flops=tiles * 6 * BLK * BLK * depth,
            bytes_accessed=(shifts_early + rows_early) * SPAN * depth * 4,
            transcendentals=0,
        ),
        name="grams",
    )(meta, listing, *columns, *rows)


def weights_kernel(sizes, counts, meta, listing, seeds, grams, high_c, low_c, high_last, low_last, *rest):
    row_count, col_count = sizes
    shifts_early, rows_early = counts
    shifts, rows_late = shifts_early + 1, col_count - rows_early
    spans = CB * (1 + rows_late)
    last, late, col_packs = rest[:CB], rest[CB:spans], rest[spans : spans + shifts]
    even_packs, odd_packs = rest[spans + shifts :][:2]
    out, high_l, low_l, high_r, low_r, late_grams, col_params, row_params = rest[spans + shifts + 2 :]
    row, col = meta[0], meta[1]

    for block in range(CB):
        high_l[block * BLK : (block + 1) * BLK], low_l[block * BLK : (block + 1) * BLK] = split(last[block][...])
    for shift in range(shifts):
        for block in range(CB):
            lanes = slice(block * BLK, (block + 1) * BLK)
            col_params[shift, block] = col_packs[shift][RHO : RHO + 8, lanes].T
    for bits in range(col_count):
        row_params[bits] = (even_packs, odd_packs)[bits % 2][bits // 2, RHO : RHO + 8, :]
    for line in range(rows_late):
        for block in range(CB):
            part = slice(block * BLK, (block + 1) * BLK)
            high_r[line, part], low_r[line, part] = split(late[CB * line + block][...])

    def early_last(line):
        _, start_j, _ = pick_of(sizes, meta, listing, meta[3 + line], shifts_early)
        span_j = pl.ds(start_j, BLK)
        late_grams[shifts_early, meta[3 + line]] = gram_of(
            high_l[span_j, :], low_l[span_j, :], high_last[line], low_last[line]
        )

    each(rows_early, early_last)

    def late_row(line):
        bits = meta[3 + rows_early + line]
        for shift in range(shifts):
            start_i, start_j, _ = pick_of(sizes, meta, listing, bits, shift)
            span_i, span_j = pl.ds(start_i, BLK), pl.ds(start_j, BLK)
            if shift == shifts_early:
                high_j, low_j = high_l[span_j, :], low_l[span_j, :]
            else:
                high_j, low_j = high_c[shift, span_j, :], low_c[shift, span_j, :]
            late_grams[shift, bits] = gram_of(high_j, low_j, high_r[line, span_i, :], low_r[line, span_i, :])

    each(rows_late, late_row)

    positions_j = lax.broadcasted_iota(I32, (BLK, BLK), 0)
    positions_i = lax.broadcasted_iota(I32, (BLK, BLK), 1)
    wanted_seed = lax.broadcasted_iota(I32, (1, SPAN), 1) == col * row_count + row

    def finish(bits, shift, gram):
        start_i, start_j, place = pick_of(sizes, meta, listing, bits, shift)
        params_i = row_params[bits, :, pl.ds(start_i, BLK)]
        rho_i, sigma_i, square_i = params_i[0:1], params_i[1:2], params_i[2:3]
        params_j = col_params[shift, lax.div(start_j, BLK)]
        rho_j, sigma_j, square_j = params_j[:, 0:1], params_j[:, 1:2], params_j[:, 2:3]
        distance = jnp.sqrt(jnp.maximum(square_j + square_i - 2.0 * gram, 1.0))
        plane_seeds = row_params[bits, SEEDS - RHO + shift : SEEDS - RHO + shift + 1, :]
        seed_back = jnp.sum(jnp.where(wanted_seed, plane_seeds, 0.0), axis=1, keepdims=True).astype(I32)
        ahead = hash_bits(seeds[place], positions_i, positions_j) * jnp.exp(
            jnp.maximum(distance - rho_i, 0.0) * (-1.0 / sigma_i)
        )
        behind = hash_bits(seed_back, positions_j, positions_i) * jnp.exp(
            jnp.maximum(distance - rho_j, 0.0) * (-1.0 / sigma_j)
        )
        weights = (ahead + behind - ahead * behind).astype(BF16)
        if shift == 0:
            weights = (weights.astype(F32) * jnp.where(bits == 0, 0.5, 1.0)).astype(BF16)
        out[shift * col_count + bits] = weights

    def early_rows(line):
        bits = meta[3 + line]
        for shift in range(shifts):
            finish(bits, shift, grams[line, shift] if shift < shifts_early else late_grams[shift, bits])

    def late_rows(line):
        bits = meta[3 + rows_early + line]
        for shift in range(shifts):
            finish(bits, shift, late_grams[shift, bits])

    each(rows_early, early_rows)
    each(rows_late, late_rows)


def pair_weights(sizes, meta, listing, seeds, early, last, late, packs):
    _, col_count = sizes
    shifts, depth = len(packs) - 2, late[0].shape[-1]
    rows_late = len(late) // CB
    smem = pl.BlockSpec(memory_space=pltpu.SMEM)
    vmem = pl.BlockSpec(memory_space=pltpu.VMEM)
    tiles = shifts * col_count
    return pl.pallas_call(
        functools.partial(weights_kernel, sizes, (shifts - 1, col_count - rows_late)),
        in_specs=[smem] * 3 + [vmem] * (5 + len(last) + len(late) + len(packs)),
        out_specs=vmem,
        out_shape=jax.ShapeDtypeStruct((tiles, BLK, BLK), BF16),
        scratch_shapes=[
            pltpu.VMEM((SPAN, depth), BF16),
            pltpu.VMEM((SPAN, depth), BF16),
            pltpu.VMEM((rows_late, SPAN, depth), BF16),
            pltpu.VMEM((rows_late, SPAN, depth), BF16),
            pltpu.VMEM((shifts, col_count, BLK, BLK), F32),
            pltpu.VMEM((shifts, CB, BLK, 8), F32),
            pltpu.VMEM((col_count, 8, SPAN), F32),
        ],
        compiler_params=pltpu.CompilerParams(vmem_limit_bytes=vmem_limit(sizes)),
        cost_estimate=pl.CostEstimate(
            flops=tiles * 3 * BLK * BLK * depth,
            bytes_accessed=(1 + rows_late) * SPAN * depth * 4,
            transcendentals=tiles * 3 * BLK * BLK,
        ),
        name="weights",
    )(meta, listing, seeds, *early, *last, *late, *packs)


def force_kernel(row_count, col_count, by_bits, meta, listing, neg_rows, neg_cols, weights, *rest):
    shifts = row_count // 2 + 1
    row_arrays, rest = (rest[:2], rest[2:]) if by_bits else (rest[:1], rest[1:])
    col_y = rest[:row_count]
    row_force, col_force = rest[row_count], rest[row_count + 1 : 2 * row_count + 1]
    left_gram, right_gram, left_pull, right_pull, left_acc, right_acc, held_v, held_h = rest[2 * row_count + 1 :]
    row, col, live = meta[0], meta[1], meta[2]
    iota = lax.broadcasted_iota(I32, (D_EMB, BLK), 0)
    ones = jnp.ones((16, BLK), BF16)
    blank = jnp.zeros((D_EMB, BLK), BF16)

    def norm_rows(value, first):
        norm = jnp.sum(value * value, axis=0, keepdims=True)
        high, rest_ = split(norm)
        left_over = norm - high.astype(F32) - rest_.astype(F32)
        high, middle = high.astype(F32), rest_.astype(F32)
        return jnp.where(
            iota == first,
            high,
            jnp.where(iota == first + 1, middle, jnp.where(iota == first + 2, left_over, 0.0)),
        )

    def pulls(high, low):
        top = jnp.concatenate([high, ones, low], axis=0)
        bottom = jnp.concatenate([high, ones, blank], axis=0)
        return jnp.concatenate([top, bottom], axis=1)

    def left_block(index, value):
        high, low = split(value)
        extra = norm_rows(value, 0) + jnp.where((iota >= 3) & (iota < 7), 1.0, 0.0)
        left_gram[index] = jnp.concatenate([high, low, high, extra.astype(BF16)], axis=0)
        left_pull[index] = pulls(high, low)
        left_acc[index] = jnp.zeros((PULL, BLK), F32)

    def right_block(index, value):
        high, low = split(value)
        extra = norm_rows(value, 3) + jnp.where((iota < 3) | (iota == 6), 1.0, 0.0)
        twice_high, twice_low = -2.0 * high.astype(F32), -2.0 * low.astype(F32)
        stack = jnp.concatenate([twice_high, twice_high, twice_low, extra], axis=0)
        right_gram[index] = stack.T.astype(BF16)
        right_pull[index] = pulls(high, low)
        right_acc[index] = jnp.zeros((PULL, BLK), F32)

    def row_y(pair, side, block):
        lanes = slice(block * BLK, (block + 1) * BLK)
        line = pair * 2 + side
        if by_bits:
            return row_arrays[side][pair, :D_EMB, lanes], lax.bitwise_xor(line, col)
        return row_arrays[0][line, :D_EMB, lanes], line

    @pl.loop(0, col_count // 2)
    def _(pair):
        for side in range(2):
            for block in range(CB):
                value, group = row_y(pair, side, block)
                left_block(group * CB + block, value)

    for shift in range(row_count):
        for block in range(CB):
            right_block(shift * CB + block, col_y[shift][:D_EMB, block * BLK : (block + 1) * BLK])

    def kernel_of(left, right):
        return 1.0 / nn_dot(right_gram[right], left_gram[left])

    def apply_all(tiles_):
        for lane, (left, right, coefficient) in enumerate(tiles_):
            high, low = split(coefficient())
            held_v[lane, :BLK], held_v[lane, BLK:] = high, low
            held_h[lane, :, :BLK], held_h[lane, :, BLK:] = high, low
        for lane, (left, right, _) in enumerate(tiles_):
            left_acc[left] += nn_dot(right_pull[right], held_v[lane])
        for lane, (left, right, _) in enumerate(tiles_):
            right_acc[right] += nt_dot(left_pull[left], held_h[lane])

    def near_active(group):
        offset = lax.rem(group - col + col_count, col_count)
        return (2 * offset < col_count) | ((2 * offset == col_count) & (2 * col < col_count))

    near = col_count // 2 + 1
    tiles = near + col_count * (shifts - 1)
    last = jnp.where(takes_shift(shifts - 1, row, row_count), tiles, tiles - col_count)

    @pl.loop(0, lax.div(last + UNROLL - 1, UNROLL))
    def _(step):
        batch = []
        for lane in range(UNROLL):
            index = step * UNROLL + lane
            far = jnp.maximum(index - near, 0)
            shift = jnp.where(index < near, 0, 1 + lax.div(far, col_count))
            group = jnp.where(index < near, lax.rem(col + index, col_count), lax.rem(far, col_count))
            inside = index < last
            shift = jnp.where(inside, shift, 0)
            inside &= (shift > 0) | near_active(group)
            slot = shift * col_count + lax.bitwise_xor(group, col)
            entry = (group * row_count + lax.rem(row + shift, row_count)) * 2
            left = group * CB + listing[entry]
            right = shift * CB + listing[entry + 1]

            def pull(left=left, right=right, slot=slot, inside=inside):
                return weights[slot].astype(F32) * (kernel_of(left, right) * jnp.where(inside, 1.0, 0.0))

            batch.append((left, right, pull))
        apply_all(batch)

    @pl.loop(0, lax.div(live + UNROLL - 1, UNROLL))
    def _(step):
        batch = []
        for lane in range(UNROLL):
            index = step * UNROLL + lane
            strength = jnp.where(index < live, -REPULSION, 0.0)
            place = jnp.minimum(index, live - 1)
            left = neg_rows[place]
            other = neg_cols[place]
            shift = lax.rem(lax.div(other, CB) - row + row_count, row_count)
            right = shift * CB + lax.rem(other, CB)
            def push(left=left, right=right, strength=strength):
                kernel = kernel_of(left, right)
                return strength * kernel * kernel
            batch.append((left, right, push))
        apply_all(batch)

    def force_of(acc, value):
        return acc[:D_EMB] + acc[D_EMB + 16 :] - value * acc[D_EMB : D_EMB + 1]

    @pl.loop(0, col_count // 2)
    def _(pair):
        for side in range(2):
            for block in range(CB):
                value, group = row_y(pair, side, block)
                lanes = slice(block * BLK, (block + 1) * BLK)
                row_force[group, :, lanes] = force_of(left_acc[group * CB + block], value)

    for shift in range(row_count):
        for block in range(CB):
            lanes = slice(block * BLK, (block + 1) * BLK)
            col_force[shift][:, lanes] = force_of(right_acc[shift * CB + block], col_y[shift][:D_EMB, lanes])


def pair_forces(sizes, meta, listing, neg_rows, neg_cols, weights, row_y, col_y):
    row_count, col_count = sizes
    smem = pl.BlockSpec(memory_space=pltpu.SMEM)
    vmem = pl.BlockSpec(memory_space=pltpu.VMEM)
    lefts, rights = col_count * CB, row_count * CB
    tiles = col_count * 2 + 48
    outs = pl.pallas_call(
        functools.partial(force_kernel, row_count, col_count, len(row_y) > 1),
        in_specs=[smem] * 4 + [vmem] * (1 + len(row_y) + row_count),
        out_specs=[vmem] * (1 + row_count),
        out_shape=[jax.ShapeDtypeStruct((col_count, D_EMB, SPAN), F32)]
        + [jax.ShapeDtypeStruct((D_EMB, SPAN), F32)] * row_count,
        scratch_shapes=[
            pltpu.VMEM((lefts, STACK, BLK), BF16),
            pltpu.VMEM((rights, BLK, STACK), BF16),
            pltpu.VMEM((lefts, PULL, 2 * BLK), BF16),
            pltpu.VMEM((rights, PULL, 2 * BLK), BF16),
            pltpu.VMEM((lefts, PULL, BLK), F32),
            pltpu.VMEM((rights, PULL, BLK), F32),
            pltpu.VMEM((UNROLL, 2 * BLK, BLK), BF16),
            pltpu.VMEM((UNROLL, BLK, 2 * BLK), BF16),
        ],
        compiler_params=pltpu.CompilerParams(vmem_limit_bytes=vmem_limit(sizes)),
        cost_estimate=pl.CostEstimate(
            flops=tiles * 2 * BLK * BLK * (STACK + 4 * PULL),
            bytes_accessed=4 * D_EMB * SPAN * 2 * (col_count + row_count),
            transcendentals=tiles * BLK * BLK,
        ),
        name="forces",
    )(meta, listing, neg_rows, neg_cols, weights, *row_y, *col_y)
    return outs[0], outs[1:]


def shards(inputs, rho, sigma, embed, knn_blocks, knn_seeds, neg_rows, neg_cols, neg_count):
    row_count = lax.axis_size("row")
    col_count = lax.axis_size("col")
    shifts = row_count // 2 + 1
    row, col = lax.axis_index("row"), lax.axis_index("col")
    listing = knn_blocks.reshape(-1)
    seeds = knn_seeds.reshape(-1)
    row_list, col_list = neg_rows.reshape(-1), neg_cols.reshape(-1)
    meta = jnp.stack([row, col, neg_count[0, 0]]).astype(I32)

    def from_shift(value, shift):
        pairs = [((r + shift) % row_count, r) for r in range(row_count)]
        return lax.ppermute(value, "row", pairs)

    def from_half(value):
        half = row_count // 2
        pairs = [(r + half, r) if r % 2 == 0 else (r, r + half) for r in range(half)]
        return lax.ppermute(value, "row", pairs)

    def to_shift(value, shift):
        pairs = [(r, (r + shift) % row_count) for r in range(row_count)]
        return lax.ppermute(value, "row", pairs)

    def from_bits(value, bits):
        pairs = [(c ^ bits, c) for c in range(col_count)]
        return lax.ppermute(value, "col", pairs)

    sizes = row_count, col_count
    single = [1 << place for place in range(1, (col_count - 1).bit_length())]
    early_bits = [0, 1] + [bits + core for bits in single for core in range(2)]
    late_bits = [bits for bits in range(col_count) if bits not in early_bits]
    meta = jnp.concatenate([meta, jnp.array(early_bits + late_bits, I32)])

    def after(value, *others):
        return lax.optimization_barrier((value, *others))[0]

    row_x = {0: inputs}
    for bits in single:
        row_x[bits] = from_bits(inputs, bits)
    col_x = [inputs] + [from_shift(inputs, shift) for shift in range(1, shifts - 1)]
    row_x[1] = from_bits(inputs, 1)
    blocks = [inputs[block * BLK : (block + 1) * BLK] for block in range(CB)]
    first = {bits: from_bits(blocks[0], bits) for bits in late_bits if bits % 2 == 0}
    seed_row = jnp.pad(seeds.astype(F32)[None], ((0, 0), (0, SPAN - seeds.shape[0])))
    params = jnp.stack([rho, sigma, jnp.sum(inputs * inputs, axis=1)])
    blank = jnp.zeros((PACK - SEEDS - 1, SPAN), F32)
    pack = jnp.concatenate([embed, params, seed_row, blank], axis=0)
    held_pack, held_y = lax.optimization_barrier((pack, embed, *[row_x[bits] for bits in single]))[:2]
    col_packs = [pack] + [from_shift(held_pack, shift) for shift in range(1, shifts)]
    far_y = [from_shift(held_y, shift) for shift in range(shifts, row_count)]
    last = [from_half(blocks[0])]
    near = [row_x[bits] for bits in single] + col_x[1:] + list(first.values()) + last
    near += col_packs[1:] + far_y
    meta, listing, seeds, *near = lax.optimization_barrier((meta, listing, seeds, *near))
    for bits in single:
        row_x[bits + 1] = from_bits(after(row_x[bits], *near), 1)
    last.append(from_half(after(blocks[1], last[0])))
    late_x = {bits: [first[bits], from_bits(after(blocks[1], first[bits]), bits)] for bits in first}
    late_x |= {bits + 1: [from_bits(after(first[bits], *near), 1)] for bits in first}

    own_pack = pack
    for shift in range(1, shifts):
        place = SEEDS + shift
        far_seed = col_packs[shift][SEEDS : SEEDS + 1]
        own_pack = own_pack + jnp.pad(far_seed, ((place, PACK - place - 1), (0, 0)))
    own_pack = after(own_pack, *[row_x[bits + 1] for bits in single])
    early = early_grams(sizes, meta, listing, col_x, [row_x[bits] for bits in early_bits[1:]])
    even_packs = jnp.stack([own_pack] + [from_bits(own_pack, bits) for bits in range(2, col_count, 2)])
    even_packs = after(even_packs, early[0])
    odd_packs = from_bits(even_packs, 1)
    for bits in late_bits:
        if bits % 2 == 0:
            late_x[bits + 1].append(from_bits(after(late_x[bits][1], even_packs), 1))
    col_y = col_packs + far_y

    weights = pair_weights(
        sizes,
        meta,
        listing,
        seeds,
        early,
        last,
        [part for bits in late_bits for part in late_x[bits]],
        col_packs + [even_packs, odd_packs],
    )

    row_y = (even_packs, odd_packs)
    for step in range(STEPS):
        if step:
            row_y = (lax.all_gather(embed, "col", axis=0, tiled=False),)
            col_y = [embed] + [from_shift(embed, shift) for shift in range(1, row_count)]
        row_force, col_force = pair_forces(sizes, meta, listing, row_list, col_list, weights, row_y, col_y)
        row_parts = lax.all_to_all(row_force, "col", split_axis=0, concat_axis=0, tiled=True)
        force = jnp.sum(row_parts, axis=0) + col_force[0]
        for shift in range(1, row_count):
            force = force + to_shift(col_force[shift], shift)
        embed = embed + STEP_SIZE * force
    return (embed, force * FORCE_SCALE)


def solution(mesh):
    in_specs = (
        P(("row", "col"), None),
        P(("row", "col")),
        P(("row", "col")),
        P(None, ("row", "col")),
        P("row", "col", None, None, None),
        P("row", "col", None, None),
        P("row", "col", None),
        P("row", "col", None),
        P("row", "col"),
    )
    out_specs = (P(None, ("row", "col")), P(None, ("row", "col")))
    return jax.shard_map(shards, mesh=mesh, in_specs=in_specs, out_specs=out_specs, check_vma=False)
```

```python
import functools

import jax
import jax.numpy as jnp
from jax import lax
from jax.experimental import pallas as pl
from jax.experimental.pallas import tpu as pltpu
from jax.sharding import PartitionSpec as P

D_EMB = 64
BLK = 128
CB = 2
SPAN = CB * BLK
STEPS = 2

STEP_SIZE = 0.0005
REPULSION = 2.0
FORCE_SCALE = 0.015625

RHO, SIGMA, SQUARES, SEEDS = D_EMB, D_EMB + 1, D_EMB + 2, D_EMB + 3
PACK = 72
STACK = 4 * D_EMB
PULL = 2 * D_EMB + 16
UNROLL = 12
F32, BF16, I32 = jnp.float32, jnp.bfloat16, jnp.int32


def split(value):
    high = value.astype(BF16)
    return high, (value - high.astype(F32)).astype(BF16)


def nt_dot(left, right):
    return lax.dot_general(left, right, (((1,), (1,)), ((), ())), preferred_element_type=F32)


def nn_dot(left, right):
    return lax.dot_general(left, right, (((1,), (0,)), ((), ())), preferred_element_type=F32)


def hash_bits(salt_value, first, second):
    mixed = first * 1103515245 + salt_value
    mixed = (mixed ^ second * 747796405) * 277803737
    return (mixed >> 17 & 1).astype(F32)


def takes_shift(shift, row, row_count):
    if 2 * shift != row_count:
        return True
    half = row_count // 2
    return jnp.where(row < half, row % 2 == 0, (row - half) % 2 == 1)


def each(count, body):
    if count <= 8:
        for index in range(count):
            body(index)
    else:
        pl.loop(0, count)(body)


def pick_of(sizes, meta, listing, bits, shift):
    row_count, _ = sizes
    place = lax.bitwise_xor(meta[1], bits) * row_count + lax.rem(meta[0] + shift, row_count)
    start_i = pl.multiple_of(listing[2 * place] * BLK, BLK)
    start_j = pl.multiple_of(listing[2 * place + 1] * BLK, BLK)
    return start_i, start_j, place


def vmem_limit(sizes):
    return (8 + 2 * sizes[1]) * 2**20


def gram_of(high_j, low_j, high_i, low_i):
    return nt_dot(high_j, low_i) + nt_dot(low_j, high_i) + nt_dot(high_j, high_i)


def grams_kernel(sizes, counts, meta, listing, *rest):
    shifts_early, rows_early = counts
    row_count, _ = sizes
    columns, rows = rest[:shifts_early], rest[shifts_early : shifts_early + rows_early - 1]
    grams, high_c, low_c, high_last, low_last, high_r, low_r = rest[shifts_early + rows_early - 1 :]
    for shift in range(shifts_early):
        high_c[shift], low_c[shift] = split(columns[shift][...])
    high_r[0], low_r[0] = high_c[0], low_c[0]
    for line in range(1, rows_early):
        high_r[line], low_r[line] = split(rows[line - 1][...])

    def row_span(line):
        bits = meta[3 + line]
        for shift in range(shifts_early):
            start_i, start_j, _ = pick_of(sizes, meta, listing, bits, shift)
            span_i, span_j = pl.ds(start_i, BLK), pl.ds(start_j, BLK)
            grams[line, shift] = gram_of(
                high_c[shift, span_j, :], low_c[shift, span_j, :], high_r[line, span_i, :], low_r[line, span_i, :]
            )
        start_i, _, _ = pick_of(sizes, meta, listing, bits, shifts_early)
        high_last[line] = high_r[line, pl.ds(start_i, BLK), :]
        low_last[line] = low_r[line, pl.ds(start_i, BLK), :]

    each(rows_early, row_span)


def early_grams(sizes, meta, listing, columns, rows):
    shifts_early, rows_early, depth = len(columns), len(rows) + 1, rows[0].shape[-1]
    smem = pl.BlockSpec(memory_space=pltpu.SMEM)
    vmem = pl.BlockSpec(memory_space=pltpu.VMEM)
    tiles = shifts_early * rows_early
    return pl.pallas_call(
        functools.partial(grams_kernel, sizes, (shifts_early, rows_early)),
        in_specs=[smem] * 2 + [vmem] * (len(columns) + len(rows)),
        out_specs=[vmem] * 5,
        out_shape=[
            jax.ShapeDtypeStruct((rows_early, shifts_early, BLK, BLK), F32),
            jax.ShapeDtypeStruct((shifts_early, SPAN, depth), BF16),
            jax.ShapeDtypeStruct((shifts_early, SPAN, depth), BF16),
            jax.ShapeDtypeStruct((rows_early, BLK, depth), BF16),
            jax.ShapeDtypeStruct((rows_early, BLK, depth), BF16),
        ],
        scratch_shapes=[pltpu.VMEM((rows_early, SPAN, depth), BF16)] * 2,
        compiler_params=pltpu.CompilerParams(vmem_limit_bytes=vmem_limit(sizes)),
        cost_estimate=pl.CostEstimate(
            flops=tiles * 6 * BLK * BLK * depth,
            bytes_accessed=(shifts_early + rows_early) * SPAN * depth * 4,
            transcendentals=0,
        ),
        name="grams",
    )(meta, listing, *columns, *rows)


def weights_kernel(sizes, counts, meta, listing, seeds, grams, high_c, low_c, high_last, low_last, *rest):
    row_count, col_count = sizes
    shifts_early, rows_early = counts
    shifts, rows_late = shifts_early + 1, col_count - rows_early
    last, late, col_packs = rest[0], rest[1 : 1 + rows_late], rest[1 + rows_late :][:shifts]
    even_packs, odd_packs = rest[1 + rows_late + shifts :][:2]
    out, high_l, low_l, high_r, low_r, late_grams, col_params, row_params = rest[3 + rows_late + shifts :]
    row, col = meta[0], meta[1]

    high_l[...], low_l[...] = split(last[...])
    for shift in range(shifts):
        for block in range(CB):
            lanes = slice(block * BLK, (block + 1) * BLK)
            col_params[shift, block] = col_packs[shift][RHO : RHO + 8, lanes].T
    for bits in range(col_count):
        row_params[bits] = (even_packs, odd_packs)[bits % 2][bits // 2, RHO : RHO + 8, :]
    for line in range(rows_late):
        high_r[line], low_r[line] = split(late[line][...])

    def early_last(line):
        _, start_j, _ = pick_of(sizes, meta, listing, meta[3 + line], shifts_early)
        span_j = pl.ds(start_j, BLK)
        late_grams[shifts_early, meta[3 + line]] = gram_of(
            high_l[span_j, :], low_l[span_j, :], high_last[line], low_last[line]
        )

    each(rows_early, early_last)

    def late_row(line):
        bits = meta[3 + rows_early + line]
        for shift in range(shifts):
            start_i, start_j, _ = pick_of(sizes, meta, listing, bits, shift)
            span_i, span_j = pl.ds(start_i, BLK), pl.ds(start_j, BLK)
            if shift == shifts_early:
                high_j, low_j = high_l[span_j, :], low_l[span_j, :]
            else:
                high_j, low_j = high_c[shift, span_j, :], low_c[shift, span_j, :]
            late_grams[shift, bits] = gram_of(high_j, low_j, high_r[line, span_i, :], low_r[line, span_i, :])

    each(rows_late, late_row)

    positions_j = lax.broadcasted_iota(I32, (BLK, BLK), 0)
    positions_i = lax.broadcasted_iota(I32, (BLK, BLK), 1)
    wanted_seed = lax.broadcasted_iota(I32, (1, SPAN), 1) == col * row_count + row

    def finish(bits, shift, gram):
        start_i, start_j, place = pick_of(sizes, meta, listing, bits, shift)
        params_i = row_params[bits, :, pl.ds(start_i, BLK)]
        rho_i, sigma_i, square_i = params_i[0:1], params_i[1:2], params_i[2:3]
        params_j = col_params[shift, lax.div(start_j, BLK)]
        rho_j, sigma_j, square_j = params_j[:, 0:1], params_j[:, 1:2], params_j[:, 2:3]
        distance = jnp.sqrt(jnp.maximum(square_j + square_i - 2.0 * gram, 1.0))
        plane_seeds = row_params[bits, SEEDS - RHO + shift : SEEDS - RHO + shift + 1, :]
        seed_back = jnp.sum(jnp.where(wanted_seed, plane_seeds, 0.0), axis=1, keepdims=True).astype(I32)
        ahead = hash_bits(seeds[place], positions_i, positions_j) * jnp.exp(
            jnp.maximum(distance - rho_i, 0.0) * (-1.0 / sigma_i)
        )
        behind = hash_bits(seed_back, positions_j, positions_i) * jnp.exp(
            jnp.maximum(distance - rho_j, 0.0) * (-1.0 / sigma_j)
        )
        weights = (ahead + behind - ahead * behind).astype(BF16)
        if shift == 0:
            weights = (weights.astype(F32) * jnp.where(bits == 0, 0.5, 1.0)).astype(BF16)
        out[shift * col_count + bits] = weights

    def early_rows(line):
        bits = meta[3 + line]
        for shift in range(shifts):
            finish(bits, shift, grams[line, shift] if shift < shifts_early else late_grams[shift, bits])

    def late_rows(line):
        bits = meta[3 + rows_early + line]
        for shift in range(shifts):
            finish(bits, shift, late_grams[shift, bits])

    each(rows_early, early_rows)
    each(rows_late, late_rows)


def pair_weights(sizes, meta, listing, seeds, early, last, late, packs):
    _, col_count = sizes
    shifts, depth = len(packs) - 2, late[0].shape[-1]
    rows_late = len(late)
    smem = pl.BlockSpec(memory_space=pltpu.SMEM)
    vmem = pl.BlockSpec(memory_space=pltpu.VMEM)
    tiles = shifts * col_count
    return pl.pallas_call(
        functools.partial(weights_kernel, sizes, (shifts - 1, col_count - rows_late)),
        in_specs=[smem] * 3 + [vmem] * (5 + 1 + rows_late + len(packs)),
        out_specs=vmem,
        out_shape=jax.ShapeDtypeStruct((tiles, BLK, BLK), BF16),
        scratch_shapes=[
            pltpu.VMEM((SPAN, depth), BF16),
            pltpu.VMEM((SPAN, depth), BF16),
            pltpu.VMEM((rows_late, SPAN, depth), BF16),
            pltpu.VMEM((rows_late, SPAN, depth), BF16),
            pltpu.VMEM((shifts, col_count, BLK, BLK), F32),
            pltpu.VMEM((shifts, CB, BLK, 8), F32),
            pltpu.VMEM((col_count, 8, SPAN), F32),
        ],
        compiler_params=pltpu.CompilerParams(vmem_limit_bytes=vmem_limit(sizes)),
        cost_estimate=pl.CostEstimate(
            flops=tiles * 3 * BLK * BLK * depth,
            bytes_accessed=(1 + rows_late) * SPAN * depth * 4,
            transcendentals=tiles * 3 * BLK * BLK,
        ),
        name="weights",
    )(meta, listing, seeds, *early, last, *late, *packs)


def force_kernel(row_count, col_count, by_bits, meta, listing, neg_rows, neg_cols, weights, *rest):
    shifts = row_count // 2 + 1
    row_arrays, rest = (rest[:2], rest[2:]) if by_bits else (rest[:1], rest[1:])
    col_y = rest[:row_count]
    row_force, col_force = rest[row_count], rest[row_count + 1 : 2 * row_count + 1]
    left_gram, right_gram, left_pull, right_pull, left_acc, right_acc, held_v, held_h = rest[2 * row_count + 1 :]
    row, col, live = meta[0], meta[1], meta[2]
    iota = lax.broadcasted_iota(I32, (D_EMB, BLK), 0)
    ones = jnp.ones((16, BLK), BF16)
    blank = jnp.zeros((D_EMB, BLK), BF16)

    def norm_rows(value, first):
        norm = jnp.sum(value * value, axis=0, keepdims=True)
        high, rest_ = split(norm)
        left_over = norm - high.astype(F32) - rest_.astype(F32)
        high, middle = high.astype(F32), rest_.astype(F32)
        return jnp.where(
            iota == first,
            high,
            jnp.where(iota == first + 1, middle, jnp.where(iota == first + 2, left_over, 0.0)),
        )

    def pulls(high, low):
        top = jnp.concatenate([high, ones, low], axis=0)
        bottom = jnp.concatenate([high, ones, blank], axis=0)
        return jnp.concatenate([top, bottom], axis=1)

    def left_block(index, value):
        high, low = split(value)
        extra = norm_rows(value, 0) + jnp.where((iota >= 3) & (iota < 7), 1.0, 0.0)
        left_gram[index] = jnp.concatenate([high, low, high, extra.astype(BF16)], axis=0)
        left_pull[index] = pulls(high, low)
        left_acc[index] = jnp.zeros((PULL, BLK), F32)

    def right_block(index, value):
        high, low = split(value)
        extra = norm_rows(value, 3) + jnp.where((iota < 3) | (iota == 6), 1.0, 0.0)
        twice_high, twice_low = -2.0 * high.astype(F32), -2.0 * low.astype(F32)
        stack = jnp.concatenate([twice_high, twice_high, twice_low, extra], axis=0)
        right_gram[index] = stack.T.astype(BF16)
        right_pull[index] = pulls(high, low)
        right_acc[index] = jnp.zeros((PULL, BLK), F32)

    def row_y(pair, side, block):
        lanes = slice(block * BLK, (block + 1) * BLK)
        line = pair * 2 + side
        if by_bits:
            return row_arrays[side][pair, :D_EMB, lanes], lax.bitwise_xor(line, col)
        return row_arrays[0][line, :D_EMB, lanes], line

    @pl.loop(0, col_count // 2)
    def _(pair):
        for side in range(2):
            for block in range(CB):
                value, group = row_y(pair, side, block)
                left_block(group * CB + block, value)

    for shift in range(row_count):
        for block in range(CB):
            right_block(shift * CB + block, col_y[shift][:D_EMB, block * BLK : (block + 1) * BLK])

    def kernel_of(left, right):
        return 1.0 / nn_dot(right_gram[right], left_gram[left])

    def apply_all(tiles_):
        for lane, (left, right, coefficient) in enumerate(tiles_):
            high, low = split(coefficient())
            held_v[lane, :BLK], held_v[lane, BLK:] = high, low
            held_h[lane, :, :BLK], held_h[lane, :, BLK:] = high, low
        for lane, (left, right, _) in enumerate(tiles_):
            left_acc[left] += nn_dot(right_pull[right], held_v[lane])
        for lane, (left, right, _) in enumerate(tiles_):
            right_acc[right] += nt_dot(left_pull[left], held_h[lane])

    def near_active(group):
        offset = lax.rem(group - col + col_count, col_count)
        return (2 * offset < col_count) | ((2 * offset == col_count) & (2 * col < col_count))

    near = col_count // 2 + 1
    tiles = near + col_count * (shifts - 1)
    last = jnp.where(takes_shift(shifts - 1, row, row_count), tiles, tiles - col_count)

    @pl.loop(0, lax.div(last + UNROLL - 1, UNROLL))
    def _(step):
        batch = []
        for lane in range(UNROLL):
            index = step * UNROLL + lane
            far = jnp.maximum(index - near, 0)
            shift = jnp.where(index < near, 0, 1 + lax.div(far, col_count))
            group = jnp.where(index < near, lax.rem(col + index, col_count), lax.rem(far, col_count))
            inside = index < last
            shift = jnp.where(inside, shift, 0)
            inside &= (shift > 0) | near_active(group)
            slot = shift * col_count + lax.bitwise_xor(group, col)
            entry = (group * row_count + lax.rem(row + shift, row_count)) * 2
            left = group * CB + listing[entry]
            right = shift * CB + listing[entry + 1]

            def pull(left=left, right=right, slot=slot, inside=inside):
                return weights[slot].astype(F32) * (kernel_of(left, right) * jnp.where(inside, 1.0, 0.0))

            batch.append((left, right, pull))
        apply_all(batch)

    @pl.loop(0, lax.div(live + UNROLL - 1, UNROLL))
    def _(step):
        batch = []
        for lane in range(UNROLL):
            index = step * UNROLL + lane
            strength = jnp.where(index < live, -REPULSION, 0.0)
            place = jnp.minimum(index, live - 1)
            left = neg_rows[place]
            other = neg_cols[place]
            shift = lax.rem(lax.div(other, CB) - row + row_count, row_count)
            right = shift * CB + lax.rem(other, CB)
            def push(left=left, right=right, strength=strength):
                kernel = kernel_of(left, right)
                return strength * kernel * kernel
            batch.append((left, right, push))
        apply_all(batch)

    def force_of(acc, value):
        return acc[:D_EMB] + acc[D_EMB + 16 :] - value * acc[D_EMB : D_EMB + 1]

    @pl.loop(0, col_count // 2)
    def _(pair):
        for side in range(2):
            for block in range(CB):
                value, group = row_y(pair, side, block)
                lanes = slice(block * BLK, (block + 1) * BLK)
                row_force[group, :, lanes] = force_of(left_acc[group * CB + block], value)

    for shift in range(row_count):
        for block in range(CB):
            lanes = slice(block * BLK, (block + 1) * BLK)
            col_force[shift][:, lanes] = force_of(right_acc[shift * CB + block], col_y[shift][:D_EMB, lanes])


def pair_forces(sizes, meta, listing, neg_rows, neg_cols, weights, row_y, col_y):
    row_count, col_count = sizes
    smem = pl.BlockSpec(memory_space=pltpu.SMEM)
    vmem = pl.BlockSpec(memory_space=pltpu.VMEM)
    lefts, rights = col_count * CB, row_count * CB
    tiles = col_count * 2 + 48
    outs = pl.pallas_call(
        functools.partial(force_kernel, row_count, col_count, len(row_y) > 1),
        in_specs=[smem] * 4 + [vmem] * (1 + len(row_y) + row_count),
        out_specs=[vmem] * (1 + row_count),
        out_shape=[jax.ShapeDtypeStruct((col_count, D_EMB, SPAN), F32)]
        + [jax.ShapeDtypeStruct((D_EMB, SPAN), F32)] * row_count,
        scratch_shapes=[
            pltpu.VMEM((lefts, STACK, BLK), BF16),
            pltpu.VMEM((rights, BLK, STACK), BF16),
            pltpu.VMEM((lefts, PULL, 2 * BLK), BF16),
            pltpu.VMEM((rights, PULL, 2 * BLK), BF16),
            pltpu.VMEM((lefts, PULL, BLK), F32),
            pltpu.VMEM((rights, PULL, BLK), F32),
            pltpu.VMEM((UNROLL, 2 * BLK, BLK), BF16),
            pltpu.VMEM((UNROLL, BLK, 2 * BLK), BF16),
        ],
        compiler_params=pltpu.CompilerParams(vmem_limit_bytes=vmem_limit(sizes)),
        cost_estimate=pl.CostEstimate(
            flops=tiles * 2 * BLK * BLK * (STACK + 4 * PULL),
            bytes_accessed=4 * D_EMB * SPAN * 2 * (col_count + row_count),
            transcendentals=tiles * BLK * BLK,
        ),
        name="forces",
    )(meta, listing, neg_rows, neg_cols, weights, *row_y, *col_y)
    return outs[0], outs[1:]


def shards(inputs, rho, sigma, embed, knn_blocks, knn_seeds, neg_rows, neg_cols, neg_count):
    row_count = lax.axis_size("row")
    col_count = lax.axis_size("col")
    shifts = row_count // 2 + 1
    row, col = lax.axis_index("row"), lax.axis_index("col")
    listing = knn_blocks.reshape(-1)
    seeds = knn_seeds.reshape(-1)
    row_list, col_list = neg_rows.reshape(-1), neg_cols.reshape(-1)
    meta = jnp.stack([row, col, neg_count[0, 0]]).astype(I32)

    def from_shift(value, shift):
        pairs = [((r + shift) % row_count, r) for r in range(row_count)]
        return lax.ppermute(value, "row", pairs)

    def from_half(value):
        half = row_count // 2
        pairs = [(r + half, r) if r % 2 == 0 else (r, r + half) for r in range(half)]
        return lax.ppermute(value, "row", pairs)

    def to_shift(value, shift):
        pairs = [(r, (r + shift) % row_count) for r in range(row_count)]
        return lax.ppermute(value, "row", pairs)

    def from_bits(value, bits):
        pairs = [(c ^ bits, c) for c in range(col_count)]
        return lax.ppermute(value, "col", pairs)

    sizes = row_count, col_count
    single = [1 << place for place in range(1, (col_count - 1).bit_length())]
    early_bits = [0, 1] + [bits + core for bits in single for core in range(2)]
    late_bits = [bits for bits in range(col_count) if bits not in early_bits]
    meta = jnp.concatenate([meta, jnp.array(early_bits + late_bits, I32)])

    def after(value, *others):
        return lax.optimization_barrier((value, *others))[0]

    row_x = {0: inputs}
    for bits in single:
        row_x[bits] = from_bits(inputs, bits)
    col_x = [inputs] + [from_shift(inputs, shift) for shift in range(1, shifts - 1)]
    near = [row_x[bits] for bits in single] + col_x[1:]
    for bits in late_bits:
        if bits % 2 == 0:
            row_x[bits] = from_bits(inputs, bits)
    seed_row = jnp.pad(seeds.astype(F32)[None], ((0, 0), (0, SPAN - seeds.shape[0])))
    params = jnp.stack([rho, sigma, jnp.sum(inputs * inputs, axis=1)])
    blank = jnp.zeros((PACK - SEEDS - 1, SPAN), F32)
    pack = jnp.concatenate([embed, params, seed_row, blank], axis=0)
    col_packs = [pack] + [from_shift(pack, shift) for shift in range(1, shifts)]
    held, meta, listing, seeds = lax.optimization_barrier((inputs, meta, listing, seeds, *col_packs[1:]))[:4]
    row_x[1] = from_bits(held, 1)
    for bits in single:
        row_x[bits + 1] = from_bits(after(row_x[bits], *near), 1)
    col_x.append(from_half(after(inputs, row_x[1])))

    own_pack = pack
    for shift in range(1, shifts):
        place = SEEDS + shift
        far_seed = col_packs[shift][SEEDS : SEEDS + 1]
        own_pack = own_pack + jnp.pad(far_seed, ((place, PACK - place - 1), (0, 0)))
    own_pack = after(own_pack, *[row_x[bits + 1] for bits in single])
    early = early_grams(sizes, meta, listing, col_x[:-1], [row_x[bits] for bits in early_bits[1:]])
    even_packs = jnp.stack([own_pack] + [from_bits(own_pack, bits) for bits in range(2, col_count, 2)])
    even_packs = after(even_packs, early[0])
    odd_packs = from_bits(even_packs, 1)
    for bits in late_bits:
        if bits % 2 == 0:
            row_x[bits + 1] = from_bits(after(row_x[bits], even_packs), 1)
    held = after(embed, *[row_x[bits] for bits in late_bits if bits % 2 == 0])
    col_y = col_packs + [from_shift(held, shift) for shift in range(shifts, row_count)]

    weights = pair_weights(
        sizes,
        meta,
        listing,
        seeds,
        early,
        col_x[-1],
        [row_x[bits] for bits in late_bits],
        col_packs + [even_packs, odd_packs],
    )

    row_y = (even_packs, odd_packs)
    for step in range(STEPS):
        if step:
            row_y = (lax.all_gather(embed, "col", axis=0, tiled=False),)
            col_y = [embed] + [from_shift(embed, shift) for shift in range(1, row_count)]
        row_force, col_force = pair_forces(sizes, meta, listing, row_list, col_list, weights, row_y, col_y)
        row_parts = lax.all_to_all(row_force, "col", split_axis=0, concat_axis=0, tiled=True)
        force = jnp.sum(row_parts, axis=0) + col_force[0]
        for shift in range(1, row_count):
            force = force + to_shift(col_force[shift], shift)
        embed = embed + STEP_SIZE * force
    return (embed, force * FORCE_SCALE)


def solution(mesh):
    in_specs = (
        P(("row", "col"), None),
        P(("row", "col")),
        P(("row", "col")),
        P(None, ("row", "col")),
        P("row", "col", None, None, None),
        P("row", "col", None, None),
        P("row", "col", None),
        P("row", "col", None),
        P("row", "col"),
    )
    out_specs = (P(None, ("row", "col")), P(None, ("row", "col")))
    return jax.shard_map(shards, mesh=mesh, in_specs=in_specs, out_specs=out_specs, check_vma=False)
```
